32 devices in a mesh: bond: 8 (over z, x), mpo: 4 (over y, core).
Axes of the slice: x: 2, y: 2, z: 4, core: 2. Of those that a mesh axis runs over, the one named last changes fastest.
Arguments:
- wave_blocks: bfloat16 [8, 16, 256, 256], P('bond'), may hold values from -6 to 6
- left_environment: bfloat16 [8, 8, 256, 256], P('mpo', 'bond'), may hold values from -0.375 to 0.375
- right_environment: bfloat16 [8, 8, 256, 256], P('mpo', 'bond'), may hold values from -0.375 to 0.375
- site_operators: bfloat16 [8, 16, 16], P('mpo'), may hold values from -1.1953125 to 1.1953125
- right_sector: int32 [8, 16, 1], P('bond'), may hold values from 0 to 7; in each aligned block of 16 rows (0 to 15, 16 to 31, ..., all dimensions but the last counted through in order) at most 2 rows name the same one
- left_sizes: int32 [8], replicated, may hold values from 128 to 256
- right_sizes: int32 [8], replicated, may hold values from 128 to 256
- sector_place: int32 [8], replicated, may hold values from 0 to 7, each once
Outputs:
- applied: bfloat16 [8, 16, 256, 256], P('bond', 'mpo')
The draws below stay inside these ranges and needn't reach their ends.
Inputs may be any that keep to these rules, and one draw needn't show every extreme that they name: `right_sector`: among the 16 blocks of one bond index no right sector is named more than 2 times, a bound that some block reaches. `sector_place`: every position is taken by exactly one right sector.
All inputs are finite; a program needn't handle non-finite values.
Results may differ from the reference program's by a relative error of at most 0.0057.
Values may be sent and summed in bfloat16 or wider, within the bound.
A program may use at most 64 MiB of HBM per device.

```python
import math
import jax
import jax.numpy as jnp
import numpy as np
from jax import lax

SB = 256
P_SIZE = 16
CAPP = 2
NSD = 1
WM = 8
NS = 8


def touch_ends(array, own_key, smallest, top_value):
    index_at = [jax.random.randint(jax.random.fold_in(own_key, axis), (), 0, length) for axis, length in enumerate(array.shape)]
    widest = array.shape.index(max(array.shape))
    neighbour = index_at[:widest] + [(index_at[widest] + 1) % array.shape[widest]] + index_at[widest + 1:]
    return array.at[tuple(index_at)].set(smallest).at[tuple(neighbour)].set(top_value)


def levels(rng, extent, cuts, low, largest):
    def one(dim, parts):
        heights = jax.random.uniform(jax.random.fold_in(jax.random.fold_in(rng, 6), dim), (parts,), jnp.float32, low / len(cuts), largest / len(cuts))
        return jnp.repeat(jnp.exp(heights), extent[dim] // parts).reshape((-1,) + (1,) * (len(extent) - dim - 1))

    gain = one(*cuts[0])
    for cut in cuts[1:]:
        gain = gain * one(*cut)
    return gain


def shared_out(stream_key, own, number, rows, number_of, top, reach, skew):
    ranking = jax.random.permutation(stream_key, number_of)
    crowded, ordinary = portions_of(number_of, rows * top, reach, skew, True), portions_of(number_of, rows * top, reach, skew, False)
    places = jnp.arange(number_of)

    def named(tallies, turn):
        used = int((tallies > 0).sum())
        fixed = max(1, used // 4)
        shifted = fixed + (places - fixed + turn * (used - fixed)) % max(1, number_of - fixed)
        return jnp.zeros((number_of,), jnp.int32).at[ranking[jnp.where(places < fixed, places, shifted)]].set(jnp.asarray(tallies, jnp.int32))

    tallies = jnp.where(number % 4 == 0, named(crowded, number // 4), named(ordinary, number - number // 4 - 1))
    mixed = jax.random.permutation(jax.random.fold_in(own, 3), number_of)
    donor, receiver = mixed[0:number_of // 2 * 2:2], mixed[1:number_of // 2 * 2:2]
    slack = jnp.minimum(tallies[donor] - 1, reach - tallies[receiver]) // 2
    slack = jnp.where((donor == ranking[0]) | (receiver == ranking[0]) | (tallies[receiver] == 0), 0, jnp.maximum(slack, 0))
    shifted = jax.random.randint(jax.random.fold_in(own, 4), (number_of // 2,), 0, 1 << 20) % (slack + 1)
    tallies = tallies.at[donor].add(-shifted).at[receiver].add(shifted)
    labels = jnp.searchsorted(jnp.cumsum(tallies), jnp.arange(rows * top), side="right").astype(jnp.int32)
    listing = labels.reshape(top, rows).T
    listing = listing[jax.random.permutation(jax.random.fold_in(own, 1), rows)]
    turn = jax.random.randint(jax.random.fold_in(own, 2), (rows, 1), 0, top)
    return jnp.take_along_axis(listing, (jnp.arange(top)[None, :] + turn) % top, axis=1)


def portions_of(number_of, total, limit, slope, full):
    loads = [(1 << 20) // math.isqrt(grade ** slope) + 1 for grade in range(1, number_of + 1)]
    largest = limit if full else min(limit, max(-(-total // number_of), total * loads[0] // sum(loads)))
    least = 1 if total - largest >= number_of - 1 else 0
    given, spare = [largest] + [least] * (number_of - 1), total - largest - least * (number_of - 1)
    while spare > 0:
        free = [i for i in range(1, number_of) if given[i] < largest] or [i for i in range(1, number_of) if given[i] < limit]
        whole, remaining = sum([loads[i] for i in free]), spare
        for i in free:
            addition = min(limit - given[i], max(1, remaining * loads[i] // whole), spare)
            given[i] = given[i] + addition
            spare = spare - addition
    return np.array(given)


def normal_values(own_key, dims, scale, bound, pieces=(), kind=jnp.bfloat16):
    factor_of = levels(own_key, dims, pieces, -0.22, 0.18) if pieces else 1.0
    entries = jax.random.normal(own_key, dims, jnp.float32) * scale * factor_of
    return jnp.minimum(jnp.maximum(entries, -bound), bound).astype(kind)


def setup_inputs(seed: int = 0) -> dict:
    arg_keys = jax.random.split(jax.random.key(seed), 9)
    wave_blocks = normal_values(arg_keys[0], (NS, P_SIZE, SB, SB), 1.0, 6.0, ((0, 8),))
    left_environment = normal_values(arg_keys[1], (WM, NS, SB, SB), SB ** -0.5, 0.375, ((0, 4), (1, 8)))
    right_environment = normal_values(arg_keys[2], (WM, NS, SB, SB), SB ** -0.5, 0.375, ((0, 4), (1, 8)))
    site_operators = normal_values(arg_keys[3], (WM, P_SIZE, P_SIZE), 0.2, 1.1953125, ((0, 4),))
    right_sector_keys = jax.random.split(jax.random.fold_in(arg_keys[4], 1), NS * P_SIZE // (NSD * P_SIZE))
    right_sector_turns = jax.random.permutation(jax.random.fold_in(arg_keys[4], 3), NS * P_SIZE // (NSD * P_SIZE))
    right_sector = jax.vmap(lambda own, number: shared_out(jax.random.fold_in(arg_keys[4], 2), own, number, NSD * P_SIZE, NS, 1, CAPP, 2))(right_sector_keys, right_sector_turns).reshape((NS, P_SIZE, 1))
    left_sizes = touch_ends(jax.random.randint(arg_keys[5], (NS,), SB // 2, SB + 1), jax.random.fold_in(arg_keys[5], 1), SB // 2, SB).astype(jnp.int32)
    right_sizes = touch_ends(jax.random.randint(arg_keys[6], (NS,), SB // 2, SB + 1), jax.random.fold_in(arg_keys[6], 1), SB // 2, SB).astype(jnp.int32)
    sector_place = jax.random.permutation(arg_keys[7], NS).astype(jnp.int32)
    return {"wave_blocks": wave_blocks, "left_environment": left_environment, "right_environment": right_environment, "site_operators": site_operators, "right_sector": right_sector, "left_sizes": left_sizes, "right_sizes": right_sizes, "sector_place": sector_place}


def reference(wave_blocks, left_environment, right_environment, site_operators, right_sector, left_sizes, right_sizes, sector_place):
    sector_ids = right_sector[:, :, 0]
    offsets = jnp.arange(SB, dtype=jnp.int32)
    row_mask = offsets[None, :] < left_sizes[:, None]
    column_mask = offsets[None, None, :] < right_sizes[sector_ids][:, :, None]
    live_mask = row_mask[:, None, :, None] & column_mask[:, :, None, :]
    masked = jnp.where(live_mask, wave_blocks, jnp.zeros((), jnp.bfloat16))
    position = sector_place[sector_ids]
    same_sector = sector_ids[:, :, None] == sector_ids[:, None, :]
    masked_wide = masked.astype(jnp.float32)

    def one_channel(channel, running):
        chosen = jnp.take(right_environment[channel], position, axis=0).astype(jnp.float32)
        right_part = jnp.einsum('ksac,ksxc->ksax', masked_wide, chosen).astype(jnp.bfloat16)
        mixing = jnp.where(same_sector, site_operators[channel][None], jnp.zeros((), jnp.bfloat16))
        mixed = jnp.einsum('kst,ktac->ksac', mixing.astype(jnp.float32), right_part.astype(jnp.float32)).astype(jnp.bfloat16)
        return running + jnp.einsum('kab,ksbc->ksac', left_environment[channel].astype(jnp.float32), mixed.astype(jnp.float32))

    running = lax.fori_loop(0, WM, one_channel, jnp.zeros(wave_blocks.shape, jnp.float32))
    return jnp.where(live_mask, running, jnp.zeros((), jnp.float32)).astype(jnp.bfloat16)
```

```python
import functools

import jax
import jax.numpy as jnp
from jax import lax
from jax.experimental import pallas as pl
from jax.experimental.pallas import tpu as pltpu
from jax.sharding import PartitionSpec as P

MESH = pl.DeviceIdType.MESH


def plane_of(count):
    nx = 1
    while (2 * nx) * (2 * nx) * 2 <= count and count % (2 * nx) == 0:
        nx *= 2
    return count // nx, nx


def kernel(
    n, m,
    sector, place, left_sizes, right_sizes, ops,
    wave_hbm, left_hbm, right_hbm,
    out_ref,
    right_all, wave, left, local_sem, gather_send, gather_recv, *rest,
):
    nz, nx = plane_of(n)
    cores = 2 if m % 2 == 0 else 1
    ny = m // cores
    states, rows, _ = wave.shape
    channels = left.shape[0]
    per = out_ref.shape[0]
    count = ny * per
    pair = ny == 2 and cores == 2
    if pair:
        (part, part_out, part_in, sums,
         part_send, part_recv, sum_send, sum_recv) = rest
    else:
        (mixed, out_core, in_core, out_chip, in_chip, own,
         core_send, core_recv, chip_send, chip_recv) = rest
    b = lax.axis_index("bond")
    p = lax.axis_index("mpo")
    z, x = b // nx, b % nx
    y, c = p // cores, p % cores
    sibling = y * cores + (1 - c)

    wave_copy = pltpu.make_async_copy(wave_hbm, wave, local_sem.at[0])
    left_copy = pltpu.make_async_copy(left_hbm, left, local_sem.at[1])
    own_copy = pltpu.make_async_copy(right_hbm, right_all.at[b], local_sem.at[2])
    wave_copy.start()
    left_copy.start()
    own_copy.start()

    steps = ((nx, z + 1 < nz), (-nx, z > 0), (1, x + 1 < nx), (-1, x > 0))
    barrier = pltpu.get_barrier_semaphore()
    greeted = ny
    for step, there in steps:
        greeted = greeted + there.astype(jnp.int32)

        @pl.when(there)
        def _():
            pl.semaphore_signal(barrier, inc=1, device_id=(b + step, p), device_id_type=MESH)

    pl.semaphore_signal(barrier, inc=1, device_id=(b, sibling), device_id_type=MESH)
    for dy in range(1, ny):
        other = lax.rem(y + dy, ny) * cores + c
        pl.semaphore_signal(barrier, inc=1, device_id=(b, other), device_id_type=MESH)
    pl.semaphore_wait(barrier, greeted)

    def hop(pos, h, k, src):
        return pltpu.make_async_remote_copy(
            src_ref=src,
            dst_ref=right_all.at[pos, h],
            send_sem=gather_send.at[pos, h, k],
            recv_sem=gather_recv.at[pos, h],
            device_id=(b + steps[k][0], p),
            device_id_type=MESH,
        )

    def sends(zs, xs, h):
        column = xs == x
        if nx == 2 and h == channels - 1 and channels > 1:
            detour = (zs == 0) | (zs == nz - 1)
            along, across = column | detour, ~detour | (zs == z)
        else:
            along, across = column, True
        return (
            along & (zs <= z) & (z + 1 < nz),
            along & (zs >= z) & (z > 0),
            across & (xs <= x) & (x + 1 < nx),
            across & (xs >= x) & (x > 0),
        )

    def forward(zs, xs, h):
        pos = zs * nx + xs
        for k, wanted in enumerate(sends(zs, xs, h)):
            @pl.when(wanted)
            def _():
                hop(pos, h, k, right_all.at[pos, h]).start()

    def arrived(pos, h):
        hop(pos, h, 0, right_all.at[pos, h]).wait_recv()

    for h in range(channels):
        for k in (0, 1, 2, 3):
            @pl.when(steps[k][1])
            def _():
                hop(b, h, k, right_hbm.at[h]).start()

    wave_copy.wait()
    left_copy.wait()
    own_copy.wait()

    row_index = lax.broadcasted_iota(jnp.int32, (rows, rows), 0)
    column_index = lax.broadcasted_iota(jnp.int32, (rows, rows), 1)
    live_rows = row_index < left_sizes[b]
    op_row = lax.broadcasted_iota(jnp.int32, (states, states), 0)
    op_column = lax.broadcasted_iota(jnp.int32, (states, states), 1)

    def to_sibling(pos):
        return pltpu.make_async_remote_copy(
            src_ref=part_out.at[pos], dst_ref=part_in.at[pos],
            send_sem=part_send.at[pos], recv_sem=part_recv.at[pos],
            device_id=(b, sibling), device_id_type=MESH,
        )

    def share(kind, pos):
        source, target = (0, 0, 1)[kind], (0, 1, 1)[kind]
        device = (1 - y) * cores + c if kind == 1 else sibling
        return pltpu.make_async_remote_copy(
            src_ref=sums.at[source, pos, c], dst_ref=sums.at[target, pos, c],
            send_sem=sum_send.at[kind, pos], recv_sem=sum_recv.at[target, pos, c],
            device_id=(b, device), device_id_type=MESH,
        )

    def sum_arrived(target, pos, rank):
        pltpu.make_async_remote_copy(
            src_ref=sums.at[target, pos, rank], dst_ref=sums.at[target, pos, rank],
            send_sem=sum_send.at[0, pos], recv_sem=sum_recv.at[target, pos, rank],
            device_id=(b, sibling), device_id_type=MESH,
        ).wait_recv()

    def add_up(pos):
        to_sibling(pos).wait_recv()
        sums[0, pos, c] = (part[pos] + part_in[pos].astype(jnp.float32)).astype(jnp.bfloat16)
        share(1, pos).start()
        share(0, pos).start()

    def pass_on(pos):
        sum_arrived(1, pos, c)
        share(2, pos).start()

    def work(pos):
        def look(s, carry):
            first, last, hits = carry
            hit = place[sector[s]] == pos
            first = jnp.where(hit & (hits == 0), s, first)
            last = jnp.where(hit, s, last)
            return first, last, hits + hit.astype(jnp.int32)

        zero = jnp.int32(0)
        s1, s2, hits = lax.fori_loop(0, states, look, (zero, zero, zero), unroll=True)
        if pair:
            s1, s2 = jnp.where(c == 0, s1, s2), jnp.where(c == 0, s2, s1)
        live = live_rows & (column_index < right_sizes[sector[s1]])

        def masked(s):
            return jnp.where(live, wave[s].astype(jnp.float32), 0.0).astype(jnp.bfloat16)

        both = jnp.concatenate([masked(s1), masked(s2)], axis=0)
        two = hits == 2
        for h in range(channels):
            factor = right_all[pos, h]

            parts = lax.dot_general(
                both, factor, (((1,), (1,)), ((), ())), preferred_element_type=jnp.float32
            ).astype(jnp.bfloat16).astype(jnp.float32)
            p1, p2 = parts[:rows], parts[rows:]
            table = ops[h].astype(jnp.float32)

            def op(s, t, keep=True):
                picked = (op_row == s) & (op_column == t) & keep
                return jnp.sum(jnp.where(picked, table, 0.0), keepdims=True)

            m1 = (op(s1, s1) * p1 + op(s1, s2, two) * p2).astype(jnp.bfloat16)
            m2 = (op(s2, s1, two) * p1 + op(s2, s2) * p2).astype(jnp.bfloat16)
            if pair:
                left_m = left[h]
                q1 = jnp.dot(left_m, m1, preferred_element_type=jnp.float32)
                q2 = jnp.dot(left_m, m2, preferred_element_type=jnp.float32)
                total1, total2 = (q1, q2) if h == 0 else (total1 + q1, total2 + q2)
            else:
                mixed[2 * pos, h] = m1
                mixed[2 * pos + 1, h] = m2
        if pair:
            part_out[pos] = total2.astype(jnp.bfloat16)
            to_sibling(pos).start()
            part[pos] = total1

    def at(g, i, body):
        sign = 1 - 2 * (i % 2)
        e = i // 2
        d = g - (e > 0).astype(jnp.int32)
        zs = z + sign * d
        xs = x + (e + 1) // 2 * (1 - 2 * (e % 2))

        @pl.when((zs >= 0) & (zs < nz) & (xs >= 0) & (xs < nx) & (d >= 0) & ((d > 0) | (sign > 0)))
        def _():
            body(zs, xs)

    items = 2 * (2 * nx - 1)

    def each(g, body):
        def one(i, _):
            at(g, i, body)
            return 0

        lax.fori_loop(0, items, one, 0)

    def multiply(g):
        def one(i, _):
            @pl.when(i < items)
            def _():
                at(g, i, use)

            @pl.when(i >= 2)
            def _():
                at(g, i - 2, lambda zs, xs: add_up(zs * nx + xs))

            return 0

        lax.fori_loop(0, items + 2, one, 0)

    def use(zs, xs):
        pos = zs * nx + xs

        @pl.when(xs != x)
        def _():
            for h in range(channels):
                arrived(pos, h)
                forward(zs, xs, h)

        work(pos)

    def gather_round(g, _):
        @pl.when((g > 0) & (g < nz))
        def _():
            for h in range(channels):
                for sign in (1, -1):
                    zs = z + sign * g

                    @pl.when((zs >= 0) & (zs < nz))
                    def _():
                        arrived(zs * nx + x, h)
                        forward(zs, x, h)

        @pl.when(g <= nz)
        def _():
            if pair:
                multiply(g)
            else:
                each(g, use)

        if pair:
            @pl.when(g > 1)
            def _():
                each(g - 2, lambda zs, xs: pass_on(zs * nx + xs))

        return 0

    lax.fori_loop(0, nz + (3 if pair else 1), gather_round, 0)

    def rank_of(s):
        def look(t, rank):
            return rank + ((t < s) & (sector[t] == sector[s])).astype(jnp.int32)

        return jnp.minimum(lax.fori_loop(0, states, look, jnp.int32(0), unroll=True), 1)

    def finish(pos, _):
        for h in range(channels):
            for k, wanted in enumerate(sends(pos // nx, pos % nx, h)):
                @pl.when(wanted)
                def _():
                    hop(pos, h, k, right_all.at[pos, h]).wait_send()
        if pair:
            to_sibling(pos).wait_send()
            for kind in range(3):
                share(kind, pos).wait_send()
        return 0

    if pair:
        def all_here(pos, _):
            sum_arrived(0, pos, 1 - c)
            sum_arrived(1, pos, 1 - c)
            return 0

        lax.fori_loop(0, n, all_here, 0)
        for q in range(per):
            s = p * per + q
            at, rank = place[sector[s]], rank_of(s)
            total = sums[0, at, rank].astype(jnp.float32) + sums[1, at, rank].astype(jnp.float32)
            live = live_rows & (column_index < right_sizes[sector[s]])
            out_ref[q] = jnp.where(live, total, 0.0).astype(jnp.bfloat16)
        lax.fori_loop(0, n, finish, 0)
        return

    def product(s):
        slot = 2 * place[sector[s]] + rank_of(s)
        total = jnp.dot(left[0], mixed[slot, 0], preferred_element_type=jnp.float32)
        for h in range(1, channels):
            total += jnp.dot(left[h], mixed[slot, h], preferred_element_type=jnp.float32)
        return total

    def owner_chip(i):
        return lax.rem(y + 1 + i // per, ny)

    def to_core(i):
        return pltpu.make_async_remote_copy(
            src_ref=out_core.at[i], dst_ref=in_core.at[i],
            send_sem=core_send.at[i], recv_sem=core_recv.at[i],
            device_id=(b, sibling), device_id_type=MESH,
        )

    def to_chip(i):
        return pltpu.make_async_remote_copy(
            src_ref=out_chip.at[i], dst_ref=in_chip.at[i],
            send_sem=chip_send.at[i], recv_sem=chip_recv.at[i],
            device_id=(b, owner_chip(i) * cores + c), device_id_type=MESH,
        )

    remote = (ny - 1) * per
    lag = min(3, count)

    def reduce_step(i, _):
        @pl.when(i < count)
        def _():
            s = (owner_chip(i) * cores + (1 - c)) * per + i % per
            out_core[i] = product(s).astype(jnp.bfloat16)
            to_core(i).start()

        @pl.when(i >= lag)
        def _():
            j = i - lag
            s = (owner_chip(j) * cores + c) * per + j % per
            total = product(s)
            to_core(j).wait_recv()
            total = total + in_core[j].astype(jnp.float32)

            @pl.when(j < remote)
            def _():
                out_chip[j] = total.astype(jnp.bfloat16)
                to_chip(j).start()

            @pl.when(j >= remote)
            def _():
                own[j - remote] = total

        return 0

    lax.fori_loop(0, count + lag, reduce_step, 0)

    for q in range(per):
        total = own[q]
        for dy in range(ny - 1):
            to_chip(dy * per + q).wait_recv()
            total = total + in_chip[dy * per + q].astype(jnp.float32)
        live = live_rows & (column_index < right_sizes[sector[p * per + q]])
        out_ref[q] = jnp.where(live, total, 0.0).astype(jnp.bfloat16)

    lax.fori_loop(0, n, finish, 0)

    def finish_core(i, _):
        to_core(i).wait_send()
        return 0

    lax.fori_loop(0, count, finish_core, 0)

    def finish_chip(i, _):
        to_chip(i).wait_send()
        return 0

    lax.fori_loop(0, remote, finish_chip, 0)


def sum_of(k, values):
    if isinstance(k, int):
        return values[k]
    total = 0
    for i, v in enumerate(values):
        if v:
            total = total + (k == i).astype(jnp.int32) * v
    return total


def halves_kernel(
    n, m,
    sector, place, left_sizes, right_sizes, ops_ref,
    wave_hbm, left_hbm, right_hbm,
    out_ref,
    right_all, wave, left, ops, coef, part, part_out, part_in, fin, arr, states_of, mine,
    local_sem, gather_send, gather_recv, first_send, left_send, left_recv, ops_send, ops_recv,
    part_send, part_recv, fin_send, fin_recv, pass_send, pass_recv,
):
    nz, nx = plane_of(n)
    states, rows, _ = wave.shape
    half = rows // 2
    channels = left_hbm.shape[0]
    per = out_ref.shape[0]
    units = 2 * channels
    b = lax.axis_index("bond")
    p = lax.axis_index("mpo")
    z, x = b // nx, b % nx
    y, c = p // 2, p % 2
    sibling = y * 2 + (1 - c)
    peer = (1 - y) * 2 + c
    end = (z == 0) | (z == nz - 1)
    way = 1 - 2 * (z >= nz // 2).astype(jnp.int32)
    bf16, f32 = jnp.bfloat16, jnp.float32
    L, S, X = 0, 1, 2
    targets = (b + way * nx, b - way * nx, z * nx + (1 - x))

    def own_half(h, of):
        return right_hbm.at[h, pl.ds(pl.multiple_of(of * half, half), half)]

    wave_copy = pltpu.make_async_copy(wave_hbm, wave, local_sem.at[0])
    left_copy = pltpu.make_async_copy(left_hbm, left.at[pl.ds(0, channels)], local_sem.at[1])
    own_copies = [
        pltpu.make_async_copy(own_half(h, y), right_all.at[b, h], local_sem.at[2 + h])
        for h in range(channels)
    ]
    wave_copy.start()
    left_copy.start()
    for own in own_copies:
        own.start()

    barrier = pltpu.get_barrier_semaphore()
    for target in (L, X):
        pl.semaphore_signal(barrier, inc=1, device_id=(targets[target], p), device_id_type=MESH)

    @pl.when(jnp.logical_not(end))
    def _():
        pl.semaphore_signal(barrier, inc=1, device_id=(targets[S], p), device_id_type=MESH)

    for other in (sibling, peer):
        pl.semaphore_signal(barrier, inc=1, device_id=(b, other), device_id_type=MESH)
    pl.semaphore_wait(barrier, 5 - end.astype(jnp.int32))

    def to_device(src, dst, send, recv, device):
        return pltpu.make_async_remote_copy(
            src_ref=src, dst_ref=dst, send_sem=send, recv_sem=recv,
            device_id=device, device_id_type=MESH,
        )

    def hop(pos, u, kind, src):
        return to_device(
            src, right_all.at[pos, u], gather_send.at[pos, u, kind], gather_recv.at[pos, u],
            (targets[kind], p),
        )

    def first(h):
        return to_device(
            own_half(h, 1 - y), right_all.at[b, channels + h], first_send.at[h],
            gather_recv.at[b, channels + h], (b, peer),
        )

    def left_to_peer(h):
        return to_device(
            left_hbm.at[h], left.at[channels + h], left_send.at[h], left_recv.at[h], (b, peer)
        )

    ops_to_peer = to_device(
        ops_ref, ops.at[pl.ds(channels, channels)], ops_send, ops_recv, (b, peer)
    )

    for h in range(channels):
        first(h).start()
        for kind in (L, X):
            hop(b, h, kind, own_half(h, y)).start()

        @pl.when(jnp.logical_not(end))
        def _():
            hop(b, h, S, own_half(h, y)).start()

    ops_to_peer.start()
    for h in range(channels):
        left_to_peer(h).start()

    def place_of(off, other):
        return (z + way * off) * nx + ((1 - x) if other else x)

    def event(off, other, u, kinds):
        pos = place_of(off, other)
        hop(pos, u, X, right_all.at[pos, u]).wait_recv()
        for kind in kinds:
            hop(pos, u, kind, right_all.at[pos, u]).start()

    def sent(off, other, u, kinds):
        pos = place_of(off, other)
        for kind in kinds:
            hop(pos, u, kind, right_all.at[pos, u]).wait_send()

    lo, hi = range(channels), range(channels, units)
    end_order = [(0, 0), (0, 1), (1, 0), (1, 1), (2, 0), (2, 1), (3, 0), (3, 1)]
    mid_order = [(0, 0), (0, 1), (-1, 0), (1, 0), (-1, 1), (2, 0), (1, 1), (2, 1)]
    end_before = {
        "start": [(0, 0, 2, (L, X)), (1, 0, 0, (X,)), (0, 0, 3, (L, X))]
        + [(1, 0, u, (X,)) for u in (1, 2, 3)]
        + [(0, 1, u, ()) for u in lo] + [(0, 1, u, (L,)) for u in hi] + [(2, 0, 0, (X,))],
        1: [(2, 0, 1, (X,))],
        2: [(2, 0, 2, (X,))],
        3: [(2, 0, 3, (X,))] + [(1, 1, u, ()) for u in range(units)],
        5: [(3, 0, u, (X,)) for u in lo] + [(2, 1, u, ()) for u in range(units)],
        6: [(3, 0, u, ()) for u in hi],
        7: [(3, 1, u, ()) for u in range(units)],
    }
    mid_before = {
        "start": [
            (0, 0, 2, (L, S, X)), (-1, 0, 0, (L, X)), (1, 0, 0, (S, X)),
            (0, 0, 3, (L, S, X)), (-1, 0, 1, (L, X)), (1, 0, 1, (S, X)),
            (-1, 0, 2, (L,)), (1, 0, 2, (S, X)), (-1, 0, 3, (L,)), (1, 0, 3, (S, X)),
        ] + [(0, 1, u, ()) for u in range(units)] + [(2, 0, 0, (S, X)), (-1, 1, 2, (L,))],
        1: [(2, 0, 1, (S, X)), (-1, 1, 3, (L,))],
        2: [(2, 0, 2, (S,))],
        3: [(2, 0, 3, (S,))],
        4: [(-1, 1, u, ()) for u in lo],
        6: [(2, 1, u, (S,)) for u in hi] + [(1, 1, u, ()) for u in range(units)],
        7: [(2, 1, u, ()) for u in lo],
    }

    def run(stage):
        @pl.when(end)
        def _():
            for e in end_before.get(stage, ()):
                event(*e)

        @pl.when(jnp.logical_not(end))
        def _():
            for e in mid_before.get(stage, ()):
                event(*e)

    def pos_of(k):
        off = jnp.where(end, sum_of(k, [o for o, _ in end_order]), sum_of(k, [o for o, _ in mid_order]))
        other = jnp.where(end, sum_of(k, [o for _, o in end_order]), sum_of(k, [o for _, o in mid_order]))
        return (z + way * off) * nx + x + other * (1 - 2 * x)

    def list_states(k, _):
        pos = pos_of(k)

        def look(s, carry):
            s1, s2 = carry
            hit = place[sector[s]] == pos
            return jnp.where(hit & (s < s1), s, s1), jnp.where(hit, s, s2)

        s1, s2 = lax.fori_loop(0, states, look, (jnp.int32(states - 1), jnp.int32(0)), unroll=True)
        states_of[k, 0] = s1
        states_of[k, 1] = s2
        states_of[k, 2] = right_sizes[sector[s1]]
        return 0

    lax.fori_loop(0, n, list_states, 0)

    def list_mine(q, _):
        s = p * per + q

        def look(t, rank):
            return rank + ((t < s) & (sector[t] == sector[s])).astype(jnp.int32)

        mine[q, 0] = place[sector[s]]
        mine[q, 1] = jnp.minimum(lax.fori_loop(0, states, look, jnp.int32(0), unroll=True), 1)
        return 0

    lax.fori_loop(0, per, list_mine, 0)

    ops[pl.ds(0, channels)] = ops_ref[...]
    run("start")

    ops_to_peer.wait_recv()
    square = (states, states)
    op_row = lax.broadcasted_iota(jnp.int32, square, 0)
    op_column = lax.broadcasted_iota(jnp.int32, square, 1)
    named = jnp.zeros(square, jnp.int32)
    for r in range(states):
        named = jnp.where(op_row == r, states_of[r // 2, r % 2], named)
    pick = jnp.where(named == op_column, 1.0, 0.0).astype(bf16)
    same = op_row == op_column
    twin = op_row + 1 - 2 * (op_row % 2) == op_column
    for u in range(units):
        picked = jnp.dot(pick, ops[u], preferred_element_type=f32).astype(bf16)
        table = lax.dot_general(
            picked, pick, (((1,), (1,)), ((), ())), preferred_element_type=f32
        )
        for i, chosen in enumerate((same, twin)):
            column = jnp.sum(jnp.where(chosen, table, 0.0), axis=1, keepdims=True)
            coef[u, i] = jnp.broadcast_to(column, (states, 128))

    wave_copy.wait()
    left_copy.wait()
    for own in own_copies:
        own.wait()
    for h in range(channels):
        left_to_peer(h).wait_recv()

    row_index = lax.broadcasted_iota(jnp.int32, (rows, rows), 0)
    column_index = lax.broadcasted_iota(jnp.int32, (rows, rows), 1)
    half_row = lax.broadcasted_iota(jnp.int32, (rows, half), 0)
    half_column = lax.broadcasted_iota(jnp.int32, (rows, half), 1) + y * half

    def to_sibling(pos):
        return to_device(
            part_out.at[pos], part_in.at[pos], part_send.at[pos], part_recv.at[pos], (b, sibling)
        )

    def to_peer(pos):
        return to_device(
            fin.at[pos, c], arr.at[pos, c], fin_send.at[pos], fin_recv.at[pos], (b, peer)
        )

    def passing(pos, rank):
        return to_device(
            arr.at[pos, rank], arr.at[pos, rank], pass_send.at[pos], pass_recv.at[pos], (b, sibling)
        )

    def compute(k):
        pos = pos_of(k)
        s1, s2 = states_of[k, 0], states_of[k, 1]
        live = (row_index < left_sizes[b]) & (column_index < states_of[k, 2])

        def masked(s):
            return jnp.where(live, wave[s].astype(f32), 0.0).astype(bf16)

        both = jnp.concatenate([masked(s1), masked(s2)], axis=0)
        total = None
        for g in range(2):
            factor = right_all[pos, pl.ds(g * channels, channels)].reshape(channels * half, rows)
            parts = lax.dot_general(
                both, factor, (((1,), (1,)), ((), ())), preferred_element_type=f32
            ).astype(bf16).astype(f32)
            for h in range(channels):
                u = g * channels + h
                p1 = parts[:rows, h * half:(h + 1) * half]
                p2 = parts[rows:, h * half:(h + 1) * half]
                own1, own2 = coef[u, 0, pl.ds(2 * k, 1)], coef[u, 0, pl.ds(2 * k + 1, 1)]
                cross1, cross2 = coef[u, 1, pl.ds(2 * k, 1)], coef[u, 1, pl.ds(2 * k + 1, 1)]
                mixed = jnp.concatenate(
                    [(own1 * p1 + cross1 * p2).astype(bf16), (cross2 * p1 + own2 * p2).astype(bf16)],
                    axis=1,
                )
                product = jnp.dot(left[u], mixed, preferred_element_type=f32)
                total = product if total is None else total + product
        part_out[pos] = total.astype(bf16)
        to_sibling(pos).start()
        part[pos] = total

    def add_up(k):
        pos = pos_of(k)
        to_sibling(pos).wait_recv()
        live = (half_row < left_sizes[b]) & (half_column < states_of[k, 2])
        for r in range(2):
            cut = slice(r * half, (r + 1) * half)
            total = part[pos, :, cut] + part_in[pos, :, cut].astype(f32)
            fin[pos, r] = jnp.where(live, total, 0.0).astype(bf16)
        to_peer(pos).start()

    def pass_on(k):
        pos = pos_of(k)
        to_peer(pos).wait_recv()
        passing(pos, c).start()

    def step(k, _):
        @pl.when(k >= 5)
        def _():
            add_up(k - 1)

        @pl.when(k == 7)
        def _():
            pass_on(4)
            pass_on(5)

            @pl.when(end)
            def _():
                for h in lo:
                    sent(0, 0, h, (L, X))
                for events in end_before.values():
                    for e in events:
                        sent(*e)

            @pl.when(jnp.logical_not(end))
            def _():
                for h in lo:
                    sent(0, 0, h, (L, S, X))
                for stage, events in mid_before.items():
                    for e in events:
                        if stage != 6:
                            sent(*e)

        for stage in range(1, n):
            if stage in end_before or stage in mid_before:
                @pl.when(k == stage)
                def _():
                    run(stage)

        compute(k)

        @pl.when((k >= 1) & (k < 5))
        def _():
            add_up(k - 1)

        @pl.when((k >= 3) & (k < 7))
        def _():
            pass_on(k - 3)

        return 0

    lax.fori_loop(0, n, step, 0)
    pass_on(6)
    add_up(7)
    for h in range(channels):
        first(h).wait_send()
        left_to_peer(h).wait_send()
    ops_to_peer.wait_send()

    @pl.when(jnp.logical_not(end))
    def _():
        for e in mid_before[6]:
            sent(*e)

    def settle(pos, _):
        to_sibling(pos).wait_send()
        to_peer(pos).wait_send()
        return 0

    lax.fori_loop(0, n, settle, 0)
    pass_on(7)

    def all_here(pos, _):
        passing(pos, 1 - c).wait_recv()
        return 0

    lax.fori_loop(0, n, all_here, 0)
    mine_at = pl.ds(pl.multiple_of(y * half, half), half)
    others_at = pl.ds(pl.multiple_of((1 - y) * half, half), half)
    for q in range(per):
        pos, rank = mine[q, 0], mine[q, 1]
        out_ref[q, :, mine_at] = fin[pos, rank]
        out_ref[q, :, others_at] = arr[pos, rank]

    def let_go(pos, _):
        passing(pos, c).wait_send()
        return 0

    lax.fori_loop(0, n, let_go, 0)


def shards(n, m, wave_blocks, left_environment, right_environment, site_operators,
           right_sector, left_sizes, right_sizes, sector_place):
    states, rows = wave_blocks.shape[1:3]
    channels = left_environment.shape[0]
    per = states // m
    cores = 2 if m % 2 == 0 else 1
    ny = m // cores
    count = ny * per
    remote = max(1, (ny - 1) * per)
    block = (rows, rows)
    bf16, f32 = jnp.bfloat16, jnp.float32
    smem = pl.BlockSpec(memory_space=pltpu.SMEM)
    hbm = pl.BlockSpec(memory_space=pl.ANY)
    dma = pltpu.SemaphoreType.DMA
    nz, nx = plane_of(n)
    by_halves = (nz, nx, ny, cores, channels) == (4, 2, 2, 2, 2) and states == 2 * n
    if by_halves:
        half = (rows // 2, rows)
        tall = (rows, rows // 2)
        scratch = [
            pltpu.VMEM((n, 2 * channels) + half, bf16),
            pltpu.VMEM((states,) + block, bf16),
            pltpu.VMEM((2 * channels,) + block, bf16),
            pltpu.VMEM((2 * channels, states, states), bf16),
            pltpu.VMEM((2 * channels, 2, states, 128), f32),
            pltpu.VMEM((n,) + block, f32),
            pltpu.VMEM((n,) + block, bf16),
            pltpu.VMEM((n,) + block, bf16),
            pltpu.VMEM((n, 2) + tall, bf16),
            pltpu.VMEM((n, 2) + tall, bf16),
            pltpu.SMEM((n, 3), jnp.int32),
            pltpu.SMEM((per, 2), jnp.int32),
            dma((2 + channels,)),
            dma((n, 2 * channels, 3)), dma((n, 2 * channels)),
            dma((channels,)), dma((channels,)), dma((channels,)), dma, dma,
            dma((n,)), dma((n,)), dma((n,)), dma((n,)), dma((n,)), dma((n,)),
        ]
    elif ny == 2 and cores == 2:
        rest = [
            pltpu.VMEM((n,) + block, f32),
            pltpu.VMEM((n,) + block, bf16),
            pltpu.VMEM((n,) + block, bf16),
            pltpu.VMEM((2, n, 2) + block, bf16),
            dma((n,)), dma((n,)), dma((3, n)), dma((2, n, 2)),
        ]
    else:
        rest = [
            pltpu.VMEM((2 * n, channels) + block, bf16),
            pltpu.VMEM((count,) + block, bf16),
            pltpu.VMEM((count,) + block, bf16),
            pltpu.VMEM((remote,) + block, bf16),
            pltpu.VMEM((remote,) + block, bf16),
            pltpu.VMEM((per,) + block, f32),
            dma((count,)), dma((count,)), dma((remote,)), dma((remote,)),
        ]
    if not by_halves:
        scratch = [
            pltpu.VMEM((n, channels) + block, bf16),
            pltpu.VMEM((states,) + block, bf16),
            pltpu.VMEM((channels,) + block, bf16),
            dma((3,)), dma((n, channels, 4)), dma((n, channels)),
            *rest,
        ]
    out = pl.pallas_call(
        functools.partial(halves_kernel if by_halves else kernel, n, m),
        out_shape=jax.ShapeDtypeStruct((per,) + block, bf16),
        in_specs=[smem] * 4 + [pl.BlockSpec(memory_space=pltpu.VMEM)] + [hbm] * 3,
        out_specs=pl.BlockSpec(memory_space=pltpu.VMEM),
        scratch_shapes=scratch,
        compiler_params=pltpu.CompilerParams(
            collective_id=0, has_side_effects=True, vmem_limit_bytes=60 * 1024 * 1024
        ),
    )(
        right_sector.reshape(states), sector_place, left_sizes, right_sizes,
        site_operators,
        wave_blocks.reshape((states,) + block),
        left_environment.reshape((channels,) + block),
        right_environment.reshape((channels,) + block),
    )
    return out.reshape((1, per) + block)


def solution(mesh):
    placed = (
        P("bond", None, None, None),
        P("mpo", "bond", None, None),
        P("mpo", "bond", None, None),
        P("mpo", None, None),
        P("bond", None, None),
        P(),
        P(),
        P(),
    )
    body = functools.partial(shards, mesh.shape["bond"], mesh.shape["mpo"])
    return jax.shard_map(
        body, mesh=mesh, in_specs=placed, out_specs=P("bond", "mpo", None, None), check_vma=False
    )
```

```python
import functools

import jax
import jax.numpy as jnp
from jax import lax
from jax.experimental import pallas as pl
from jax.experimental.pallas import tpu as pltpu
from jax.sharding import PartitionSpec as P

MESH = pl.DeviceIdType.MESH


def plane_of(count):
    nx = 1
    while (2 * nx) * (2 * nx) * 2 <= count and count % (2 * nx) == 0:
        nx *= 2
    return count // nx, nx


def kernel(
    n, m,
    sector, place, left_sizes, right_sizes, ops,
    wave_hbm, left_hbm, right_hbm,
    out_ref,
    right_all, wave, left, local_sem, gather_send, gather_recv, *rest,
):
    nz, nx = plane_of(n)
    cores = 2 if m % 2 == 0 else 1
    ny = m // cores
    states, rows, _ = wave.shape
    channels = left.shape[0]
    per = out_ref.shape[0]
    count = ny * per
    pair = ny == 2 and cores == 2
    if pair:
        (part, part_out, part_in, sums,
         part_send, part_recv, sum_send, sum_recv) = rest
    else:
        (mixed, out_core, in_core, out_chip, in_chip, own,
         core_send, core_recv, chip_send, chip_recv) = rest
    b = lax.axis_index("bond")
    p = lax.axis_index("mpo")
    z, x = b // nx, b % nx
    y, c = p // cores, p % cores
    sibling = y * cores + (1 - c)

    wave_copy = pltpu.make_async_copy(wave_hbm, wave, local_sem.at[0])
    left_copy = pltpu.make_async_copy(left_hbm, left, local_sem.at[1])
    own_copy = pltpu.make_async_copy(right_hbm, right_all.at[b], local_sem.at[2])
    wave_copy.start()
    left_copy.start()
    own_copy.start()

    steps = ((nx, z + 1 < nz), (-nx, z > 0), (1, x + 1 < nx), (-1, x > 0))
    barrier = pltpu.get_barrier_semaphore()
    greeted = ny
    for step, there in steps:
        greeted = greeted + there.astype(jnp.int32)

        @pl.when(there)
        def _():
            pl.semaphore_signal(barrier, inc=1, device_id=(b + step, p), device_id_type=MESH)

    pl.semaphore_signal(barrier, inc=1, device_id=(b, sibling), device_id_type=MESH)
    for dy in range(1, ny):
        other = lax.rem(y + dy, ny) * cores + c
        pl.semaphore_signal(barrier, inc=1, device_id=(b, other), device_id_type=MESH)
    pl.semaphore_wait(barrier, greeted)

    def hop(pos, h, k, src):
        return pltpu.make_async_remote_copy(
            src_ref=src,
            dst_ref=right_all.at[pos, h],
            send_sem=gather_send.at[pos, h, k],
            recv_sem=gather_recv.at[pos, h],
            device_id=(b + steps[k][0], p),
            device_id_type=MESH,
        )

    def sends(zs, xs, h):
        column = xs == x
        if nx == 2 and h == channels - 1 and channels > 1:
            detour = (zs == 0) | (zs == nz - 1)
            along, across = column | detour, ~detour | (zs == z)
        else:
            along, across = column, True
        return (
            along & (zs <= z) & (z + 1 < nz),
            along & (zs >= z) & (z > 0),
            across & (xs <= x) & (x + 1 < nx),
            across & (xs >= x) & (x > 0),
        )

    def forward(zs, xs, h):
        pos = zs * nx + xs
        for k, wanted in enumerate(sends(zs, xs, h)):
            @pl.when(wanted)
            def _():
                hop(pos, h, k, right_all.at[pos, h]).start()

    def arrived(pos, h):
        hop(pos, h, 0, right_all.at[pos, h]).wait_recv()

    for h in range(channels):
        for k in (0, 1, 2, 3):
            @pl.when(steps[k][1])
            def _():
                hop(b, h, k, right_hbm.at[h]).start()

    wave_copy.wait()
    left_copy.wait()
    own_copy.wait()

    row_index = lax.broadcasted_iota(jnp.int32, (rows, rows), 0)
    column_index = lax.broadcasted_iota(jnp.int32, (rows, rows), 1)
    live_rows = row_index < left_sizes[b]
    op_row = lax.broadcasted_iota(jnp.int32, (states, states), 0)
    op_column = lax.broadcasted_iota(jnp.int32, (states, states), 1)

    def to_sibling(pos):
        return pltpu.make_async_remote_copy(
            src_ref=part_out.at[pos], dst_ref=part_in.at[pos],
            send_sem=part_send.at[pos], recv_sem=part_recv.at[pos],
            device_id=(b, sibling), device_id_type=MESH,
        )

    def share(kind, pos):
        source, target = (0, 0, 1)[kind], (0, 1, 1)[kind]
        device = (1 - y) * cores + c if kind == 1 else sibling
        return pltpu.make_async_remote_copy(
            src_ref=sums.at[source, pos, c], dst_ref=sums.at[target, pos, c],
            send_sem=sum_send.at[kind, pos], recv_sem=sum_recv.at[target, pos, c],
            device_id=(b, device), device_id_type=MESH,
        )

    def sum_arrived(target, pos, rank):
        pltpu.make_async_remote_copy(
            src_ref=sums.at[target, pos, rank], dst_ref=sums.at[target, pos, rank],
            send_sem=sum_send.at[0, pos], recv_sem=sum_recv.at[target, pos, rank],
            device_id=(b, sibling), device_id_type=MESH,
        ).wait_recv()

    def add_up(pos):
        to_sibling(pos).wait_recv()
        sums[0, pos, c] = (part[pos] + part_in[pos].astype(jnp.float32)).astype(jnp.bfloat16)
        share(1, pos).start()
        share(0, pos).start()

    def pass_on(pos):
        sum_arrived(1, pos, c)
        share(2, pos).start()

    def work(pos):
        def look(s, carry):
            first, last, hits = carry
            hit = place[sector[s]] == pos
            first = jnp.where(hit & (hits == 0), s, first)
            last = jnp.where(hit, s, last)
            return first, last, hits + hit.astype(jnp.int32)

        zero = jnp.int32(0)
        s1, s2, hits = lax.fori_loop(0, states, look, (zero, zero, zero), unroll=True)
        if pair:
            s1, s2 = jnp.where(c == 0, s1, s2), jnp.where(c == 0, s2, s1)
        live = live_rows & (column_index < right_sizes[sector[s1]])

        def masked(s):
            return jnp.where(live, wave[s].astype(jnp.float32), 0.0).astype(jnp.bfloat16)

        both = jnp.concatenate([masked(s1), masked(s2)], axis=0)
        two = hits == 2
        for h in range(channels):
            factor = right_all[pos, h]

            parts = lax.dot_general(
                both, factor, (((1,), (1,)), ((), ())), preferred_element_type=jnp.float32
            ).astype(jnp.bfloat16).astype(jnp.float32)
            p1, p2 = parts[:rows], parts[rows:]
            table = ops[h].astype(jnp.float32)

            def op(s, t, keep=True):
                picked = (op_row == s) & (op_column == t) & keep
                return jnp.sum(jnp.where(picked, table, 0.0), keepdims=True)

            m1 = (op(s1, s1) * p1 + op(s1, s2, two) * p2).astype(jnp.bfloat16)
            m2 = (op(s2, s1, two) * p1 + op(s2, s2) * p2).astype(jnp.bfloat16)
            if pair:
                left_m = left[h]
                q1 = jnp.dot(left_m, m1, preferred_element_type=jnp.float32)
                q2 = jnp.dot(left_m, m2, preferred_element_type=jnp.float32)
                total1, total2 = (q1, q2) if h == 0 else (total1 + q1, total2 + q2)
            else:
                mixed[2 * pos, h] = m1
                mixed[2 * pos + 1, h] = m2
        if pair:
            part_out[pos] = total2.astype(jnp.bfloat16)
            to_sibling(pos).start()
            part[pos] = total1

    def at(g, i, body):
        sign = 1 - 2 * (i % 2)
        e = i // 2
        d = g - (e > 0).astype(jnp.int32)
        zs = z + sign * d
        xs = x + (e + 1) // 2 * (1 - 2 * (e % 2))

        @pl.when((zs >= 0) & (zs < nz) & (xs >= 0) & (xs < nx) & (d >= 0) & ((d > 0) | (sign > 0)))
        def _():
            body(zs, xs)

    items = 2 * (2 * nx - 1)

    def each(g, body):
        def one(i, _):
            at(g, i, body)
            return 0

        lax.fori_loop(0, items, one, 0)

    def multiply(g):
        def one(i, _):
            @pl.when(i < items)
            def _():
                at(g, i, use)

            @pl.when(i >= 2)
            def _():
                at(g, i - 2, lambda zs, xs: add_up(zs * nx + xs))

            return 0

        lax.fori_loop(0, items + 2, one, 0)

    def use(zs, xs):
        pos = zs * nx + xs

        @pl.when(xs != x)
        def _():
            for h in range(channels):
                arrived(pos, h)
                forward(zs, xs, h)

        work(pos)

    def gather_round(g, _):
        @pl.when((g > 0) & (g < nz))
        def _():
            for h in range(channels):
                for sign in (1, -1):
                    zs = z + sign * g

                    @pl.when((zs >= 0) & (zs < nz))
                    def _():
                        arrived(zs * nx + x, h)
                        forward(zs, x, h)

        @pl.when(g <= nz)
        def _():
            if pair:
                multiply(g)
            else:
                each(g, use)

        if pair:
            @pl.when(g > 1)
            def _():
                each(g - 2, lambda zs, xs: pass_on(zs * nx + xs))

        return 0

    lax.fori_loop(0, nz + (3 if pair else 1), gather_round, 0)

    def rank_of(s):
        def look(t, rank):
            return rank + ((t < s) & (sector[t] == sector[s])).astype(jnp.int32)

        return jnp.minimum(lax.fori_loop(0, states, look, jnp.int32(0), unroll=True), 1)

    def finish(pos, _):
        for h in range(channels):
            for k, wanted in enumerate(sends(pos // nx, pos % nx, h)):
                @pl.when(wanted)
                def _():
                    hop(pos, h, k, right_all.at[pos, h]).wait_send()
        if pair:
            to_sibling(pos).wait_send()
            for kind in range(3):
                share(kind, pos).wait_send()
        return 0

    if pair:
        def all_here(pos, _):
            sum_arrived(0, pos, 1 - c)
            sum_arrived(1, pos, 1 - c)
            return 0

        lax.fori_loop(0, n, all_here, 0)
        for q in range(per):
            s = p * per + q
            at, rank = place[sector[s]], rank_of(s)
            total = sums[0, at, rank].astype(jnp.float32) + sums[1, at, rank].astype(jnp.float32)
            live = live_rows & (column_index < right_sizes[sector[s]])
            out_ref[q] = jnp.where(live, total, 0.0).astype(jnp.bfloat16)
        lax.fori_loop(0, n, finish, 0)
        return

    def product(s):
        slot = 2 * place[sector[s]] + rank_of(s)
        total = jnp.dot(left[0], mixed[slot, 0], preferred_element_type=jnp.float32)
        for h in range(1, channels):
            total += jnp.dot(left[h], mixed[slot, h], preferred_element_type=jnp.float32)
        return total

    def owner_chip(i):
        return lax.rem(y + 1 + i // per, ny)

    def to_core(i):
        return pltpu.make_async_remote_copy(
            src_ref=out_core.at[i], dst_ref=in_core.at[i],
            send_sem=core_send.at[i], recv_sem=core_recv.at[i],
            device_id=(b, sibling), device_id_type=MESH,
        )

    def to_chip(i):
        return pltpu.make_async_remote_copy(
            src_ref=out_chip.at[i], dst_ref=in_chip.at[i],
            send_sem=chip_send.at[i], recv_sem=chip_recv.at[i],
            device_id=(b, owner_chip(i) * cores + c), device_id_type=MESH,
        )

    remote = (ny - 1) * per
    lag = min(3, count)

    def reduce_step(i, _):
        @pl.when(i < count)
        def _():
            s = (owner_chip(i) * cores + (1 - c)) * per + i % per
            out_core[i] = product(s).astype(jnp.bfloat16)
            to_core(i).start()

        @pl.when(i >= lag)
        def _():
            j = i - lag
            s = (owner_chip(j) * cores + c) * per + j % per
            total = product(s)
            to_core(j).wait_recv()
            total = total + in_core[j].astype(jnp.float32)

            @pl.when(j < remote)
            def _():
                out_chip[j] = total.astype(jnp.bfloat16)
                to_chip(j).start()

            @pl.when(j >= remote)
            def _():
                own[j - remote] = total

        return 0

    lax.fori_loop(0, count + lag, reduce_step, 0)

    for q in range(per):
        total = own[q]
        for dy in range(ny - 1):
            to_chip(dy * per + q).wait_recv()
            total = total + in_chip[dy * per + q].astype(jnp.float32)
        live = live_rows & (column_index < right_sizes[sector[p * per + q]])
        out_ref[q] = jnp.where(live, total, 0.0).astype(jnp.bfloat16)

    lax.fori_loop(0, n, finish, 0)

    def finish_core(i, _):
        to_core(i).wait_send()
        return 0

    lax.fori_loop(0, count, finish_core, 0)

    def finish_chip(i, _):
        to_chip(i).wait_send()
        return 0

    lax.fori_loop(0, remote, finish_chip, 0)


def sum_of(k, values):
    if isinstance(k, int):
        return values[k]
    total = 0
    for i, v in enumerate(values):
        if v:
            total = total + (k == i).astype(jnp.int32) * v
    return total


def halves_kernel(
    n, m,
    sector, place, left_sizes, right_sizes, ops_ref,
    wave_hbm, left_hbm, right_hbm,
    out_ref,
    right_all, away, wave, left, ops, coef, part, part_out, part_in, fin, arr, states_of, mine,
    local_sem, gather_send, gather_recv, early_send, left_recv, ops_send, ops_recv,
    part_send, part_recv, fin_send, fin_recv, pass_send, pass_recv,
):
    nz, nx = plane_of(n)
    states, rows, _ = wave.shape
    half = rows // 2
    channels = left_hbm.shape[0]
    per = out_ref.shape[0]
    units = 2 * channels
    b = lax.axis_index("bond")
    p = lax.axis_index("mpo")
    z, x = b // nx, b % nx
    y, c = p // 2, p % 2
    sibling = y * 2 + (1 - c)
    peer = (1 - y) * 2 + c
    end = (z == 0) | (z == nz - 1)
    way = 1 - 2 * (z >= nz // 2).astype(jnp.int32)
    bf16, f32 = jnp.bfloat16, jnp.float32
    L, S, X = 0, 1, 2
    targets = (b + way * nx, b - way * nx, z * nx + (1 - x))

    def own_half(h, of):
        return right_hbm.at[h, pl.ds(pl.multiple_of(of * half, half), half)]

    wave_copy = pltpu.make_async_copy(wave_hbm, wave, local_sem.at[0])
    left_copy = pltpu.make_async_copy(left_hbm, left.at[pl.ds(0, channels)], local_sem.at[1])
    own_copies = [
        pltpu.make_async_copy(own_half(h, 1 - y), away.at[h], local_sem.at[2])
        for h in range(channels)
    ] + [
        pltpu.make_async_copy(own_half(h, y), right_all.at[b, h], local_sem.at[2])
        for h in range(channels)
    ]
    for own in own_copies:
        own.start()
    left_copy.start()
    wave_copy.start()

    barrier = pltpu.get_barrier_semaphore()
    for target in (L, X):
        pl.semaphore_signal(barrier, inc=1, device_id=(targets[target], p), device_id_type=MESH)

    @pl.when(jnp.logical_not(end))
    def _():
        pl.semaphore_signal(barrier, inc=1, device_id=(targets[S], p), device_id_type=MESH)

    for other in (sibling, peer):
        pl.semaphore_signal(barrier, inc=1, device_id=(b, other), device_id_type=MESH)
    pl.semaphore_wait(barrier, 5 - end.astype(jnp.int32))

    def to_device(src, dst, send, recv, device):
        return pltpu.make_async_remote_copy(
            src_ref=src, dst_ref=dst, send_sem=send, recv_sem=recv,
            device_id=device, device_id_type=MESH,
        )

    def hop(pos, u, kind, src, batch=1):
        return to_device(
            src, right_all.at[pos, u], gather_send.at[batch], gather_recv.at[pos, u],
            (targets[kind], p),
        )

    def first(h):
        return to_device(
            away.at[h], right_all.at[b, channels + h], early_send,
            gather_recv.at[b, channels + h], (b, peer),
        )

    def left_to_peer(h):
        return to_device(
            left.at[h], left.at[channels + h], early_send, left_recv, (b, peer)
        )

    ops_to_peer = to_device(
        ops_ref, ops.at[pl.ds(channels, channels)], ops_send, ops_recv, (b, peer)
    )

    pltpu.make_async_copy(right_hbm, left.at[pl.ds(0, channels)], local_sem.at[2]).wait()
    for h in range(channels):
        first(h).start()
        for kind in (L, X):
            hop(b, h, kind, right_all.at[b, h], 0).start()

        @pl.when(jnp.logical_not(end))
        def _():
            hop(b, h, S, right_all.at[b, h], 0).start()

    left_copy.wait()
    ops_to_peer.start()
    for h in range(channels):
        left_to_peer(h).start()

    def place_of(off, other):
        return (z + way * off) * nx + ((1 - x) if other else x)

    def event(off, other, u, kinds):
        pos = place_of(off, other)
        hop(pos, u, X, right_all.at[pos, u]).wait_recv()
        for kind in kinds:
            hop(pos, u, kind, right_all.at[pos, u], 0 if (off, other) == (0, 0) else 1).start()

    def settled(view, sem):
        to_device(view, view, sem, sem, (b, sibling)).wait_send()

    lo, hi = range(channels), range(channels, units)
    end_order = [(0, 0), (0, 1), (1, 0), (1, 1), (2, 0), (2, 1), (3, 0), (3, 1)]
    mid_order = [(0, 0), (0, 1), (-1, 0), (1, 0), (-1, 1), (2, 0), (1, 1), (2, 1)]
    end_before = {
        "own": [(0, 0, 2, (L, X)), (1, 0, 0, (X,)), (0, 0, 3, (L, X)), (1, 0, 1, (X,))],
        "start": [(1, 0, u, (X,)) for u in hi]
        + [(0, 1, u, ()) for u in lo] + [(0, 1, u, (L,)) for u in hi] + [(2, 0, 0, (X,))],
        1: [(2, 0, 1, (X,))],
        2: [(2, 0, 2, (X,))],
        3: [(2, 0, 3, (X,))] + [(1, 1, u, ()) for u in range(units)],
        4: [(3, 0, 0, (X,))],
        5: [(3, 0, 1, (X,))],
        "5+": [(2, 1, u, ()) for u in range(units)],
        6: [(3, 0, u, ()) for u in hi],
        7: [(3, 1, u, ()) for u in range(units)],
    }
    mid_before = {
        "own": [
            (0, 0, 2, (L, S, X)), (0, 0, 3, (L, S, X)),
            (-1, 0, 0, (L, X)), (1, 0, 0, (S, X)), (-1, 0, 1, (L, X)), (1, 0, 1, (S, X)),
        ],
        "start": [
            (-1, 0, 2, (L,)), (1, 0, 2, (S, X)), (-1, 0, 3, (L,)), (1, 0, 3, (S, X)),
        ] + [(0, 1, u, ()) for u in range(units)] + [(2, 0, 0, (S, X))],
        1: [(2, 0, 1, (S, X)), (-1, 1, 2, (L,))],
        2: [(-1, 1, 3, (L,)), (2, 0, 2, (S,))],
        3: [(2, 0, 3, (S,))],
        4: [(2, 1, 2, (S,))] + [(-1, 1, u, ()) for u in lo],
        5: [(2, 1, 3, (S,))],
        6: [(1, 1, u, ()) for u in range(units)],
        7: [(2, 1, u, ()) for u in lo],
    }

    def run(stage):
        @pl.when(end)
        def _():
            for e in end_before.get(stage, ()):
                event(*e)

        @pl.when(jnp.logical_not(end))
        def _():
            for e in mid_before.get(stage, ()):
                event(*e)

    def pos_of(k):
        off = jnp.where(end, sum_of(k, [o for o, _ in end_order]), sum_of(k, [o for o, _ in mid_order]))
        other = jnp.where(end, sum_of(k, [o for _, o in end_order]), sum_of(k, [o for _, o in mid_order]))
        return (z + way * off) * nx + x + other * (1 - 2 * x)

    def list_states(k, _):
        pos = pos_of(k)

        def look(s, carry):
            s1, s2 = carry
            hit = place[sector[s]] == pos
            return jnp.where(hit & (s < s1), s, s1), jnp.where(hit, s, s2)

        s1, s2 = lax.fori_loop(0, states, look, (jnp.int32(states - 1), jnp.int32(0)), unroll=True)
        states_of[k, 0] = s1
        states_of[k, 1] = s2
        states_of[k, 2] = right_sizes[sector[s1]]
        return 0

    lax.fori_loop(0, n, list_states, 0)

    def list_mine(q, _):
        s = p * per + q

        def look(t, rank):
            return rank + ((t < s) & (sector[t] == sector[s])).astype(jnp.int32)

        mine[q, 0] = place[sector[s]]
        mine[q, 1] = jnp.minimum(lax.fori_loop(0, states, look, jnp.int32(0), unroll=True), 1)
        return 0

    lax.fori_loop(0, per, list_mine, 0)

    def pick_operators():
        ops_to_peer.wait_recv()
        square = (states, states)
        op_row = lax.broadcasted_iota(jnp.int32, square, 0)
        op_column = lax.broadcasted_iota(jnp.int32, square, 1)
        named = jnp.zeros(square, jnp.int32)
        for r in range(states):
            named = jnp.where(op_row == r, states_of[r // 2, r % 2], named)
        pick = jnp.where(named == op_column, 1.0, 0.0).astype(bf16)
        same = op_row == op_column
        twin = op_row + 1 - 2 * (op_row % 2) == op_column
        for u in range(units):
            picked = jnp.dot(pick, ops[u], preferred_element_type=f32).astype(bf16)
            table = lax.dot_general(
                picked, pick, (((1,), (1,)), ((), ())), preferred_element_type=f32
            )
            for i, chosen in enumerate((same, twin)):
                column = jnp.sum(jnp.where(chosen, table, 0.0), axis=1, keepdims=True)
                coef[u, i] = jnp.broadcast_to(column, (states, 128))

    ops[pl.ds(0, channels)] = ops_ref[...]
    run("own")
    pick_operators()
    run("start")

    wave_copy.wait()
    both_left = left.at[pl.ds(channels, channels)]
    to_device(both_left, both_left, early_send, left_recv, (b, peer)).wait_recv()

    row_index = lax.broadcasted_iota(jnp.int32, (rows, rows), 0)
    column_index = lax.broadcasted_iota(jnp.int32, (rows, rows), 1)
    half_row = lax.broadcasted_iota(jnp.int32, (rows, half), 0)
    half_column = lax.broadcasted_iota(jnp.int32, (rows, half), 1) + y * half

    def to_sibling(pos):
        return to_device(
            part_out.at[pos], part_in.at[pos], part_send, part_recv.at[pos], (b, sibling)
        )

    def to_peer(pos):
        return to_device(
            fin.at[pos, c], arr.at[pos, c], fin_send, fin_recv.at[pos], (b, peer)
        )

    def passing(pos, rank):
        return to_device(
            arr.at[pos, rank], arr.at[pos, rank], pass_send, pass_recv, (b, sibling)
        )

    def compute(k):
        pos = pos_of(k)
        s1, s2 = states_of[k, 0], states_of[k, 1]
        live = (row_index < left_sizes[b]) & (column_index < states_of[k, 2])

        def masked(s):
            return jnp.where(live, wave[s].astype(f32), 0.0).astype(bf16)

        both = jnp.concatenate([masked(s1), masked(s2)], axis=0)
        total = None
        for g in range(2):
            factor = right_all[pos, pl.ds(g * channels, channels)].reshape(channels * half, rows)
            parts = lax.dot_general(
                both, factor, (((1,), (1,)), ((), ())), preferred_element_type=f32
            ).astype(bf16).astype(f32)
            for h in range(channels):
                u = g * channels + h
                p1 = parts[:rows, h * half:(h + 1) * half]
                p2 = parts[rows:, h * half:(h + 1) * half]
                own1, own2 = coef[u, 0, pl.ds(2 * k, 1)], coef[u, 0, pl.ds(2 * k + 1, 1)]
                cross1, cross2 = coef[u, 1, pl.ds(2 * k, 1)], coef[u, 1, pl.ds(2 * k + 1, 1)]
                mixed = jnp.concatenate(
                    [(own1 * p1 + cross1 * p2).astype(bf16), (cross2 * p1 + own2 * p2).astype(bf16)],
                    axis=1,
                )
                product = jnp.dot(left[u], mixed, preferred_element_type=f32)
                total = product if total is None else total + product
        part_out[pos] = total.astype(bf16)
        to_sibling(pos).start()
        part[pos] = total

    def add_up(k):
        pos = pos_of(k)
        to_sibling(pos).wait_recv()
        live = (half_row < left_sizes[b]) & (half_column < states_of[k, 2])
        for r in range(2):
            cut = slice(r * half, (r + 1) * half)
            total = part[pos, :, cut] + part_in[pos, :, cut].astype(f32)
            fin[pos, r] = jnp.where(live, total, 0.0).astype(bf16)
        to_peer(pos).start()

    def pass_on(k):
        pos = pos_of(k)
        to_peer(pos).wait_recv()
        passing(pos, c).start()

    def free_sends():
        settled(left.at[pl.ds(0, channels + channels // 2)], early_send)
        ops_to_peer.wait_send()

        @pl.when(end)
        def _():
            settled(right_all.at[pl.ds(0, 2)], gather_send.at[0])
            settled(right_all.at[pl.ds(0, 3)], gather_send.at[1])

        @pl.when(jnp.logical_not(end))
        def _():
            settled(right_all.at[pl.ds(0, 3)], gather_send.at[0])

    def step(k, _):
        for stage in range(1, n):
            @pl.when(k == stage)
            def _():
                if stage == 7:
                    add_up(6)
                    pass_on(3)
                    pass_on(4)
                    free_sends()
                run(stage)
                if stage == 5:
                    add_up(4)
                    pass_on(1)
                    run("5+")

        compute(k)

        @pl.when((k >= 1) & (k != 5) & (k != 7))
        def _():
            add_up(k - 1)

        @pl.when((k == 4) | (k == 6))
        def _():
            pass_on(k - 4)

        return 0

    lax.fori_loop(0, n, step, 0)
    add_up(7)
    pass_on(5)
    pass_on(6)

    @pl.when(jnp.logical_not(end))
    def _():
        settled(right_all.at[pl.ds(0, 6)], gather_send.at[1])

    settled(part_out, part_send)
    settled(arr.at[pl.ds(0, n // 2)], fin_send)
    pass_on(7)
    passed = arr.at[pl.ds(0, n // 2)]
    to_device(passed, passed, pass_send, pass_recv, (b, sibling)).wait_recv()
    mine_at = pl.ds(pl.multiple_of(y * half, half), half)
    others_at = pl.ds(pl.multiple_of((1 - y) * half, half), half)
    for q in range(per):
        pos, rank = mine[q, 0], mine[q, 1]
        out_ref[q, :, mine_at] = fin[pos, rank]
        out_ref[q, :, others_at] = arr[pos, rank]

    settled(arr.at[pl.ds(0, n // 2)], pass_send)


def shards(n, m, wave_blocks, left_environment, right_environment, site_operators,
           right_sector, left_sizes, right_sizes, sector_place):
    states, rows = wave_blocks.shape[1:3]
    channels = left_environment.shape[0]
    per = states // m
    cores = 2 if m % 2 == 0 else 1
    ny = m // cores
    count = ny * per
    remote = max(1, (ny - 1) * per)
    block = (rows, rows)
    bf16, f32 = jnp.bfloat16, jnp.float32
    smem = pl.BlockSpec(memory_space=pltpu.SMEM)
    hbm = pl.BlockSpec(memory_space=pl.ANY)
    dma = pltpu.SemaphoreType.DMA
    nz, nx = plane_of(n)
    by_halves = (nz, nx, ny, cores, channels) == (4, 2, 2, 2, 2) and states == 2 * n
    if by_halves:
        half = (rows // 2, rows)
        tall = (rows, rows // 2)
        scratch = [
            pltpu.VMEM((n, 2 * channels) + half, bf16),
            pltpu.VMEM((channels,) + half, bf16),
            pltpu.VMEM((states,) + block, bf16),
            pltpu.VMEM((2 * channels,) + block, bf16),
            pltpu.VMEM((2 * channels, states, states), bf16),
            pltpu.VMEM((2 * channels, 2, states, 128), f32),
            pltpu.VMEM((n,) + block, f32),
            pltpu.VMEM((n,) + block, bf16),
            pltpu.VMEM((n,) + block, bf16),
            pltpu.VMEM((n, 2) + tall, bf16),
            pltpu.VMEM((n, 2) + tall, bf16),
            pltpu.SMEM((n, 3), jnp.int32),
            pltpu.SMEM((per, 2), jnp.int32),
            dma((3,)), dma((2,)), dma((n, 2 * channels)), dma, dma, dma, dma,
            dma, dma((n,)), dma, dma((n,)), dma, dma,
        ]
    elif ny == 2 and cores == 2:
        rest = [
            pltpu.VMEM((n,) + block, f32),
            pltpu.VMEM((n,) + block, bf16),
            pltpu.VMEM((n,) + block, bf16),
            pltpu.VMEM((2, n, 2) + block, bf16),
            dma((n,)), dma((n,)), dma((3, n)), dma((2, n, 2)),
        ]
    else:
        rest = [
            pltpu.VMEM((2 * n, channels) + block, bf16),
            pltpu.VMEM((count,) + block, bf16),
            pltpu.VMEM((count,) + block, bf16),
            pltpu.VMEM((remote,) + block, bf16),
            pltpu.VMEM((remote,) + block, bf16),
            pltpu.VMEM((per,) + block, f32),
            dma((count,)), dma((count,)), dma((remote,)), dma((remote,)),
        ]
    if not by_halves:
        scratch = [
            pltpu.VMEM((n, channels) + block, bf16),
            pltpu.VMEM((states,) + block, bf16),
            pltpu.VMEM((channels,) + block, bf16),
            dma((3,)), dma((n, channels, 4)), dma((n, channels)),
            *rest,
        ]
    out = pl.pallas_call(
        functools.partial(halves_kernel if by_halves else kernel, n, m),
        out_shape=pltpu.VMEM((per,) + block, bf16),
        in_specs=[smem] * 4 + [pl.BlockSpec(memory_space=pltpu.VMEM)] + [hbm] * 3,
        out_specs=pl.BlockSpec(memory_space=pltpu.VMEM),
        scratch_shapes=scratch,
        compiler_params=pltpu.CompilerParams(
            collective_id=0, has_side_effects=True, vmem_limit_bytes=60 * 1024 * 1024
        ),
    )(
        right_sector.reshape(states), sector_place, left_sizes, right_sizes,
        site_operators,
        wave_blocks.reshape((states,) + block),
        left_environment.reshape((channels,) + block),
        right_environment.reshape((channels,) + block),
    )
    return out.reshape((1, per) + block)


def solution(mesh):
    placed = (
        P("bond", None, None, None),
        P("mpo", "bond", None, None),
        P("mpo", "bond", None, None),
        P("mpo", None, None),
        P("bond", None, None),
        P(),
        P(),
        P(),
    )
    body = functools.partial(shards, mesh.shape["bond"], mesh.shape["mpo"])
    return jax.shard_map(
        body, mesh=mesh, in_specs=placed, out_specs=P("bond", "mpo", None, None), check_vma=False
    )
```

```python
import functools

import jax
import jax.numpy as jnp
from jax import lax
from jax.experimental import pallas as pl
from jax.experimental.pallas import tpu as pltpu
from jax.sharding import PartitionSpec as P

MESH = pl.DeviceIdType.MESH


def plane_of(count):
    nx = 1
    while (2 * nx) * (2 * nx) * 2 <= count and count % (2 * nx) == 0:
        nx *= 2
    return count // nx, nx


def kernel(
    n, m,
    sector, place, left_sizes, right_sizes, ops,
    wave_hbm, left_hbm, right_hbm,
    out_ref,
    right_all, wave, left, local_sem, gather_send, gather_recv, *rest,
):
    nz, nx = plane_of(n)
    cores = 2 if m % 2 == 0 else 1
    ny = m // cores
    states, rows, _ = wave.shape
    channels = left.shape[0]
    per = out_ref.shape[0]
    count = ny * per
    pair = ny == 2 and cores == 2
    if pair:
        (part, part_out, part_in, sums,
         part_send, part_recv, sum_send, sum_recv) = rest
    else:
        (mixed, out_core, in_core, out_chip, in_chip, own,
         core_send, core_recv, chip_send, chip_recv) = rest
    b = lax.axis_index("bond")
    p = lax.axis_index("mpo")
    z, x = b // nx, b % nx
    y, c = p // cores, p % cores
    sibling = y * cores + (1 - c)

    wave_copy = pltpu.make_async_copy(wave_hbm, wave, local_sem.at[0])
    left_copy = pltpu.make_async_copy(left_hbm, left, local_sem.at[1])
    own_copy = pltpu.make_async_copy(right_hbm, right_all.at[b], local_sem.at[2])
    wave_copy.start()
    left_copy.start()
    own_copy.start()

    steps = ((nx, z + 1 < nz), (-nx, z > 0), (1, x + 1 < nx), (-1, x > 0))
    barrier = pltpu.get_barrier_semaphore()
    greeted = ny
    for step, there in steps:
        greeted = greeted + there.astype(jnp.int32)

        @pl.when(there)
        def _():
            pl.semaphore_signal(barrier, inc=1, device_id=(b + step, p), device_id_type=MESH)

    pl.semaphore_signal(barrier, inc=1, device_id=(b, sibling), device_id_type=MESH)
    for dy in range(1, ny):
        other = lax.rem(y + dy, ny) * cores + c
        pl.semaphore_signal(barrier, inc=1, device_id=(b, other), device_id_type=MESH)
    pl.semaphore_wait(barrier, greeted)

    def hop(pos, h, k, src):
        return pltpu.make_async_remote_copy(
            src_ref=src,
            dst_ref=right_all.at[pos, h],
            send_sem=gather_send.at[pos, h, k],
            recv_sem=gather_recv.at[pos, h],
            device_id=(b + steps[k][0], p),
            device_id_type=MESH,
        )

    def sends(zs, xs, h):
        column = xs == x
        if nx == 2 and h == channels - 1 and channels > 1:
            detour = (zs == 0) | (zs == nz - 1)
            along, across = column | detour, ~detour | (zs == z)
        else:
            along, across = column, True
        return (
            along & (zs <= z) & (z + 1 < nz),
            along & (zs >= z) & (z > 0),
            across & (xs <= x) & (x + 1 < nx),
            across & (xs >= x) & (x > 0),
        )

    def forward(zs, xs, h):
        pos = zs * nx + xs
        for k, wanted in enumerate(sends(zs, xs, h)):
            @pl.when(wanted)
            def _():
                hop(pos, h, k, right_all.at[pos, h]).start()

    def arrived(pos, h):
        hop(pos, h, 0, right_all.at[pos, h]).wait_recv()

    for h in range(channels):
        for k in (0, 1, 2, 3):
            @pl.when(steps[k][1])
            def _():
                hop(b, h, k, right_hbm.at[h]).start()

    wave_copy.wait()
    left_copy.wait()
    own_copy.wait()

    row_index = lax.broadcasted_iota(jnp.int32, (rows, rows), 0)
    column_index = lax.broadcasted_iota(jnp.int32, (rows, rows), 1)
    live_rows = row_index < left_sizes[b]
    op_row = lax.broadcasted_iota(jnp.int32, (states, states), 0)
    op_column = lax.broadcasted_iota(jnp.int32, (states, states), 1)

    def to_sibling(pos):
        return pltpu.make_async_remote_copy(
            src_ref=part_out.at[pos], dst_ref=part_in.at[pos],
            send_sem=part_send.at[pos], recv_sem=part_recv.at[pos],
            device_id=(b, sibling), device_id_type=MESH,
        )

    def share(kind, pos):
        source, target = (0, 0, 1)[kind], (0, 1, 1)[kind]
        device = (1 - y) * cores + c if kind == 1 else sibling
        return pltpu.make_async_remote_copy(
            src_ref=sums.at[source, pos, c], dst_ref=sums.at[target, pos, c],
            send_sem=sum_send.at[kind, pos], recv_sem=sum_recv.at[target, pos, c],
            device_id=(b, device), device_id_type=MESH,
        )

    def sum_arrived(target, pos, rank):
        pltpu.make_async_remote_copy(
            src_ref=sums.at[target, pos, rank], dst_ref=sums.at[target, pos, rank],
            send_sem=sum_send.at[0, pos], recv_sem=sum_recv.at[target, pos, rank],
            device_id=(b, sibling), device_id_type=MESH,
        ).wait_recv()

    def add_up(pos):
        to_sibling(pos).wait_recv()
        sums[0, pos, c] = (part[pos] + part_in[pos].astype(jnp.float32)).astype(jnp.bfloat16)
        share(1, pos).start()
        share(0, pos).start()

    def pass_on(pos):
        sum_arrived(1, pos, c)
        share(2, pos).start()

    def work(pos):
        def look(s, carry):
            first, last, hits = carry
            hit = place[sector[s]] == pos
            first = jnp.where(hit & (hits == 0), s, first)
            last = jnp.where(hit, s, last)
            return first, last, hits + hit.astype(jnp.int32)

        zero = jnp.int32(0)
        s1, s2, hits = lax.fori_loop(0, states, look, (zero, zero, zero), unroll=True)
        if pair:
            s1, s2 = jnp.where(c == 0, s1, s2), jnp.where(c == 0, s2, s1)
        live = live_rows & (column_index < right_sizes[sector[s1]])

        def masked(s):
            return jnp.where(live, wave[s].astype(jnp.float32), 0.0).astype(jnp.bfloat16)

        both = jnp.concatenate([masked(s1), masked(s2)], axis=0)
        two = hits == 2
        for h in range(channels):
            factor = right_all[pos, h]

            parts = lax.dot_general(
                both, factor, (((1,), (1,)), ((), ())), preferred_element_type=jnp.float32
            ).astype(jnp.bfloat16).astype(jnp.float32)
            p1, p2 = parts[:rows], parts[rows:]
            table = ops[h].astype(jnp.float32)

            def op(s, t, keep=True):
                picked = (op_row == s) & (op_column == t) & keep
                return jnp.sum(jnp.where(picked, table, 0.0), keepdims=True)

            m1 = (op(s1, s1) * p1 + op(s1, s2, two) * p2).astype(jnp.bfloat16)
            m2 = (op(s2, s1, two) * p1 + op(s2, s2) * p2).astype(jnp.bfloat16)
            if pair:
                left_m = left[h]
                q1 = jnp.dot(left_m, m1, preferred_element_type=jnp.float32)
                q2 = jnp.dot(left_m, m2, preferred_element_type=jnp.float32)
                total1, total2 = (q1, q2) if h == 0 else (total1 + q1, total2 + q2)
            else:
                mixed[2 * pos, h] = m1
                mixed[2 * pos + 1, h] = m2
        if pair:
            part_out[pos] = total2.astype(jnp.bfloat16)
            to_sibling(pos).start()
            part[pos] = total1

    def at(g, i, body):
        sign = 1 - 2 * (i % 2)
        e = i // 2
        d = g - (e > 0).astype(jnp.int32)
        zs = z + sign * d
        xs = x + (e + 1) // 2 * (1 - 2 * (e % 2))

        @pl.when((zs >= 0) & (zs < nz) & (xs >= 0) & (xs < nx) & (d >= 0) & ((d > 0) | (sign > 0)))
        def _():
            body(zs, xs)

    items = 2 * (2 * nx - 1)

    def each(g, body):
        def one(i, _):
            at(g, i, body)
            return 0

        lax.fori_loop(0, items, one, 0)

    def multiply(g):
        def one(i, _):
            @pl.when(i < items)
            def _():
                at(g, i, use)

            @pl.when(i >= 2)
            def _():
                at(g, i - 2, lambda zs, xs: add_up(zs * nx + xs))

            return 0

        lax.fori_loop(0, items + 2, one, 0)

    def use(zs, xs):
        pos = zs * nx + xs

        @pl.when(xs != x)
        def _():
            for h in range(channels):
                arrived(pos, h)
                forward(zs, xs, h)

        work(pos)

    def gather_round(g, _):
        @pl.when((g > 0) & (g < nz))
        def _():
            for h in range(channels):
                for sign in (1, -1):
                    zs = z + sign * g

                    @pl.when((zs >= 0) & (zs < nz))
                    def _():
                        arrived(zs * nx + x, h)
                        forward(zs, x, h)

        @pl.when(g <= nz)
        def _():
            if pair:
                multiply(g)
            else:
                each(g, use)

        if pair:
            @pl.when(g > 1)
            def _():
                each(g - 2, lambda zs, xs: pass_on(zs * nx + xs))

        return 0

    lax.fori_loop(0, nz + (3 if pair else 1), gather_round, 0)

    def rank_of(s):
        def look(t, rank):
            return rank + ((t < s) & (sector[t] == sector[s])).astype(jnp.int32)

        return jnp.minimum(lax.fori_loop(0, states, look, jnp.int32(0), unroll=True), 1)

    def finish(pos, _):
        for h in range(channels):
            for k, wanted in enumerate(sends(pos // nx, pos % nx, h)):
                @pl.when(wanted)
                def _():
                    hop(pos, h, k, right_all.at[pos, h]).wait_send()
        if pair:
            to_sibling(pos).wait_send()
            for kind in range(3):
                share(kind, pos).wait_send()
        return 0

    if pair:
        def all_here(pos, _):
            sum_arrived(0, pos, 1 - c)
            sum_arrived(1, pos, 1 - c)
            return 0

        lax.fori_loop(0, n, all_here, 0)
        for q in range(per):
            s = p * per + q
            at, rank = place[sector[s]], rank_of(s)
            total = sums[0, at, rank].astype(jnp.float32) + sums[1, at, rank].astype(jnp.float32)
            live = live_rows & (column_index < right_sizes[sector[s]])
            out_ref[q] = jnp.where(live, total, 0.0).astype(jnp.bfloat16)
        lax.fori_loop(0, n, finish, 0)
        return

    def product(s):
        slot = 2 * place[sector[s]] + rank_of(s)
        total = jnp.dot(left[0], mixed[slot, 0], preferred_element_type=jnp.float32)
        for h in range(1, channels):
            total += jnp.dot(left[h], mixed[slot, h], preferred_element_type=jnp.float32)
        return total

    def owner_chip(i):
        return lax.rem(y + 1 + i // per, ny)

    def to_core(i):
        return pltpu.make_async_remote_copy(
            src_ref=out_core.at[i], dst_ref=in_core.at[i],
            send_sem=core_send.at[i], recv_sem=core_recv.at[i],
            device_id=(b, sibling), device_id_type=MESH,
        )

    def to_chip(i):
        return pltpu.make_async_remote_copy(
            src_ref=out_chip.at[i], dst_ref=in_chip.at[i],
            send_sem=chip_send.at[i], recv_sem=chip_recv.at[i],
            device_id=(b, owner_chip(i) * cores + c), device_id_type=MESH,
        )

    remote = (ny - 1) * per
    lag = min(3, count)

    def reduce_step(i, _):
        @pl.when(i < count)
        def _():
            s = (owner_chip(i) * cores + (1 - c)) * per + i % per
            out_core[i] = product(s).astype(jnp.bfloat16)
            to_core(i).start()

        @pl.when(i >= lag)
        def _():
            j = i - lag
            s = (owner_chip(j) * cores + c) * per + j % per
            total = product(s)
            to_core(j).wait_recv()
            total = total + in_core[j].astype(jnp.float32)

            @pl.when(j < remote)
            def _():
                out_chip[j] = total.astype(jnp.bfloat16)
                to_chip(j).start()

            @pl.when(j >= remote)
            def _():
                own[j - remote] = total

        return 0

    lax.fori_loop(0, count + lag, reduce_step, 0)

    for q in range(per):
        total = own[q]
        for dy in range(ny - 1):
            to_chip(dy * per + q).wait_recv()
            total = total + in_chip[dy * per + q].astype(jnp.float32)
        live = live_rows & (column_index < right_sizes[sector[p * per + q]])
        out_ref[q] = jnp.where(live, total, 0.0).astype(jnp.bfloat16)

    lax.fori_loop(0, n, finish, 0)

    def finish_core(i, _):
        to_core(i).wait_send()
        return 0

    lax.fori_loop(0, count, finish_core, 0)

    def finish_chip(i, _):
        to_chip(i).wait_send()
        return 0

    lax.fori_loop(0, remote, finish_chip, 0)


def sum_of(k, values):
    if isinstance(k, int):
        return values[k]
    total = 0
    for i, v in enumerate(values):
        if v:
            total = total + (k == i).astype(jnp.int32) * v
    return total


def halves_kernel(
    n, m,
    sector, place, left_sizes, right_sizes, ops_ref,
    wave_hbm, left_hbm, right_hbm,
    out_ref,
    right_all, away, wave, left, ops, coef, part, part_out, part_in, fin, arr, states_of, mine,
    local_sem, gather_send, gather_recv, early_send, left_recv, ops_send, ops_recv,
    part_send, part_recv, fin_send, fin_recv, pass_send, pass_recv,
):
    nz, nx = plane_of(n)
    states, rows, _ = wave.shape
    half = rows // 2
    channels = left_hbm.shape[0]
    per = out_ref.shape[0]
    units = 2 * channels
    b = lax.axis_index("bond")
    p = lax.axis_index("mpo")
    z, x = b // nx, b % nx
    y, c = p // 2, p % 2
    sibling = y * 2 + (1 - c)
    peer = (1 - y) * 2 + c
    end = (z == 0) | (z == nz - 1)
    way = 1 - 2 * (z >= nz // 2).astype(jnp.int32)
    bf16, f32 = jnp.bfloat16, jnp.float32
    L, S, X = 0, 1, 2
    targets = (b + way * nx, b - way * nx, z * nx + (1 - x))

    def own_half(h, of):
        return right_hbm.at[h, pl.ds(pl.multiple_of(of * half, half), half)]

    barrier = pltpu.get_barrier_semaphore()
    for target in (L, X):
        pl.semaphore_signal(barrier, inc=1, device_id=(targets[target], p), device_id_type=MESH)

    @pl.when(jnp.logical_not(end))
    def _():
        pl.semaphore_signal(barrier, inc=1, device_id=(targets[S], p), device_id_type=MESH)

    for other in (sibling, peer):
        pl.semaphore_signal(barrier, inc=1, device_id=(b, other), device_id_type=MESH)

    wave_copy = pltpu.make_async_copy(wave_hbm, wave, local_sem.at[0])
    left_copy = pltpu.make_async_copy(left_hbm, left.at[pl.ds(0, channels)], local_sem.at[1])
    own_copies = [
        pltpu.make_async_copy(own_half(h, 1 - y), away.at[h], local_sem.at[2])
        for h in range(channels)
    ] + [
        pltpu.make_async_copy(own_half(h, y), right_all.at[b, h], local_sem.at[2])
        for h in range(channels)
    ]
    for own in own_copies:
        own.start()
    left_copy.start()
    pl.semaphore_wait(barrier, 5 - end.astype(jnp.int32))

    def to_device(src, dst, send, recv, device):
        return pltpu.make_async_remote_copy(
            src_ref=src, dst_ref=dst, send_sem=send, recv_sem=recv,
            device_id=device, device_id_type=MESH,
        )

    def hop(pos, u, kind, src, batch=1):
        return to_device(
            src, right_all.at[pos, u], gather_send.at[batch], gather_recv.at[pos, u],
            (targets[kind], p),
        )

    def first(h):
        return to_device(
            away.at[h], right_all.at[b, channels + h], early_send,
            gather_recv.at[b, channels + h], (b, peer),
        )

    def left_to_peer(h):
        return to_device(
            left.at[h], left.at[channels + h], early_send, left_recv, (b, peer)
        )

    ops_to_peer = to_device(
        ops_ref, ops.at[pl.ds(channels, channels)], ops_send, ops_recv, (b, peer)
    )

    pltpu.make_async_copy(right_hbm, left.at[pl.ds(0, channels)], local_sem.at[2]).wait()
    for h in range(channels):
        first(h).start()
        for kind in (L, X):
            hop(b, h, kind, right_all.at[b, h], 0).start()

        @pl.when(jnp.logical_not(end))
        def _():
            hop(b, h, S, right_all.at[b, h], 0).start()

    left_copy.wait()
    ops_to_peer.start()
    for h in range(channels):
        left_to_peer(h).start()

    def place_of(off, other):
        return (z + way * off) * nx + ((1 - x) if other else x)

    def event(off, other, u, kinds):
        pos = place_of(off, other)
        hop(pos, u, X, right_all.at[pos, u]).wait_recv()
        for kind in kinds:
            hop(pos, u, kind, right_all.at[pos, u], 0 if (off, other) == (0, 0) else 1).start()

    def settled(view, sem):
        to_device(view, view, sem, sem, (b, sibling)).wait_send()

    lo, hi = range(channels), range(channels, units)
    end_order = [(0, 0), (0, 1), (1, 0), (1, 1), (2, 0), (2, 1), (3, 0), (3, 1)]
    mid_order = [(0, 0), (0, 1), (-1, 0), (1, 0), (-1, 1), (2, 0), (1, 1), (2, 1)]
    end_before = {
        "own": [(0, 0, 2, (L, X)), (1, 0, 0, (X,)), (0, 0, 3, (L, X)), (1, 0, 1, (X,))],
        "start": [(1, 0, u, (X,)) for u in hi]
        + [(0, 1, u, ()) for u in lo] + [(0, 1, u, (L,)) for u in hi] + [(2, 0, 0, (X,))],
        1: [(2, 0, 1, (X,))],
        2: [(2, 0, 2, (X,))],
        3: [(2, 0, 3, (X,))] + [(1, 1, u, ()) for u in range(units)],
        4: [(3, 0, 0, (X,))],
        5: [(3, 0, 1, (X,))],
        "5+": [(2, 1, u, ()) for u in range(units)],
        6: [(3, 0, u, ()) for u in hi],
        7: [(3, 1, u, ()) for u in range(units)],
    }
    mid_before = {
        "own": [
            (0, 0, 2, (L, S, X)), (0, 0, 3, (L, S, X)),
            (-1, 0, 0, (L, X)), (1, 0, 0, (S, X)), (-1, 0, 1, (L, X)), (1, 0, 1, (S, X)),
        ],
        "start": [
            (-1, 0, 2, (L,)), (1, 0, 2, (S, X)), (-1, 0, 3, (L,)), (1, 0, 3, (S, X)),
        ] + [(0, 1, u, ()) for u in range(units)] + [(2, 0, 0, (S, X))],
        1: [(2, 0, 1, (S, X)), (-1, 1, 2, (L,))],
        2: [(-1, 1, 3, (L,)), (2, 0, 2, (S,))],
        3: [(2, 0, 3, (S,))],
        4: [(2, 1, 2, (S,))] + [(-1, 1, u, ()) for u in lo],
        5: [(2, 1, 3, (S,))],
        6: [(1, 1, u, ()) for u in range(units)],
        7: [(2, 1, u, ()) for u in lo],
    }

    def run(stage):
        @pl.when(end)
        def _():
            for e in end_before.get(stage, ()):
                event(*e)

        @pl.when(jnp.logical_not(end))
        def _():
            for e in mid_before.get(stage, ()):
                event(*e)

    def pos_of(k):
        off = jnp.where(end, sum_of(k, [o for o, _ in end_order]), sum_of(k, [o for o, _ in mid_order]))
        other = jnp.where(end, sum_of(k, [o for _, o in end_order]), sum_of(k, [o for _, o in mid_order]))
        return (z + way * off) * nx + x + other * (1 - 2 * x)

    def list_states(k, _):
        pos = pos_of(k)

        def look(s, carry):
            s1, s2 = carry
            hit = place[sector[s]] == pos
            return jnp.where(hit & (s < s1), s, s1), jnp.where(hit, s, s2)

        s1, s2 = lax.fori_loop(0, states, look, (jnp.int32(states - 1), jnp.int32(0)), unroll=True)
        states_of[k, 0] = s1
        states_of[k, 1] = s2
        states_of[k, 2] = right_sizes[sector[s1]]
        return 0

    lax.fori_loop(0, n, list_states, 0)

    def list_mine(q, _):
        s = p * per + q

        def look(t, rank):
            return rank + ((t < s) & (sector[t] == sector[s])).astype(jnp.int32)

        mine[q, 0] = place[sector[s]]
        mine[q, 1] = jnp.minimum(lax.fori_loop(0, states, look, jnp.int32(0), unroll=True), 1)
        return 0

    lax.fori_loop(0, per, list_mine, 0)

    def pick_operators():
        ops_to_peer.wait_recv()
        square = (states, states)
        op_row = lax.broadcasted_iota(jnp.int32, square, 0)
        op_column = lax.broadcasted_iota(jnp.int32, square, 1)
        named = jnp.zeros(square, jnp.int32)
        for r in range(states):
            named = jnp.where(op_row == r, states_of[r // 2, r % 2], named)
        pick = jnp.where(named == op_column, 1.0, 0.0).astype(bf16)
        same = op_row == op_column
        twin = op_row + 1 - 2 * (op_row % 2) == op_column
        for u in range(units):
            picked = jnp.dot(pick, ops[u], preferred_element_type=f32).astype(bf16)
            table = lax.dot_general(
                picked, pick, (((1,), (1,)), ((), ())), preferred_element_type=f32
            )
            for i, chosen in enumerate((same, twin)):
                column = jnp.sum(jnp.where(chosen, table, 0.0), axis=1, keepdims=True)
                coef[u, i] = jnp.broadcast_to(column, (states, 128))

    ops[pl.ds(0, channels)] = ops_ref[...]
    wave_copy.start()
    run("own")
    pick_operators()
    run("start")

    wave_copy.wait()
    both_left = left.at[pl.ds(channels, channels)]
    to_device(both_left, both_left, early_send, left_recv, (b, peer)).wait_recv()

    row_index = lax.broadcasted_iota(jnp.int32, (rows, rows), 0)
    column_index = lax.broadcasted_iota(jnp.int32, (rows, rows), 1)
    half_row = lax.broadcasted_iota(jnp.int32, (rows, half), 0)
    half_column = lax.broadcasted_iota(jnp.int32, (rows, half), 1) + y * half

    def to_sibling(pos):
        return to_device(
            part_out.at[pos], part_in.at[pos], part_send, part_recv.at[pos], (b, sibling)
        )

    def to_peer(pos):
        return to_device(
            fin.at[pos, c], arr.at[pos, c], fin_send, fin_recv.at[pos], (b, peer)
        )

    def passing(pos, rank):
        return to_device(
            arr.at[pos, rank], arr.at[pos, rank], pass_send, pass_recv, (b, sibling)
        )

    def compute(k):
        pos = pos_of(k)
        s1, s2 = states_of[k, 0], states_of[k, 1]
        live = (row_index < left_sizes[b]) & (column_index < states_of[k, 2])

        def masked(s):
            return jnp.where(live, wave[s].astype(f32), 0.0).astype(bf16)

        both = jnp.concatenate([masked(s1), masked(s2)], axis=0)
        total = None
        for g in range(2):
            factor = right_all[pos, pl.ds(g * channels, channels)].reshape(channels * half, rows)
            parts = lax.dot_general(
                both, factor, (((1,), (1,)), ((), ())), preferred_element_type=f32
            ).astype(bf16).astype(f32)
            for h in range(channels):
                u = g * channels + h
                p1 = parts[:rows, h * half:(h + 1) * half]
                p2 = parts[rows:, h * half:(h + 1) * half]
                own1, own2 = coef[u, 0, pl.ds(2 * k, 1)], coef[u, 0, pl.ds(2 * k + 1, 1)]
                cross1, cross2 = coef[u, 1, pl.ds(2 * k, 1)], coef[u, 1, pl.ds(2 * k + 1, 1)]
                mixed = jnp.concatenate(
                    [(own1 * p1 + cross1 * p2).astype(bf16), (cross2 * p1 + own2 * p2).astype(bf16)],
                    axis=1,
                )
                product = jnp.dot(left[u], mixed, preferred_element_type=f32)
                total = product if total is None else total + product
        part_out[pos] = total.astype(bf16)
        to_sibling(pos).start()
        part[pos] = total

    def add_up(k):
        pos = pos_of(k)
        to_sibling(pos).wait_recv()
        live = (half_row < left_sizes[b]) & (half_column < states_of[k, 2])
        for r in range(2):
            cut = slice(r * half, (r + 1) * half)
            total = part[pos, :, cut] + part_in[pos, :, cut].astype(f32)
            fin[pos, r] = jnp.where(live, total, 0.0).astype(bf16)
        to_peer(pos).start()

    def pass_on(k):
        pos = pos_of(k)
        to_peer(pos).wait_recv()
        passing(pos, c).start()

    def free_sends():
        settled(left.at[pl.ds(0, channels + channels // 2)], early_send)
        ops_to_peer.wait_send()

        @pl.when(end)
        def _():
            settled(right_all.at[pl.ds(0, 2)], gather_send.at[0])
            settled(right_all.at[pl.ds(0, 3)], gather_send.at[1])

        @pl.when(jnp.logical_not(end))
        def _():
            settled(right_all.at[pl.ds(0, 3)], gather_send.at[0])

    def step(k, _):
        for stage in range(1, n):
            @pl.when(k == stage)
            def _():
                if stage == 7:
                    add_up(6)
                    pass_on(3)
                    pass_on(4)
                    free_sends()
                run(stage)
                if stage == 5:
                    add_up(4)
                    pass_on(1)
                    run("5+")

        compute(k)

        @pl.when((k >= 1) & (k != 5) & (k != 7))
        def _():
            add_up(k - 1)

        @pl.when((k == 4) | (k == 6))
        def _():
            pass_on(k - 4)

        return 0

    lax.fori_loop(0, n, step, 0)
    add_up(7)
    pass_on(5)
    pass_on(6)

    @pl.when(jnp.logical_not(end))
    def _():
        settled(right_all.at[pl.ds(0, 6)], gather_send.at[1])

    settled(part_out, part_send)
    settled(arr.at[pl.ds(0, n // 2)], fin_send)
    pass_on(7)
    passed = arr.at[pl.ds(0, n // 2)]
    to_device(passed, passed, pass_send, pass_recv, (b, sibling)).wait_recv()
    mine_at = pl.ds(pl.multiple_of(y * half, half), half)
    others_at = pl.ds(pl.multiple_of((1 - y) * half, half), half)
    for q in range(per):
        pos, rank = mine[q, 0], mine[q, 1]
        out_ref[q, :, mine_at] = fin[pos, rank]
        out_ref[q, :, others_at] = arr[pos, rank]

    settled(arr.at[pl.ds(0, n // 2)], pass_send)


def shards(n, m, wave_blocks, left_environment, right_environment, site_operators,
           right_sector, left_sizes, right_sizes, sector_place):
    states, rows = wave_blocks.shape[1:3]
    channels = left_environment.shape[0]
    per = states // m
    cores = 2 if m % 2 == 0 else 1
    ny = m // cores
    count = ny * per
    remote = max(1, (ny - 1) * per)
    block = (rows, rows)
    bf16, f32 = jnp.bfloat16, jnp.float32
    smem = pl.BlockSpec(memory_space=pltpu.SMEM)
    hbm = pl.BlockSpec(memory_space=pl.ANY)
    dma = pltpu.SemaphoreType.DMA
    nz, nx = plane_of(n)
    by_halves = (nz, nx, ny, cores, channels) == (4, 2, 2, 2, 2) and states == 2 * n
    if by_halves:
        half = (rows // 2, rows)
        tall = (rows, rows // 2)
        scratch = [
            pltpu.VMEM((n, 2 * channels) + half, bf16),
            pltpu.VMEM((channels,) + half, bf16),
            pltpu.VMEM((states,) + block, bf16),
            pltpu.VMEM((2 * channels,) + block, bf16),
            pltpu.VMEM((2 * channels, states, states), bf16),
            pltpu.VMEM((2 * channels, 2, states, 128), f32),
            pltpu.VMEM((n,) + block, f32),
            pltpu.VMEM((n,) + block, bf16),
            pltpu.VMEM((n,) + block, bf16),
            pltpu.VMEM((n, 2) + tall, bf16),
            pltpu.VMEM((n, 2) + tall, bf16),
            pltpu.SMEM((n, 3), jnp.int32),
            pltpu.SMEM((per, 2), jnp.int32),
            dma((3,)), dma((2,)), dma((n, 2 * channels)), dma, dma, dma, dma,
            dma, dma((n,)), dma, dma((n,)), dma, dma,
        ]
    elif ny == 2 and cores == 2:
        rest = [
            pltpu.VMEM((n,) + block, f32),
            pltpu.VMEM((n,) + block, bf16),
            pltpu.VMEM((n,) + block, bf16),
            pltpu.VMEM((2, n, 2) + block, bf16),
            dma((n,)), dma((n,)), dma((3, n)), dma((2, n, 2)),
        ]
    else:
        rest = [
            pltpu.VMEM((2 * n, channels) + block, bf16),
            pltpu.VMEM((count,) + block, bf16),
            pltpu.VMEM((count,) + block, bf16),
            pltpu.VMEM((remote,) + block, bf16),
            pltpu.VMEM((remote,) + block, bf16),
            pltpu.VMEM((per,) + block, f32),
            dma((count,)), dma((count,)), dma((remote,)), dma((remote,)),
        ]
    if not by_halves:
        scratch = [
            pltpu.VMEM((n, channels) + block, bf16),
            pltpu.VMEM((states,) + block, bf16),
            pltpu.VMEM((channels,) + block, bf16),
            dma((3,)), dma((n, channels, 4)), dma((n, channels)),
            *rest,
        ]
    out = pl.pallas_call(
        functools.partial(halves_kernel if by_halves else kernel, n, m),
        out_shape=pltpu.VMEM((per,) + block, bf16),
        in_specs=[smem] * 4 + [pl.BlockSpec(memory_space=pltpu.VMEM)] + [hbm] * 3,
        out_specs=pl.BlockSpec(memory_space=pltpu.VMEM),
        scratch_shapes=scratch,
        compiler_params=pltpu.CompilerParams(
            collective_id=0, has_side_effects=True, vmem_limit_bytes=60 * 1024 * 1024
        ),
    )(
        right_sector.reshape(states), sector_place, left_sizes, right_sizes,
        site_operators,
        wave_blocks.reshape((states,) + block),
        left_environment.reshape((channels,) + block),
        right_environment.reshape((channels,) + block),
    )
    return out.reshape((1, per) + block)


def solution(mesh):
    placed = (
        P("bond", None, None, None),
        P("mpo", "bond", None, None),
        P("mpo", "bond", None, None),
        P("mpo", None, None),
        P("bond", None, None),
        P(),
        P(),
        P(),
    )
    body = functools.partial(shards, mesh.shape["bond"], mesh.shape["mpo"])
    return jax.shard_map(
        body, mesh=mesh, in_specs=placed, out_specs=P("bond", "mpo", None, None), check_vma=False
    )
```

```python
import functools

import jax
import jax.numpy as jnp
from jax import lax
from jax.experimental import pallas as pl
from jax.experimental.pallas import tpu as pltpu
from jax.sharding import PartitionSpec as P

MESH = pl.DeviceIdType.MESH


def plane_of(count):
    nx = 1
    while (2 * nx) * (2 * nx) * 2 <= count and count % (2 * nx) == 0:
        nx *= 2
    return count // nx, nx


def kernel(
    n, m,
    sector, place, left_sizes, right_sizes, ops,
    wave_hbm, left_hbm, right_hbm,
    out_ref,
    right_all, wave, left, local_sem, gather_send, gather_recv, *rest,
):
    nz, nx = plane_of(n)
    cores = 2 if m % 2 == 0 else 1
    ny = m // cores
    states, rows, _ = wave.shape
    channels = left.shape[0]
    per = out_ref.shape[0]
    count = ny * per
    pair = ny == 2 and cores == 2
    if pair:
        (part, part_out, part_in, sums,
         part_send, part_recv, sum_send, sum_recv) = rest
    else:
        (mixed, out_core, in_core, out_chip, in_chip, own,
         core_send, core_recv, chip_send, chip_recv) = rest
    b = lax.axis_index("bond")
    p = lax.axis_index("mpo")
    z, x = b // nx, b % nx
    y, c = p // cores, p % cores
    sibling = y * cores + (1 - c)

    wave_copy = pltpu.make_async_copy(wave_hbm, wave, local_sem.at[0])
    left_copy = pltpu.make_async_copy(left_hbm, left, local_sem.at[1])
    own_copy = pltpu.make_async_copy(right_hbm, right_all.at[b], local_sem.at[2])
    wave_copy.start()
    left_copy.start()
    own_copy.start()

    steps = ((nx, z + 1 < nz), (-nx, z > 0), (1, x + 1 < nx), (-1, x > 0))
    barrier = pltpu.get_barrier_semaphore()
    greeted = ny
    for step, there in steps:
        greeted = greeted + there.astype(jnp.int32)

        @pl.when(there)
        def _():
            pl.semaphore_signal(barrier, inc=1, device_id=(b + step, p), device_id_type=MESH)

    pl.semaphore_signal(barrier, inc=1, device_id=(b, sibling), device_id_type=MESH)
    for dy in range(1, ny):
        other = lax.rem(y + dy, ny) * cores + c
        pl.semaphore_signal(barrier, inc=1, device_id=(b, other), device_id_type=MESH)
    pl.semaphore_wait(barrier, greeted)

    def hop(pos, h, k, src):
        return pltpu.make_async_remote_copy(
            src_ref=src,
            dst_ref=right_all.at[pos, h],
            send_sem=gather_send.at[pos, h, k],
            recv_sem=gather_recv.at[pos, h],
            device_id=(b + steps[k][0], p),
            device_id_type=MESH,
        )

    def sends(zs, xs, h):
        column = xs == x
        if nx == 2 and h == channels - 1 and channels > 1:
            detour = (zs == 0) | (zs == nz - 1)
            along, across = column | detour, ~detour | (zs == z)
        else:
            along, across = column, True
        return (
            along & (zs <= z) & (z + 1 < nz),
            along & (zs >= z) & (z > 0),
            across & (xs <= x) & (x + 1 < nx),
            across & (xs >= x) & (x > 0),
        )

    def forward(zs, xs, h):
        pos = zs * nx + xs
        for k, wanted in enumerate(sends(zs, xs, h)):
            @pl.when(wanted)
            def _():
                hop(pos, h, k, right_all.at[pos, h]).start()

    def arrived(pos, h):
        hop(pos, h, 0, right_all.at[pos, h]).wait_recv()

    for h in range(channels):
        for k in (0, 1, 2, 3):
            @pl.when(steps[k][1])
            def _():
                hop(b, h, k, right_hbm.at[h]).start()

    wave_copy.wait()
    left_copy.wait()
    own_copy.wait()

    row_index = lax.broadcasted_iota(jnp.int32, (rows, rows), 0)
    column_index = lax.broadcasted_iota(jnp.int32, (rows, rows), 1)
    live_rows = row_index < left_sizes[b]
    op_row = lax.broadcasted_iota(jnp.int32, (states, states), 0)
    op_column = lax.broadcasted_iota(jnp.int32, (states, states), 1)

    def to_sibling(pos):
        return pltpu.make_async_remote_copy(
            src_ref=part_out.at[pos], dst_ref=part_in.at[pos],
            send_sem=part_send.at[pos], recv_sem=part_recv.at[pos],
            device_id=(b, sibling), device_id_type=MESH,
        )

    def share(kind, pos):
        source, target = (0, 0, 1)[kind], (0, 1, 1)[kind]
        device = (1 - y) * cores + c if kind == 1 else sibling
        return pltpu.make_async_remote_copy(
            src_ref=sums.at[source, pos, c], dst_ref=sums.at[target, pos, c],
            send_sem=sum_send.at[kind, pos], recv_sem=sum_recv.at[target, pos, c],
            device_id=(b, device), device_id_type=MESH,
        )

    def sum_arrived(target, pos, rank):
        pltpu.make_async_remote_copy(
            src_ref=sums.at[target, pos, rank], dst_ref=sums.at[target, pos, rank],
            send_sem=sum_send.at[0, pos], recv_sem=sum_recv.at[target, pos, rank],
            device_id=(b, sibling), device_id_type=MESH,
        ).wait_recv()

    def add_up(pos):
        to_sibling(pos).wait_recv()
        sums[0, pos, c] = (part[pos] + part_in[pos].astype(jnp.float32)).astype(jnp.bfloat16)
        share(1, pos).start()
        share(0, pos).start()

    def pass_on(pos):
        sum_arrived(1, pos, c)
        share(2, pos).start()

    def work(pos):
        def look(s, carry):
            first, last, hits = carry
            hit = place[sector[s]] == pos
            first = jnp.where(hit & (hits == 0), s, first)
            last = jnp.where(hit, s, last)
            return first, last, hits + hit.astype(jnp.int32)

        zero = jnp.int32(0)
        s1, s2, hits = lax.fori_loop(0, states, look, (zero, zero, zero), unroll=True)
        if pair:
            s1, s2 = jnp.where(c == 0, s1, s2), jnp.where(c == 0, s2, s1)
        live = live_rows & (column_index < right_sizes[sector[s1]])

        def masked(s):
            return jnp.where(live, wave[s].astype(jnp.float32), 0.0).astype(jnp.bfloat16)

        both = jnp.concatenate([masked(s1), masked(s2)], axis=0)
        two = hits == 2
        for h in range(channels):
            factor = right_all[pos, h]

            parts = lax.dot_general(
                both, factor, (((1,), (1,)), ((), ())), preferred_element_type=jnp.float32
            ).astype(jnp.bfloat16).astype(jnp.float32)
            p1, p2 = parts[:rows], parts[rows:]
            table = ops[h].astype(jnp.float32)

            def op(s, t, keep=True):
                picked = (op_row == s) & (op_column == t) & keep
                return jnp.sum(jnp.where(picked, table, 0.0), keepdims=True)

            m1 = (op(s1, s1) * p1 + op(s1, s2, two) * p2).astype(jnp.bfloat16)
            m2 = (op(s2, s1, two) * p1 + op(s2, s2) * p2).astype(jnp.bfloat16)
            if pair:
                left_m = left[h]
                q1 = jnp.dot(left_m, m1, preferred_element_type=jnp.float32)
                q2 = jnp.dot(left_m, m2, preferred_element_type=jnp.float32)
                total1, total2 = (q1, q2) if h == 0 else (total1 + q1, total2 + q2)
            else:
                mixed[2 * pos, h] = m1
                mixed[2 * pos + 1, h] = m2
        if pair:
            part_out[pos] = total2.astype(jnp.bfloat16)
            to_sibling(pos).start()
            part[pos] = total1

    def at(g, i, body):
        sign = 1 - 2 * (i % 2)
        e = i // 2
        d = g - (e > 0).astype(jnp.int32)
        zs = z + sign * d
        xs = x + (e + 1) // 2 * (1 - 2 * (e % 2))

        @pl.when((zs >= 0) & (zs < nz) & (xs >= 0) & (xs < nx) & (d >= 0) & ((d > 0) | (sign > 0)))
        def _():
            body(zs, xs)

    items = 2 * (2 * nx - 1)

    def each(g, body):
        def one(i, _):
            at(g, i, body)
            return 0

        lax.fori_loop(0, items, one, 0)

    def multiply(g):
        def one(i, _):
            @pl.when(i < items)
            def _():
                at(g, i, use)

            @pl.when(i >= 2)
            def _():
                at(g, i - 2, lambda zs, xs: add_up(zs * nx + xs))

            return 0

        lax.fori_loop(0, items + 2, one, 0)

    def use(zs, xs):
        pos = zs * nx + xs

        @pl.when(xs != x)
        def _():
            for h in range(channels):
                arrived(pos, h)
                forward(zs, xs, h)

        work(pos)

    def gather_round(g, _):
        @pl.when((g > 0) & (g < nz))
        def _():
            for h in range(channels):
                for sign in (1, -1):
                    zs = z + sign * g

                    @pl.when((zs >= 0) & (zs < nz))
                    def _():
                        arrived(zs * nx + x, h)
                        forward(zs, x, h)

        @pl.when(g <= nz)
        def _():
            if pair:
                multiply(g)
            else:
                each(g, use)

        if pair:
            @pl.when(g > 1)
            def _():
                each(g - 2, lambda zs, xs: pass_on(zs * nx + xs))

        return 0

    lax.fori_loop(0, nz + (3 if pair else 1), gather_round, 0)

    def rank_of(s):
        def look(t, rank):
            return rank + ((t < s) & (sector[t] == sector[s])).astype(jnp.int32)

        return jnp.minimum(lax.fori_loop(0, states, look, jnp.int32(0), unroll=True), 1)

    def finish(pos, _):
        for h in range(channels):
            for k, wanted in enumerate(sends(pos // nx, pos % nx, h)):
                @pl.when(wanted)
                def _():
                    hop(pos, h, k, right_all.at[pos, h]).wait_send()
        if pair:
            to_sibling(pos).wait_send()
            for kind in range(3):
                share(kind, pos).wait_send()
        return 0

    if pair:
        def all_here(pos, _):
            sum_arrived(0, pos, 1 - c)
            sum_arrived(1, pos, 1 - c)
            return 0

        lax.fori_loop(0, n, all_here, 0)
        for q in range(per):
            s = p * per + q
            at, rank = place[sector[s]], rank_of(s)
            total = sums[0, at, rank].astype(jnp.float32) + sums[1, at, rank].astype(jnp.float32)
            live = live_rows & (column_index < right_sizes[sector[s]])
            out_ref[q] = jnp.where(live, total, 0.0).astype(jnp.bfloat16)
        lax.fori_loop(0, n, finish, 0)
        return

    def product(s):
        slot = 2 * place[sector[s]] + rank_of(s)
        total = jnp.dot(left[0], mixed[slot, 0], preferred_element_type=jnp.float32)
        for h in range(1, channels):
            total += jnp.dot(left[h], mixed[slot, h], preferred_element_type=jnp.float32)
        return total

    def owner_chip(i):
        return lax.rem(y + 1 + i // per, ny)

    def to_core(i):
        return pltpu.make_async_remote_copy(
            src_ref=out_core.at[i], dst_ref=in_core.at[i],
            send_sem=core_send.at[i], recv_sem=core_recv.at[i],
            device_id=(b, sibling), device_id_type=MESH,
        )

    def to_chip(i):
        return pltpu.make_async_remote_copy(
            src_ref=out_chip.at[i], dst_ref=in_chip.at[i],
            send_sem=chip_send.at[i], recv_sem=chip_recv.at[i],
            device_id=(b, owner_chip(i) * cores + c), device_id_type=MESH,
        )

    remote = (ny - 1) * per
    lag = min(3, count)

    def reduce_step(i, _):
        @pl.when(i < count)
        def _():
            s = (owner_chip(i) * cores + (1 - c)) * per + i % per
            out_core[i] = product(s).astype(jnp.bfloat16)
            to_core(i).start()

        @pl.when(i >= lag)
        def _():
            j = i - lag
            s = (owner_chip(j) * cores + c) * per + j % per
            total = product(s)
            to_core(j).wait_recv()
            total = total + in_core[j].astype(jnp.float32)

            @pl.when(j < remote)
            def _():
                out_chip[j] = total.astype(jnp.bfloat16)
                to_chip(j).start()

            @pl.when(j >= remote)
            def _():
                own[j - remote] = total

        return 0

    lax.fori_loop(0, count + lag, reduce_step, 0)

    for q in range(per):
        total = own[q]
        for dy in range(ny - 1):
            to_chip(dy * per + q).wait_recv()
            total = total + in_chip[dy * per + q].astype(jnp.float32)
        live = live_rows & (column_index < right_sizes[sector[p * per + q]])
        out_ref[q] = jnp.where(live, total, 0.0).astype(jnp.bfloat16)

    lax.fori_loop(0, n, finish, 0)

    def finish_core(i, _):
        to_core(i).wait_send()
        return 0

    lax.fori_loop(0, count, finish_core, 0)

    def finish_chip(i, _):
        to_chip(i).wait_send()
        return 0

    lax.fori_loop(0, remote, finish_chip, 0)


def sum_of(k, values):
    if isinstance(k, int):
        return values[k]
    total = 0
    for i, v in enumerate(values):
        if v:
            total = total + (k == i).astype(jnp.int32) * v
    return total


def halves_kernel(
    n, m,
    sector, place, left_sizes, right_sizes, ops_ref,
    wave_hbm, left_hbm, right_hbm,
    out_ref,
    right_all, away, wave, left, ops, coef, part, part_out, part_in, fin, arr, states_of, mine,
    local_sem, gather_send, gather_recv, early_send, left_recv, ops_send, ops_recv,
    part_send, part_recv, fin_send, fin_recv, pass_send, pass_recv,
):
    nz, nx = plane_of(n)
    states, rows, _ = wave.shape
    half = rows // 2
    channels = left_hbm.shape[0]
    per = out_ref.shape[0]
    units = 2 * channels
    b = lax.axis_index("bond")
    p = lax.axis_index("mpo")
    z, x = b // nx, b % nx
    y, c = p // 2, p % 2
    sibling = y * 2 + (1 - c)
    peer = (1 - y) * 2 + c
    end = (z == 0) | (z == nz - 1)
    way = 1 - 2 * (z >= nz // 2).astype(jnp.int32)
    bf16, f32 = jnp.bfloat16, jnp.float32
    L, S, X = 0, 1, 2
    targets = (b + way * nx, b - way * nx, z * nx + (1 - x))

    def own_half(h, of):
        return right_hbm.at[h, pl.ds(pl.multiple_of(of * half, half), half)]

    barrier = pltpu.get_barrier_semaphore()
    for target in (L, X):
        pl.semaphore_signal(barrier, inc=1, device_id=(targets[target], p), device_id_type=MESH)

    @pl.when(jnp.logical_not(end))
    def _():
        pl.semaphore_signal(barrier, inc=1, device_id=(targets[S], p), device_id_type=MESH)

    for other in (sibling, peer):
        pl.semaphore_signal(barrier, inc=1, device_id=(b, other), device_id_type=MESH)

    wave_copy = pltpu.make_async_copy(wave_hbm, wave, local_sem.at[0])
    left_copy = pltpu.make_async_copy(left_hbm, left.at[pl.ds(0, channels)], local_sem.at[1])
    own_copies = [
        pltpu.make_async_copy(own_half(h, 1 - y), away.at[h], local_sem.at[2])
        for h in range(channels)
    ] + [
        pltpu.make_async_copy(own_half(h, y), right_all.at[b, h], local_sem.at[2])
        for h in range(channels)
    ]
    for own in own_copies:
        own.start()
    left_copy.start()
    pl.semaphore_wait(barrier, 5 - end.astype(jnp.int32))

    def to_device(src, dst, send, recv, device):
        return pltpu.make_async_remote_copy(
            src_ref=src, dst_ref=dst, send_sem=send, recv_sem=recv,
            device_id=device, device_id_type=MESH,
        )

    def hop(pos, u, kind, src, batch=1):
        return to_device(
            src, right_all.at[pos, u], gather_send.at[batch], gather_recv.at[pos, u],
            (targets[kind], p),
        )

    def first(h):
        return to_device(
            away.at[h], right_all.at[b, channels + h], early_send,
            gather_recv.at[b, channels + h], (b, peer),
        )

    def left_to_peer(h):
        return to_device(
            left.at[h], left.at[channels + h], early_send, left_recv, (b, peer)
        )

    ops_to_peer = to_device(
        ops_ref, ops.at[pl.ds(channels, channels)], ops_send, ops_recv, (b, peer)
    )

    pltpu.make_async_copy(right_hbm, left.at[pl.ds(0, channels)], local_sem.at[2]).wait()
    for h in range(channels):
        first(h).start()
        for kind in (L, X):
            hop(b, h, kind, right_all.at[b, h], 0).start()

        @pl.when(jnp.logical_not(end))
        def _():
            hop(b, h, S, right_all.at[b, h], 0).start()

    left_copy.wait()
    ops_to_peer.start()
    for h in range(channels):
        left_to_peer(h).start()

    def place_of(off, other):
        return (z + way * off) * nx + ((1 - x) if other else x)

    def event(off, other, u, kinds):
        pos = place_of(off, other)
        hop(pos, u, X, right_all.at[pos, u]).wait_recv()
        for kind in kinds:
            hop(pos, u, kind, right_all.at[pos, u], 0 if (off, other) == (0, 0) else 1).start()

    def settled(view, sem):
        to_device(view, view, sem, sem, (b, sibling)).wait_send()

    lo, hi = range(channels), range(channels, units)
    end_order = [(0, 0), (0, 1), (1, 0), (1, 1), (2, 0), (2, 1), (3, 0), (3, 1)]
    mid_order = [(0, 0), (0, 1), (-1, 0), (1, 0), (-1, 1), (2, 0), (1, 1), (2, 1)]
    end_before = {
        "own": [(0, 0, 2, (L, X)), (1, 0, 0, (X,)), (0, 0, 3, (L, X)), (1, 0, 1, (X,))],
        "start": [(1, 0, u, (X,)) for u in hi]
        + [(0, 1, u, ()) for u in lo] + [(0, 1, u, (L,)) for u in hi] + [(2, 0, 0, (X,))],
        1: [(2, 0, 1, (X,))],
        2: [(2, 0, 2, (X,))],
        3: [(2, 0, 3, (X,))] + [(1, 1, u, ()) for u in range(units)],
        4: [(3, 0, 0, (X,))],
        5: [(3, 0, 1, (X,))],
        "5+": [(2, 1, u, ()) for u in range(units)],
        6: [(3, 0, u, ()) for u in hi],
        7: [(3, 1, u, ()) for u in range(units)],
    }
    mid_before = {
        "own": [
            (0, 0, 2, (L, S, X)), (0, 0, 3, (L, S, X)),
            (-1, 0, 0, (L, X)), (1, 0, 0, (S, X)), (-1, 0, 1, (L, X)), (1, 0, 1, (S, X)),
        ],
        "start": [
            (-1, 0, 2, (L,)), (1, 0, 2, (S, X)), (-1, 0, 3, (L,)), (1, 0, 3, (S, X)),
        ] + [(0, 1, u, ()) for u in range(units)] + [(2, 0, 0, (S, X))],
        1: [(2, 0, 1, (S, X)), (-1, 1, 2, (L,))],
        2: [(-1, 1, 3, (L,)), (2, 0, 2, (S,))],
        3: [(2, 0, 3, (S,))],
        4: [(2, 1, 2, (S,))] + [(-1, 1, u, ()) for u in lo],
        5: [(2, 1, 3, (S,))],
        6: [(1, 1, u, ()) for u in range(units)],
        7: [(2, 1, u, ()) for u in lo],
    }

    def run(stage):
        @pl.when(end)
        def _():
            for e in end_before.get(stage, ()):
                event(*e)

        @pl.when(jnp.logical_not(end))
        def _():
            for e in mid_before.get(stage, ()):
                event(*e)

    def pos_of(k):
        off = jnp.where(end, sum_of(k, [o for o, _ in end_order]), sum_of(k, [o for o, _ in mid_order]))
        other = jnp.where(end, sum_of(k, [o for _, o in end_order]), sum_of(k, [o for _, o in mid_order]))
        return (z + way * off) * nx + x + other * (1 - 2 * x)

    def list_states(k, _):
        pos = pos_of(k)

        def look(s, carry):
            s1, s2 = carry
            hit = place[sector[s]] == pos
            return jnp.where(hit & (s < s1), s, s1), jnp.where(hit, s, s2)

        s1, s2 = lax.fori_loop(0, states, look, (jnp.int32(states - 1), jnp.int32(0)), unroll=True)
        states_of[k, 0] = s1
        states_of[k, 1] = s2
        states_of[k, 2] = right_sizes[sector[s1]]
        return 0

    lax.fori_loop(0, n, list_states, 0)

    def list_mine(q, _):
        s = p * per + q

        def look(t, rank):
            return rank + ((t < s) & (sector[t] == sector[s])).astype(jnp.int32)

        mine[q, 0] = place[sector[s]]
        mine[q, 1] = jnp.minimum(lax.fori_loop(0, states, look, jnp.int32(0), unroll=True), 1)
        return 0

    lax.fori_loop(0, per, list_mine, 0)

    def pick_operators():
        ops_to_peer.wait_recv()
        square = (states, states)
        op_row = lax.broadcasted_iota(jnp.int32, square, 0)
        op_column = lax.broadcasted_iota(jnp.int32, square, 1)
        named = jnp.zeros(square, jnp.int32)
        for r in range(states):
            named = jnp.where(op_row == r, states_of[r // 2, r % 2], named)
        pick = jnp.where(named == op_column, 1.0, 0.0).astype(bf16)
        same = op_row == op_column
        twin = op_row + 1 - 2 * (op_row % 2) == op_column
        for u in range(units):
            picked = jnp.dot(pick, ops[u], preferred_element_type=f32).astype(bf16)
            table = lax.dot_general(
                picked, pick, (((1,), (1,)), ((), ())), preferred_element_type=f32
            )
            for i, chosen in enumerate((same, twin)):
                column = jnp.sum(jnp.where(chosen, table, 0.0), axis=1, keepdims=True)
                coef[u, i] = jnp.broadcast_to(column, (states, 128))

    ops[pl.ds(0, channels)] = ops_ref[...]
    wave_copy.start()
    run("own")
    pick_operators()
    run("start")

    wave_copy.wait()
    both_left = left.at[pl.ds(channels, channels)]
    to_device(both_left, both_left, early_send, left_recv, (b, peer)).wait_recv()

    row_index = lax.broadcasted_iota(jnp.int32, (rows, rows), 0)
    column_index = lax.broadcasted_iota(jnp.int32, (rows, rows), 1)
    half_row = lax.broadcasted_iota(jnp.int32, (rows, half), 0)
    half_column = lax.broadcasted_iota(jnp.int32, (rows, half), 1) + y * half

    def to_sibling(pos):
        return to_device(
            part_out.at[pos], part_in.at[pos], part_send, part_recv.at[pos], (b, sibling)
        )

    def to_peer(pos):
        return to_device(
            fin.at[pos, c], arr.at[pos, c], fin_send, fin_recv.at[pos], (b, peer)
        )

    def passing(pos, rank):
        return to_device(
            arr.at[pos, rank], arr.at[pos, rank], pass_send, pass_recv, (b, sibling)
        )

    def compute(k):
        pos = pos_of(k)
        s1, s2 = states_of[k, 0], states_of[k, 1]
        live = (row_index < left_sizes[b]) & (column_index < states_of[k, 2])

        def masked(s):
            return jnp.where(live, wave[s].astype(f32), 0.0).astype(bf16)

        both = jnp.concatenate([masked(s1), masked(s2)], axis=0)
        total = None
        for g in range(2):
            factor = right_all[pos, pl.ds(g * channels, channels)].reshape(channels * half, rows)
            parts = lax.dot_general(
                both, factor, (((1,), (1,)), ((), ())), preferred_element_type=f32
            ).astype(bf16).astype(f32)
            for h in range(channels):
                u = g * channels + h
                p1 = parts[:rows, h * half:(h + 1) * half]
                p2 = parts[rows:, h * half:(h + 1) * half]
                own1, own2 = coef[u, 0, pl.ds(2 * k, 1)], coef[u, 0, pl.ds(2 * k + 1, 1)]
                cross1, cross2 = coef[u, 1, pl.ds(2 * k, 1)], coef[u, 1, pl.ds(2 * k + 1, 1)]
                mixed = jnp.concatenate(
                    [(own1 * p1 + cross1 * p2).astype(bf16), (cross2 * p1 + own2 * p2).astype(bf16)],
                    axis=1,
                )
                product = jnp.dot(left[u], mixed, preferred_element_type=f32)
                total = product if total is None else total + product
        part_out[pos] = total.astype(bf16)
        to_sibling(pos).start()
        part[pos] = total

    def add_up(k):
        pos = pos_of(k)
        to_sibling(pos).wait_recv()
        live = (half_row < left_sizes[b]) & (half_column < states_of[k, 2])
        for r in range(2):
            cut = slice(r * half, (r + 1) * half)
            total = part[pos, :, cut] + part_in[pos, :, cut].astype(f32)
            fin[pos, r] = jnp.where(live, total, 0.0).astype(bf16)
        to_peer(pos).start()

    def pass_on(k):
        pos = pos_of(k)
        to_peer(pos).wait_recv()
        passing(pos, c).start()

    def free_sends():
        settled(left.at[pl.ds(0, channels + channels // 2)], early_send)
        ops_to_peer.wait_send()

        @pl.when(end)
        def _():
            settled(right_all.at[pl.ds(0, 2)], gather_send.at[0])
            settled(right_all.at[pl.ds(0, 3)], gather_send.at[1])

        @pl.when(jnp.logical_not(end))
        def _():
            settled(right_all.at[pl.ds(0, 3)], gather_send.at[0])

    def on_core(core, *jobs):
        @pl.when(c == core)
        def _():
            for job, k in jobs:
                job(k)

    def step(k, _):
        @pl.when(k == 7)
        def _():
            on_core(0, (add_up, 6), (pass_on, 2), (pass_on, 3))
            on_core(1, (pass_on, 0), (pass_on, 1))
            free_sends()

        for stage in range(1, n):
            @pl.when(k == stage)
            def _():
                run(stage)
                if stage == 5:
                    on_core(0, (add_up, 4), (pass_on, 1))
                    on_core(1, (add_up, 2), (add_up, 3))
                    run("5+")

        compute(k)

        @pl.when((c == 0) & (k >= 1) & (k != 5) & (k != 7))
        def _():
            add_up(k - 1)

        @pl.when((c == 1) & ((k == 3) | (k == 4)))
        def _():
            add_up(k - 3)

        @pl.when(k == 4)
        def _():
            on_core(0, (pass_on, 0))

        @pl.when(k == 6)
        def _():
            on_core(1, (add_up, 4))

        return 0

    lax.fori_loop(0, n, step, 0)
    on_core(1, (add_up, 5), (add_up, 6))
    add_up(7)
    on_core(1, (pass_on, 2), (pass_on, 3))
    pass_on(4)
    pass_on(5)
    pass_on(6)

    @pl.when(jnp.logical_not(end))
    def _():
        settled(right_all.at[pl.ds(0, 6)], gather_send.at[1])

    settled(part_out, part_send)
    settled(arr.at[pl.ds(0, n // 2)], fin_send)
    pass_on(7)
    passed = arr.at[pl.ds(0, n // 2)]
    to_device(passed, passed, pass_send, pass_recv, (b, sibling)).wait_recv()
    mine_at = pl.ds(pl.multiple_of(y * half, half), half)
    others_at = pl.ds(pl.multiple_of((1 - y) * half, half), half)
    for q in range(per):
        pos, rank = mine[q, 0], mine[q, 1]
        out_ref[q, :, mine_at] = fin[pos, rank]
        out_ref[q, :, others_at] = arr[pos, rank]

    settled(arr.at[pl.ds(0, n // 2)], pass_send)


def shards(n, m, wave_blocks, left_environment, right_environment, site_operators,
           right_sector, left_sizes, right_sizes, sector_place):
    states, rows = wave_blocks.shape[1:3]
    channels = left_environment.shape[0]
    per = states // m
    cores = 2 if m % 2 == 0 else 1
    ny = m // cores
    count = ny * per
    remote = max(1, (ny - 1) * per)
    block = (rows, rows)
    bf16, f32 = jnp.bfloat16, jnp.float32
    smem = pl.BlockSpec(memory_space=pltpu.SMEM)
    hbm = pl.BlockSpec(memory_space=pl.ANY)
    dma = pltpu.SemaphoreType.DMA
    nz, nx = plane_of(n)
    by_halves = (nz, nx, ny, cores, channels) == (4, 2, 2, 2, 2) and states == 2 * n
    if by_halves:
        half = (rows // 2, rows)
        tall = (rows, rows // 2)
        scratch = [
            pltpu.VMEM((n, 2 * channels) + half, bf16),
            pltpu.VMEM((channels,) + half, bf16),
            pltpu.VMEM((states,) + block, bf16),
            pltpu.VMEM((2 * channels,) + block, bf16),
            pltpu.VMEM((2 * channels, states, states), bf16),
            pltpu.VMEM((2 * channels, 2, states, 128), f32),
            pltpu.VMEM((n,) + block, f32),
            pltpu.VMEM((n,) + block, bf16),
            pltpu.VMEM((n,) + block, bf16),
            pltpu.VMEM((n, 2) + tall, bf16),
            pltpu.VMEM((n, 2) + tall, bf16),
            pltpu.SMEM((n, 3), jnp.int32),
            pltpu.SMEM((per, 2), jnp.int32),
            dma((3,)), dma((2,)), dma((n, 2 * channels)), dma, dma, dma, dma,
            dma, dma((n,)), dma, dma((n,)), dma, dma,
        ]
    elif ny == 2 and cores == 2:
        rest = [
            pltpu.VMEM((n,) + block, f32),
            pltpu.VMEM((n,) + block, bf16),
            pltpu.VMEM((n,) + block, bf16),
            pltpu.VMEM((2, n, 2) + block, bf16),
            dma((n,)), dma((n,)), dma((3, n)), dma((2, n, 2)),
        ]
    else:
        rest = [
            pltpu.VMEM((2 * n, channels) + block, bf16),
            pltpu.VMEM((count,) + block, bf16),
            pltpu.VMEM((count,) + block, bf16),
            pltpu.VMEM((remote,) + block, bf16),
            pltpu.VMEM((remote,) + block, bf16),
            pltpu.VMEM((per,) + block, f32),
            dma((count,)), dma((count,)), dma((remote,)), dma((remote,)),
        ]
    if not by_halves:
        scratch = [
            pltpu.VMEM((n, channels) + block, bf16),
            pltpu.VMEM((states,) + block, bf16),
            pltpu.VMEM((channels,) + block, bf16),
            dma((3,)), dma((n, channels, 4)), dma((n, channels)),
            *rest,
        ]
    out = pl.pallas_call(
        functools.partial(halves_kernel if by_halves else kernel, n, m),
        out_shape=pltpu.VMEM((per,) + block, bf16),
        in_specs=[smem] * 4 + [pl.BlockSpec(memory_space=pltpu.VMEM)] + [hbm] * 3,
        out_specs=pl.BlockSpec(memory_space=pltpu.VMEM),
        scratch_shapes=scratch,
        compiler_params=pltpu.CompilerParams(
            collective_id=0, has_side_effects=True, vmem_limit_bytes=60 * 1024 * 1024
        ),
    )(
        right_sector.reshape(states), sector_place, left_sizes, right_sizes,
        site_operators,
        wave_blocks.reshape((states,) + block),
        left_environment.reshape((channels,) + block),
        right_environment.reshape((channels,) + block),
    )
    return out.reshape((1, per) + block)


def solution(mesh):
    placed = (
        P("bond", None, None, None),
        P("mpo", "bond", None, None),
        P("mpo", "bond", None, None),
        P("mpo", None, None),
        P("bond", None, None),
        P(),
        P(),
        P(),
    )
    body = functools.partial(shards, mesh.shape["bond"], mesh.shape["mpo"])
    return jax.shard_map(
        body, mesh=mesh, in_specs=placed, out_specs=P("bond", "mpo", None, None), check_vma=False
    )
```

```python
import functools

import jax
import jax.numpy as jnp
from jax import lax
from jax.experimental import pallas as pl
from jax.experimental.pallas import tpu as pltpu
from jax.sharding import PartitionSpec as P

MESH = pl.DeviceIdType.MESH


def plane_of(count):
    nx = 1
    while (2 * nx) * (2 * nx) * 2 <= count and count % (2 * nx) == 0:
        nx *= 2
    return count // nx, nx


def kernel(
    n, m,
    sector, place, left_sizes, right_sizes, ops,
    wave_hbm, left_hbm, right_hbm,
    out_ref,
    right_all, wave, left, local_sem, gather_send, gather_recv, *rest,
):
    nz, nx = plane_of(n)
    cores = 2 if m % 2 == 0 else 1
    ny = m // cores
    states, rows, _ = wave.shape
    channels = left.shape[0]
    per = out_ref.shape[0]
    count = ny * per
    pair = ny == 2 and cores == 2
    if pair:
        (part, part_out, part_in, sums,
         part_send, part_recv, sum_send, sum_recv) = rest
    else:
        (mixed, out_core, in_core, out_chip, in_chip, own,
         core_send, core_recv, chip_send, chip_recv) = rest
    b = lax.axis_index("bond")
    p = lax.axis_index("mpo")
    z, x = b // nx, b % nx
    y, c = p // cores, p % cores
    sibling = y * cores + (1 - c)

    wave_copy = pltpu.make_async_copy(wave_hbm, wave, local_sem.at[0])
    left_copy = pltpu.make_async_copy(left_hbm, left, local_sem.at[1])
    own_copy = pltpu.make_async_copy(right_hbm, right_all.at[b], local_sem.at[2])
    wave_copy.start()
    left_copy.start()
    own_copy.start()

    steps = ((nx, z + 1 < nz), (-nx, z > 0), (1, x + 1 < nx), (-1, x > 0))
    barrier = pltpu.get_barrier_semaphore()
    greeted = ny
    for step, there in steps:
        greeted = greeted + there.astype(jnp.int32)

        @pl.when(there)
        def _():
            pl.semaphore_signal(barrier, inc=1, device_id=(b + step, p), device_id_type=MESH)

    pl.semaphore_signal(barrier, inc=1, device_id=(b, sibling), device_id_type=MESH)
    for dy in range(1, ny):
        other = lax.rem(y + dy, ny) * cores + c
        pl.semaphore_signal(barrier, inc=1, device_id=(b, other), device_id_type=MESH)
    pl.semaphore_wait(barrier, greeted)

    def hop(pos, h, k, src):
        return pltpu.make_async_remote_copy(
            src_ref=src,
            dst_ref=right_all.at[pos, h],
            send_sem=gather_send.at[pos, h, k],
            recv_sem=gather_recv.at[pos, h],
            device_id=(b + steps[k][0], p),
            device_id_type=MESH,
        )

    def sends(zs, xs, h):
        column = xs == x
        if nx == 2 and h == channels - 1 and channels > 1:
            detour = (zs == 0) | (zs == nz - 1)
            along, across = column | detour, ~detour | (zs == z)
        else:
            along, across = column, True
        return (
            along & (zs <= z) & (z + 1 < nz),
            along & (zs >= z) & (z > 0),
            across & (xs <= x) & (x + 1 < nx),
            across & (xs >= x) & (x > 0),
        )

    def forward(zs, xs, h):
        pos = zs * nx + xs
        for k, wanted in enumerate(sends(zs, xs, h)):
            @pl.when(wanted)
            def _():
                hop(pos, h, k, right_all.at[pos, h]).start()

    def arrived(pos, h):
        hop(pos, h, 0, right_all.at[pos, h]).wait_recv()

    for h in range(channels):
        for k in (0, 1, 2, 3):
            @pl.when(steps[k][1])
            def _():
                hop(b, h, k, right_hbm.at[h]).start()

    wave_copy.wait()
    left_copy.wait()
    own_copy.wait()

    row_index = lax.broadcasted_iota(jnp.int32, (rows, rows), 0)
    column_index = lax.broadcasted_iota(jnp.int32, (rows, rows), 1)
    live_rows = row_index < left_sizes[b]
    op_row = lax.broadcasted_iota(jnp.int32, (states, states), 0)
    op_column = lax.broadcasted_iota(jnp.int32, (states, states), 1)

    def to_sibling(pos):
        return pltpu.make_async_remote_copy(
            src_ref=part_out.at[pos], dst_ref=part_in.at[pos],
            send_sem=part_send.at[pos], recv_sem=part_recv.at[pos],
            device_id=(b, sibling), device_id_type=MESH,
        )

    def share(kind, pos):
        source, target = (0, 0, 1)[kind], (0, 1, 1)[kind]
        device = (1 - y) * cores + c if kind == 1 else sibling
        return pltpu.make_async_remote_copy(
            src_ref=sums.at[source, pos, c], dst_ref=sums.at[target, pos, c],
            send_sem=sum_send.at[kind, pos], recv_sem=sum_recv.at[target, pos, c],
            device_id=(b, device), device_id_type=MESH,
        )

    def sum_arrived(target, pos, rank):
        pltpu.make_async_remote_copy(
            src_ref=sums.at[target, pos, rank], dst_ref=sums.at[target, pos, rank],
            send_sem=sum_send.at[0, pos], recv_sem=sum_recv.at[target, pos, rank],
            device_id=(b, sibling), device_id_type=MESH,
        ).wait_recv()

    def add_up(pos):
        to_sibling(pos).wait_recv()
        sums[0, pos, c] = (part[pos] + part_in[pos].astype(jnp.float32)).astype(jnp.bfloat16)
        share(1, pos).start()
        share(0, pos).start()

    def pass_on(pos):
        sum_arrived(1, pos, c)
        share(2, pos).start()

    def work(pos):
        def look(s, carry):
            first, last, hits = carry
            hit = place[sector[s]] == pos
            first = jnp.where(hit & (hits == 0), s, first)
            last = jnp.where(hit, s, last)
            return first, last, hits + hit.astype(jnp.int32)

        zero = jnp.int32(0)
        s1, s2, hits = lax.fori_loop(0, states, look, (zero, zero, zero), unroll=True)
        if pair:
            s1, s2 = jnp.where(c == 0, s1, s2), jnp.where(c == 0, s2, s1)
        live = live_rows & (column_index < right_sizes[sector[s1]])

        def masked(s):
            return jnp.where(live, wave[s].astype(jnp.float32), 0.0).astype(jnp.bfloat16)

        both = jnp.concatenate([masked(s1), masked(s2)], axis=0)
        two = hits == 2
        for h in range(channels):
            factor = right_all[pos, h]

            parts = lax.dot_general(
                both, factor, (((1,), (1,)), ((), ())), preferred_element_type=jnp.float32
            ).astype(jnp.bfloat16).astype(jnp.float32)
            p1, p2 = parts[:rows], parts[rows:]
            table = ops[h].astype(jnp.float32)

            def op(s, t, keep=True):
                picked = (op_row == s) & (op_column == t) & keep
                return jnp.sum(jnp.where(picked, table, 0.0), keepdims=True)

            m1 = (op(s1, s1) * p1 + op(s1, s2, two) * p2).astype(jnp.bfloat16)
            m2 = (op(s2, s1, two) * p1 + op(s2, s2) * p2).astype(jnp.bfloat16)
            if pair:
                left_m = left[h]
                q1 = jnp.dot(left_m, m1, preferred_element_type=jnp.float32)
                q2 = jnp.dot(left_m, m2, preferred_element_type=jnp.float32)
                total1, total2 = (q1, q2) if h == 0 else (total1 + q1, total2 + q2)
            else:
                mixed[2 * pos, h] = m1
                mixed[2 * pos + 1, h] = m2
        if pair:
            part_out[pos] = total2.astype(jnp.bfloat16)
            to_sibling(pos).start()
            part[pos] = total1

    def at(g, i, body):
        sign = 1 - 2 * (i % 2)
        e = i // 2
        d = g - (e > 0).astype(jnp.int32)
        zs = z + sign * d
        xs = x + (e + 1) // 2 * (1 - 2 * (e % 2))

        @pl.when((zs >= 0) & (zs < nz) & (xs >= 0) & (xs < nx) & (d >= 0) & ((d > 0) | (sign > 0)))
        def _():
            body(zs, xs)

    items = 2 * (2 * nx - 1)

    def each(g, body):
        def one(i, _):
            at(g, i, body)
            return 0

        lax.fori_loop(0, items, one, 0)

    def multiply(g):
        def one(i, _):
            @pl.when(i < items)
            def _():
                at(g, i, use)

            @pl.when(i >= 2)
            def _():
                at(g, i - 2, lambda zs, xs: add_up(zs * nx + xs))

            return 0

        lax.fori_loop(0, items + 2, one, 0)

    def use(zs, xs):
        pos = zs * nx + xs

        @pl.when(xs != x)
        def _():
            for h in range(channels):
                arrived(pos, h)
                forward(zs, xs, h)

        work(pos)

    def gather_round(g, _):
        @pl.when((g > 0) & (g < nz))
        def _():
            for h in range(channels):
                for sign in (1, -1):
                    zs = z + sign * g

                    @pl.when((zs >= 0) & (zs < nz))
                    def _():
                        arrived(zs * nx + x, h)
                        forward(zs, x, h)

        @pl.when(g <= nz)
        def _():
            if pair:
                multiply(g)
            else:
                each(g, use)

        if pair:
            @pl.when(g > 1)
            def _():
                each(g - 2, lambda zs, xs: pass_on(zs * nx + xs))

        return 0

    lax.fori_loop(0, nz + (3 if pair else 1), gather_round, 0)

    def rank_of(s):
        def look(t, rank):
            return rank + ((t < s) & (sector[t] == sector[s])).astype(jnp.int32)

        return jnp.minimum(lax.fori_loop(0, states, look, jnp.int32(0), unroll=True), 1)

    def finish(pos, _):
        for h in range(channels):
            for k, wanted in enumerate(sends(pos // nx, pos % nx, h)):
                @pl.when(wanted)
                def _():
                    hop(pos, h, k, right_all.at[pos, h]).wait_send()
        if pair:
            to_sibling(pos).wait_send()
            for kind in range(3):
                share(kind, pos).wait_send()
        return 0

    if pair:
        def all_here(pos, _):
            sum_arrived(0, pos, 1 - c)
            sum_arrived(1, pos, 1 - c)
            return 0

        lax.fori_loop(0, n, all_here, 0)
        for q in range(per):
            s = p * per + q
            at, rank = place[sector[s]], rank_of(s)
            total = sums[0, at, rank].astype(jnp.float32) + sums[1, at, rank].astype(jnp.float32)
            live = live_rows & (column_index < right_sizes[sector[s]])
            out_ref[q] = jnp.where(live, total, 0.0).astype(jnp.bfloat16)
        lax.fori_loop(0, n, finish, 0)
        return

    def product(s):
        slot = 2 * place[sector[s]] + rank_of(s)
        total = jnp.dot(left[0], mixed[slot, 0], preferred_element_type=jnp.float32)
        for h in range(1, channels):
            total += jnp.dot(left[h], mixed[slot, h], preferred_element_type=jnp.float32)
        return total

    def owner_chip(i):
        return lax.rem(y + 1 + i // per, ny)

    def to_core(i):
        return pltpu.make_async_remote_copy(
            src_ref=out_core.at[i], dst_ref=in_core.at[i],
            send_sem=core_send.at[i], recv_sem=core_recv.at[i],
            device_id=(b, sibling), device_id_type=MESH,
        )

    def to_chip(i):
        return pltpu.make_async_remote_copy(
            src_ref=out_chip.at[i], dst_ref=in_chip.at[i],
            send_sem=chip_send.at[i], recv_sem=chip_recv.at[i],
            device_id=(b, owner_chip(i) * cores + c), device_id_type=MESH,
        )

    remote = (ny - 1) * per
    lag = min(3, count)

    def reduce_step(i, _):
        @pl.when(i < count)
        def _():
            s = (owner_chip(i) * cores + (1 - c)) * per + i % per
            out_core[i] = product(s).astype(jnp.bfloat16)
            to_core(i).start()

        @pl.when(i >= lag)
        def _():
            j = i - lag
            s = (owner_chip(j) * cores + c) * per + j % per
            total = product(s)
            to_core(j).wait_recv()
            total = total + in_core[j].astype(jnp.float32)

            @pl.when(j < remote)
            def _():
                out_chip[j] = total.astype(jnp.bfloat16)
                to_chip(j).start()

            @pl.when(j >= remote)
            def _():
                own[j - remote] = total

        return 0

    lax.fori_loop(0, count + lag, reduce_step, 0)

    for q in range(per):
        total = own[q]
        for dy in range(ny - 1):
            to_chip(dy * per + q).wait_recv()
            total = total + in_chip[dy * per + q].astype(jnp.float32)
        live = live_rows & (column_index < right_sizes[sector[p * per + q]])
        out_ref[q] = jnp.where(live, total, 0.0).astype(jnp.bfloat16)

    lax.fori_loop(0, n, finish, 0)

    def finish_core(i, _):
        to_core(i).wait_send()
        return 0

    lax.fori_loop(0, count, finish_core, 0)

    def finish_chip(i, _):
        to_chip(i).wait_send()
        return 0

    lax.fori_loop(0, remote, finish_chip, 0)


def sum_of(k, values):
    if isinstance(k, int):
        return values[k]
    total = 0
    for i, v in enumerate(values):
        if v:
            total = total + (k == i).astype(jnp.int32) * v
    return total


def halves_kernel(
    n, m,
    sector, place, left_sizes, right_sizes, ops_ref,
    wave_hbm, left_hbm, right_hbm,
    out_ref,
    right_all, away, wave, left, ops, coef, part, part_out, part_in, fin, arr, states_of, mine, held,
    local_sem, gather_send, gather_recv, early_send, left_recv, ops_send, ops_recv,
    part_send, part_recv, fin_send, fin_recv, pass_send, pass_recv, piece_recv,
):
    nz, nx = plane_of(n)
    states, rows, _ = wave.shape
    half = rows // 2
    channels = left_hbm.shape[0]
    per = out_ref.shape[0]
    units = 2 * channels
    b = lax.axis_index("bond")
    p = lax.axis_index("mpo")
    z, x = b // nx, b % nx
    y, c = p // 2, p % 2
    sibling = y * 2 + (1 - c)
    peer = (1 - y) * 2 + c
    end = (z == 0) | (z == nz - 1)
    way = 1 - 2 * (z >= nz // 2).astype(jnp.int32)
    bf16, f32 = jnp.bfloat16, jnp.float32
    L, S, X = 0, 1, 2
    targets = (b + way * nx, b - way * nx, z * nx + (1 - x))

    def own_half(h, of):
        return right_hbm.at[h, pl.ds(pl.multiple_of(of * half, half), half)]

    barrier = pltpu.get_barrier_semaphore()
    for target in (L, X):
        pl.semaphore_signal(barrier, inc=1, device_id=(targets[target], p), device_id_type=MESH)

    @pl.when(jnp.logical_not(end))
    def _():
        pl.semaphore_signal(barrier, inc=1, device_id=(targets[S], p), device_id_type=MESH)

    for other in (sibling, peer):
        pl.semaphore_signal(barrier, inc=1, device_id=(b, other), device_id_type=MESH)

    wave_copy = pltpu.make_async_copy(wave_hbm, wave, local_sem.at[0])
    left_copy = pltpu.make_async_copy(left_hbm, left.at[pl.ds(0, channels)], local_sem.at[1])
    own_copies = [
        pltpu.make_async_copy(own_half(h, 1 - y), away.at[h], local_sem.at[2])
        for h in range(channels)
    ] + [
        pltpu.make_async_copy(own_half(h, y), right_all.at[b, h], local_sem.at[2])
        for h in range(channels)
    ]
    for own in own_copies:
        own.start()
    left_copy.start()
    pl.semaphore_wait(barrier, 5 - end.astype(jnp.int32))

    def to_device(src, dst, send, recv, device):
        return pltpu.make_async_remote_copy(
            src_ref=src, dst_ref=dst, send_sem=send, recv_sem=recv,
            device_id=device, device_id_type=MESH,
        )

    def hop(pos, u, kind, src, batch=1):
        return to_device(
            src, right_all.at[pos, u], gather_send.at[batch], gather_recv.at[pos, u],
            (targets[kind], p),
        )

    whole = pl.ds(0, half)
    pieces = (pl.ds(0, half // 2), pl.ds(half // 2, half // 2))

    def first(h, at, recv):
        return to_device(
            away.at[h, at], right_all.at[b, channels + h, at], early_send, recv, (b, peer)
        )

    firsts = [(0, pieces[0], piece_recv), (0, pieces[1], gather_recv.at[b, channels])] + [
        (h, whole, gather_recv.at[b, channels + h]) for h in range(1, channels)
    ]

    def left_to_peer(h):
        return to_device(
            left.at[h], left.at[channels + h], early_send, left_recv, (b, peer)
        )

    ops_to_peer = to_device(
        ops_ref, ops.at[pl.ds(channels, channels)], ops_send, ops_recv, (b, peer)
    )

    pltpu.make_async_copy(right_hbm, left.at[pl.ds(0, channels)], local_sem.at[2]).wait()
    for h, at, recv in firsts:
        first(h, at, recv).start()
    for h in range(channels):
        for kind in (L, X):
            hop(b, h, kind, right_all.at[b, h], 0).start()

        @pl.when(jnp.logical_not(end))
        def _():
            hop(b, h, S, right_all.at[b, h], 0).start()

    left_copy.wait()
    ops_to_peer.start()
    for h in range(channels):
        left_to_peer(h).start()

    def place_of(off, other):
        return (z + way * off) * nx + ((1 - x) if other else x)

    def event(off, other, u, kinds):
        pos = place_of(off, other)
        if (off, other, u) == (0, 0, channels):
            for first_of in firsts[:2]:
                first(*first_of).wait_recv()
                view = right_all.at[b, u, first_of[1]]
                for kind in kinds:
                    to_device(
                        view, view, gather_send.at[0], gather_recv.at[b, u], (targets[kind], p)
                    ).start()
            return
        hop(pos, u, X, right_all.at[pos, u]).wait_recv()
        for kind in kinds:
            hop(pos, u, kind, right_all.at[pos, u], 0 if (off, other) == (0, 0) else 1).start()

    def settled(view, sem):
        to_device(view, view, sem, sem, (b, sibling)).wait_send()

    lo, hi = range(channels), range(channels, units)
    end_order = [(0, 0), (0, 1), (1, 0), (1, 1), (2, 0), (2, 1), (3, 0), (3, 1)]
    mid_order = [(0, 0), (0, 1), (-1, 0), (1, 0), (-1, 1), (2, 0), (1, 1), (2, 1)]
    end_before = {
        "own": [(0, 0, 2, (L, X)), (1, 0, 0, (X,)), (0, 0, 3, (L, X)), (1, 0, 1, (X,))],
        "start": [(1, 0, u, (X,)) for u in hi]
        + [(0, 1, u, ()) for u in lo] + [(0, 1, u, (L,)) for u in hi] + [(2, 0, 0, (X,))],
        1: [(2, 0, 1, (X,))],
        2: [(2, 0, 2, (X,))],
        3: [(2, 0, 3, (X,))] + [(1, 1, u, ()) for u in range(units)],
        4: [(3, 0, 0, (X,))],
        5: [(3, 0, 1, (X,))],
        "5 low": [(2, 1, u, ()) for u in lo],
        "5 high": [(2, 1, u, ()) for u in hi],
        "6 high": [(3, 0, u, ()) for u in hi],
    }
    mid_before = {
        "own": [
            (0, 0, 2, (L, S, X)), (0, 0, 3, (L, S, X)),
            (-1, 0, 0, (L, X)), (1, 0, 0, (S, X)), (-1, 0, 1, (L, X)), (1, 0, 1, (S, X)),
        ],
        "start": [
            (-1, 0, 2, (L,)), (1, 0, 2, (S, X)), (-1, 0, 3, (L,)), (1, 0, 3, (S, X)),
        ] + [(0, 1, u, ()) for u in range(units)] + [(2, 0, 0, (S, X))],
        1: [(2, 0, 1, (S, X)), (-1, 1, 2, (L,))],
        2: [(-1, 1, 3, (L,)), (2, 0, 2, (S,))],
        3: [(2, 0, 3, (S,))],
        4: [(2, 1, 2, (S,))] + [(-1, 1, u, ()) for u in lo],
        5: [(2, 1, 3, (S,))],
        "6 low": [(1, 1, u, ()) for u in lo],
        "6 high": [(1, 1, u, ()) for u in hi],
    }

    last_mid = lo

    def run(stage):
        @pl.when(end)
        def _():
            for e in end_before.get(stage, ()):
                event(*e)

        @pl.when(jnp.logical_not(end))
        def _():
            for e in mid_before.get(stage, ()):
                event(*e)

    def pos_of(k):
        off = jnp.where(end, sum_of(k, [o for o, _ in end_order]), sum_of(k, [o for o, _ in mid_order]))
        other = jnp.where(end, sum_of(k, [o for _, o in end_order]), sum_of(k, [o for _, o in mid_order]))
        return (z + way * off) * nx + x + other * (1 - 2 * x)

    def list_states(k, _):
        pos = pos_of(k)

        def look(s, carry):
            s1, s2 = carry
            hit = place[sector[s]] == pos
            return jnp.where(hit & (s < s1), s, s1), jnp.where(hit, s, s2)

        s1, s2 = lax.fori_loop(0, states, look, (jnp.int32(states - 1), jnp.int32(0)), unroll=True)
        states_of[k, 0] = s1
        states_of[k, 1] = s2
        states_of[k, 2] = right_sizes[sector[s1]]
        return 0

    lax.fori_loop(0, n, list_states, 0)

    def list_mine(q, _):
        s = p * per + q

        def look(t, rank):
            return rank + ((t < s) & (sector[t] == sector[s])).astype(jnp.int32)

        mine[q, 0] = place[sector[s]]
        mine[q, 1] = jnp.minimum(lax.fori_loop(0, states, look, jnp.int32(0), unroll=True), 1)
        return 0

    lax.fori_loop(0, per, list_mine, 0)

    def pick_operators():
        ops_to_peer.wait_recv()
        square = (states, states)
        op_row = lax.broadcasted_iota(jnp.int32, square, 0)
        op_column = lax.broadcasted_iota(jnp.int32, square, 1)
        named = jnp.zeros(square, jnp.int32)
        for r in range(states):
            named = jnp.where(op_row == r, states_of[r // 2, r % 2], named)
        pick = jnp.where(named == op_column, 1.0, 0.0).astype(bf16)
        same = op_row == op_column
        twin = op_row + 1 - 2 * (op_row % 2) == op_column
        for u in range(units):
            picked = jnp.dot(pick, ops[u], preferred_element_type=f32).astype(bf16)
            table = lax.dot_general(
                picked, pick, (((1,), (1,)), ((), ())), preferred_element_type=f32
            )
            for i, chosen in enumerate((same, twin)):
                column = jnp.sum(jnp.where(chosen, table, 0.0), axis=1, keepdims=True)
                coef[u, i] = jnp.broadcast_to(column, (states, 128))

    ops[pl.ds(0, channels)] = ops_ref[...]
    wave_copy.start()
    run("own")
    pick_operators()
    run("start")

    wave_copy.wait()
    both_left = left.at[pl.ds(channels, channels)]
    to_device(both_left, both_left, early_send, left_recv, (b, peer)).wait_recv()

    row_index = lax.broadcasted_iota(jnp.int32, (rows, rows), 0)
    column_index = lax.broadcasted_iota(jnp.int32, (rows, rows), 1)
    half_row = lax.broadcasted_iota(jnp.int32, (rows, half), 0)
    half_column = lax.broadcasted_iota(jnp.int32, (rows, half), 1) + y * half

    def to_sibling(pos):
        return to_device(
            part_out.at[pos], part_in.at[pos], part_send, part_recv.at[pos], (b, sibling)
        )

    def to_peer(pos):
        return to_device(fin.at[pos], arr.at[pos], fin_send, fin_recv.at[pos], (b, peer))

    def passing(pos):
        return to_device(arr.at[pos], arr.at[pos], pass_send, pass_recv, (b, sibling))

    def masked_pair(k):
        live = (row_index < left_sizes[b]) & (column_index < states_of[k, 2])

        def masked(s):
            return jnp.where(live, wave[s].astype(f32), 0.0).astype(bf16)

        return jnp.concatenate([masked(states_of[k, 0]), masked(states_of[k, 1])], axis=0)

    def products(k, both, units_of, factor):
        parts = lax.dot_general(
            both, factor, (((1,), (1,)), ((), ())), preferred_element_type=f32
        ).astype(bf16).astype(f32)
        total = None
        for i, u in enumerate(units_of):
            p1 = parts[:rows, i * half:(i + 1) * half]
            p2 = parts[rows:, i * half:(i + 1) * half]
            own1, own2 = coef[u, 0, pl.ds(2 * k, 1)], coef[u, 0, pl.ds(2 * k + 1, 1)]
            cross1, cross2 = coef[u, 1, pl.ds(2 * k, 1)], coef[u, 1, pl.ds(2 * k + 1, 1)]
            mixed = jnp.concatenate(
                [(own1 * p1 + cross1 * p2).astype(bf16), (cross2 * p1 + own2 * p2).astype(bf16)],
                axis=1,
            )
            product = jnp.dot(left[u], mixed, preferred_element_type=f32)
            total = product if total is None else total + product
        return total

    def some(k, both, units_of):
        factor = right_all[pos_of(k), pl.ds(units_of[0], channels)].reshape(channels * half, rows)
        return products(k, both, units_of, factor)

    def give(k, total):
        pos = pos_of(k)
        part_out[pos] = total.astype(bf16)
        to_sibling(pos).start()

    def compute(k):
        both = masked_pair(k)
        total = some(k, both, lo) + some(k, both, hi)
        give(k, total)
        part[pos_of(k)] = total

    def finish(k, total):
        part[pos_of(k)] = total

        @pl.when(c == 0)
        def _():
            add_up(k)
            send(k)

        give(k, part[pos_of(k)])

    def compute_last(k):
        pos = pos_of(k)
        held[...] = masked_pair(k)
        for i in range(channels):
            pair = (i, channels + i)

            @pl.when(end)
            def _():
                for u in pair:
                    event(3, 1, u, ())

            @pl.when(jnp.logical_not(end))
            def _():
                if pair[0] in last_mid:
                    event(2, 1, pair[0], ())

            factor = jnp.concatenate([right_all[pos, u] for u in pair], axis=0)
            total = products(k, held[...], pair, factor)
            if i == 0:
                part[pos] = total
            elif i < channels - 1:
                part[pos] += total
            else:
                finish(k, part[pos] + total)

    def add_up(k):
        pos = pos_of(k)
        to_sibling(pos).wait_recv()
        live = (half_row < left_sizes[b]) & (half_column < states_of[k, 2])
        for r in range(2):
            cut = slice(r * half, (r + 1) * half)
            total = part[pos, :, cut] + part_in[pos, :, cut].astype(f32)
            fin[pos, r] = jnp.where(live, total, 0.0).astype(bf16)

    def send(k):
        to_peer(pos_of(k)).start()

    def pass_on(k):
        pos = pos_of(k)
        to_peer(pos).wait_recv()
        passing(pos).start()

    def free_sends():
        settled(left.at[pl.ds(0, channels + channels // 2)], early_send)
        ops_to_peer.wait_send()

        @pl.when(end)
        def _():
            settled(right_all.at[pl.ds(0, 2)], gather_send.at[0])
            settled(right_all.at[pl.ds(0, 3)], gather_send.at[1])

        @pl.when(jnp.logical_not(end))
        def _():
            settled(right_all.at[pl.ds(0, 3)], gather_send.at[0])

    def on_core(core, *jobs):
        @pl.when(c == core)
        def _():
            for job, k in jobs:
                job(k)

    def step(k, _):
        for stage in range(1, 5):
            @pl.when(k == stage)
            def _():
                run(stage)

        compute(k)

        @pl.when((c == 0) & (k >= 1))
        def _():
            add_up(k - 1)
            send(k - 1)

        @pl.when((c == 1) & (k >= 3))
        def _():
            add_up(k - 3)

        return 0

    def low_half(k, _):
        for stage in (5, 6):
            @pl.when(k == stage)
            def _():
                run(f"{stage} low")

        part[pos_of(k)] = some(k, masked_pair(k), lo)
        return 0

    def high_half(k, _):
        for stage in (5, 6):
            @pl.when(k == stage)
            def _():
                run(f"{stage} high")

        finish(k, part[pos_of(k)] + some(k, masked_pair(k), hi))

        @pl.when(c == 1)
        def _():
            add_up(k - 3)

        return 0

    lax.fori_loop(0, 5, step, 0)
    run(5)
    on_core(0, (add_up, 4), (send, 4))
    lax.fori_loop(5, 7, low_half, 0)
    lax.fori_loop(5, 7, high_half, 0)
    on_core(0, (pass_on, 0), (pass_on, 1), (pass_on, 2))
    free_sends()
    compute_last(7)
    on_core(1, (add_up, 4))
    on_core(0, *[(pass_on, k) for k in range(3, n - 1)])
    on_core(1, (add_up, 5), (add_up, 6), (add_up, 7))

    @pl.when(jnp.logical_not(end))
    def _():
        settled(right_all.at[pl.ds(0, 6)], gather_send.at[1])

    settled(part_out, part_send)
    mine_at = pl.ds(pl.multiple_of(y * half, half), half)
    others_at = pl.ds(pl.multiple_of((1 - y) * half, half), half)
    for q in range(per):
        out_ref[q, :, mine_at] = fin[mine[q, 0], mine[q, 1]]

    @pl.when(c == 0)
    def _():
        settled(arr, fin_send)
        pass_on(n - 1)

    @pl.when(c == 1)
    def _():
        to_device(arr, arr, pass_send, pass_recv, (b, sibling)).wait_recv()

    for q in range(per):
        out_ref[q, :, others_at] = arr[mine[q, 0], mine[q, 1]]

    @pl.when(c == 0)
    def _():
        settled(arr, pass_send)


def shards(n, m, wave_blocks, left_environment, right_environment, site_operators,
           right_sector, left_sizes, right_sizes, sector_place):
    states, rows = wave_blocks.shape[1:3]
    channels = left_environment.shape[0]
    per = states // m
    cores = 2 if m % 2 == 0 else 1
    ny = m // cores
    count = ny * per
    remote = max(1, (ny - 1) * per)
    block = (rows, rows)
    bf16, f32 = jnp.bfloat16, jnp.float32
    smem = pl.BlockSpec(memory_space=pltpu.SMEM)
    hbm = pl.BlockSpec(memory_space=pl.ANY)
    dma = pltpu.SemaphoreType.DMA
    nz, nx = plane_of(n)
    by_halves = (nz, nx, ny, cores, channels) == (4, 2, 2, 2, 2) and states == 2 * n
    if by_halves:
        half = (rows // 2, rows)
        tall = (rows, rows // 2)
        scratch = [
            pltpu.VMEM((n, 2 * channels) + half, bf16),
            pltpu.VMEM((channels,) + half, bf16),
            pltpu.VMEM((states,) + block, bf16),
            pltpu.VMEM((2 * channels,) + block, bf16),
            pltpu.VMEM((2 * channels, states, states), bf16),
            pltpu.VMEM((2 * channels, 2, states, 128), f32),
            pltpu.VMEM((n,) + block, f32),
            pltpu.VMEM((n,) + block, bf16),
            pltpu.VMEM((n,) + block, bf16),
            pltpu.VMEM((n, 2) + tall, bf16),
            pltpu.VMEM((n, 2) + tall, bf16),
            pltpu.SMEM((n, 3), jnp.int32),
            pltpu.SMEM((per, 2), jnp.int32),
            pltpu.VMEM((2 * rows, rows), bf16),
            dma((3,)), dma((2,)), dma((n, 2 * channels)), dma, dma, dma, dma,
            dma, dma((n,)), dma, dma((n,)), dma, dma, dma,
        ]
    elif ny == 2 and cores == 2:
        rest = [
            pltpu.VMEM((n,) + block, f32),
            pltpu.VMEM((n,) + block, bf16),
            pltpu.VMEM((n,) + block, bf16),
            pltpu.VMEM((2, n, 2) + block, bf16),
            dma((n,)), dma((n,)), dma((3, n)), dma((2, n, 2)),
        ]
    else:
        rest = [
            pltpu.VMEM((2 * n, channels) + block, bf16),
            pltpu.VMEM((count,) + block, bf16),
            pltpu.VMEM((count,) + block, bf16),
            pltpu.VMEM((remote,) + block, bf16),
            pltpu.VMEM((remote,) + block, bf16),
            pltpu.VMEM((per,) + block, f32),
            dma((count,)), dma((count,)), dma((remote,)), dma((remote,)),
        ]
    if not by_halves:
        scratch = [
            pltpu.VMEM((n, channels) + block, bf16),
            pltpu.VMEM((states,) + block, bf16),
            pltpu.VMEM((channels,) + block, bf16),
            dma((3,)), dma((n, channels, 4)), dma((n, channels)),
            *rest,
        ]
    out = pl.pallas_call(
        functools.partial(halves_kernel if by_halves else kernel, n, m),
        out_shape=pltpu.VMEM((per,) + block, bf16),
        in_specs=[smem] * 4 + [pl.BlockSpec(memory_space=pltpu.VMEM)] + [hbm] * 3,
        out_specs=pl.BlockSpec(memory_space=pltpu.VMEM),
        scratch_shapes=scratch,
        compiler_params=pltpu.CompilerParams(
            collective_id=0, has_side_effects=True, vmem_limit_bytes=60 * 1024 * 1024
        ),
    )(
        right_sector.reshape(states), sector_place, left_sizes, right_sizes,
        site_operators,
        wave_blocks.reshape((states,) + block),
        left_environment.reshape((channels,) + block),
        right_environment.reshape((channels,) + block),
    )
    return out.reshape((1, per) + block)


def solution(mesh):
    placed = (
        P("bond", None, None, None),
        P("mpo", "bond", None, None),
        P("mpo", "bond", None, None),
        P("mpo", None, None),
        P("bond", None, None),
        P(),
        P(),
        P(),
    )
    body = functools.partial(shards, mesh.shape["bond"], mesh.shape["mpo"])
    return jax.shard_map(
        body, mesh=mesh, in_specs=placed, out_specs=P("bond", "mpo", None, None), check_vma=False
    )
```

```python
import functools

import jax
import jax.numpy as jnp
from jax import lax
from jax.experimental import pallas as pl
from jax.experimental.pallas import tpu as pltpu
from jax.sharding import PartitionSpec as P

MESH = pl.DeviceIdType.MESH


def plane_of(count):
    nx = 1
    while (2 * nx) * (2 * nx) * 2 <= count and count % (2 * nx) == 0:
        nx *= 2
    return count // nx, nx


def kernel(
    n, m,
    sector, place, left_sizes, right_sizes, ops,
    wave_hbm, left_hbm, right_hbm,
    out_ref,
    right_all, wave, left, local_sem, gather_send, gather_recv, *rest,
):
    nz, nx = plane_of(n)
    cores = 2 if m % 2 == 0 else 1
    ny = m // cores
    states, rows, _ = wave.shape
    channels = left.shape[0]
    per = out_ref.shape[0]
    count = ny * per
    pair = ny == 2 and cores == 2
    if pair:
        (part, part_out, part_in, sums,
         part_send, part_recv, sum_send, sum_recv) = rest
    else:
        (mixed, out_core, in_core, out_chip, in_chip, own,
         core_send, core_recv, chip_send, chip_recv) = rest
    b = lax.axis_index("bond")
    p = lax.axis_index("mpo")
    z, x = b // nx, b % nx
    y, c = p // cores, p % cores
    sibling = y * cores + (1 - c)

    wave_copy = pltpu.make_async_copy(wave_hbm, wave, local_sem.at[0])
    left_copy = pltpu.make_async_copy(left_hbm, left, local_sem.at[1])
    own_copy = pltpu.make_async_copy(right_hbm, right_all.at[b], local_sem.at[2])
    wave_copy.start()
    left_copy.start()
    own_copy.start()

    steps = ((nx, z + 1 < nz), (-nx, z > 0), (1, x + 1 < nx), (-1, x > 0))
    barrier = pltpu.get_barrier_semaphore()
    greeted = ny
    for step, there in steps:
        greeted = greeted + there.astype(jnp.int32)

        @pl.when(there)
        def _():
            pl.semaphore_signal(barrier, inc=1, device_id=(b + step, p), device_id_type=MESH)

    pl.semaphore_signal(barrier, inc=1, device_id=(b, sibling), device_id_type=MESH)
    for dy in range(1, ny):
        other = lax.rem(y + dy, ny) * cores + c
        pl.semaphore_signal(barrier, inc=1, device_id=(b, other), device_id_type=MESH)
    pl.semaphore_wait(barrier, greeted)

    def hop(pos, h, k, src):
        return pltpu.make_async_remote_copy(
            src_ref=src,
            dst_ref=right_all.at[pos, h],
            send_sem=gather_send.at[pos, h, k],
            recv_sem=gather_recv.at[pos, h],
            device_id=(b + steps[k][0], p),
            device_id_type=MESH,
        )

    def sends(zs, xs, h):
        column = xs == x
        if nx == 2 and h == channels - 1 and channels > 1:
            detour = (zs == 0) | (zs == nz - 1)
            along, across = column | detour, ~detour | (zs == z)
        else:
            along, across = column, True
        return (
            along & (zs <= z) & (z + 1 < nz),
            along & (zs >= z) & (z > 0),
            across & (xs <= x) & (x + 1 < nx),
            across & (xs >= x) & (x > 0),
        )

    def forward(zs, xs, h):
        pos = zs * nx + xs
        for k, wanted in enumerate(sends(zs, xs, h)):
            @pl.when(wanted)
            def _():
                hop(pos, h, k, right_all.at[pos, h]).start()

    def arrived(pos, h):
        hop(pos, h, 0, right_all.at[pos, h]).wait_recv()

    for h in range(channels):
        for k in (0, 1, 2, 3):
            @pl.when(steps[k][1])
            def _():
                hop(b, h, k, right_hbm.at[h]).start()

    wave_copy.wait()
    left_copy.wait()
    own_copy.wait()

    row_index = lax.broadcasted_iota(jnp.int32, (rows, rows), 0)
    column_index = lax.broadcasted_iota(jnp.int32, (rows, rows), 1)
    live_rows = row_index < left_sizes[b]
    op_row = lax.broadcasted_iota(jnp.int32, (states, states), 0)
    op_column = lax.broadcasted_iota(jnp.int32, (states, states), 1)

    def to_sibling(pos):
        return pltpu.make_async_remote_copy(
            src_ref=part_out.at[pos], dst_ref=part_in.at[pos],
            send_sem=part_send.at[pos], recv_sem=part_recv.at[pos],
            device_id=(b, sibling), device_id_type=MESH,
        )

    def share(kind, pos):
        source, target = (0, 0, 1)[kind], (0, 1, 1)[kind]
        device = (1 - y) * cores + c if kind == 1 else sibling
        return pltpu.make_async_remote_copy(
            src_ref=sums.at[source, pos, c], dst_ref=sums.at[target, pos, c],
            send_sem=sum_send.at[kind, pos], recv_sem=sum_recv.at[target, pos, c],
            device_id=(b, device), device_id_type=MESH,
        )

    def sum_arrived(target, pos, rank):
        pltpu.make_async_remote_copy(
            src_ref=sums.at[target, pos, rank], dst_ref=sums.at[target, pos, rank],
            send_sem=sum_send.at[0, pos], recv_sem=sum_recv.at[target, pos, rank],
            device_id=(b, sibling), device_id_type=MESH,
        ).wait_recv()

    def add_up(pos):
        to_sibling(pos).wait_recv()
        sums[0, pos, c] = (part[pos] + part_in[pos].astype(jnp.float32)).astype(jnp.bfloat16)
        share(1, pos).start()
        share(0, pos).start()

    def pass_on(pos):
        sum_arrived(1, pos, c)
        share(2, pos).start()

    def work(pos):
        def look(s, carry):
            first, last, hits = carry
            hit = place[sector[s]] == pos
            first = jnp.where(hit & (hits == 0), s, first)
            last = jnp.where(hit, s, last)
            return first, last, hits + hit.astype(jnp.int32)

        zero = jnp.int32(0)
        s1, s2, hits = lax.fori_loop(0, states, look, (zero, zero, zero), unroll=True)
        if pair:
            s1, s2 = jnp.where(c == 0, s1, s2), jnp.where(c == 0, s2, s1)
        live = live_rows & (column_index < right_sizes[sector[s1]])

        def masked(s):
            return jnp.where(live, wave[s].astype(jnp.float32), 0.0).astype(jnp.bfloat16)

        both = jnp.concatenate([masked(s1), masked(s2)], axis=0)
        two = hits == 2
        for h in range(channels):
            factor = right_all[pos, h]

            parts = lax.dot_general(
                both, factor, (((1,), (1,)), ((), ())), preferred_element_type=jnp.float32
            ).astype(jnp.bfloat16).astype(jnp.float32)
            p1, p2 = parts[:rows], parts[rows:]
            table = ops[h].astype(jnp.float32)

            def op(s, t, keep=True):
                picked = (op_row == s) & (op_column == t) & keep
                return jnp.sum(jnp.where(picked, table, 0.0), keepdims=True)

            m1 = (op(s1, s1) * p1 + op(s1, s2, two) * p2).astype(jnp.bfloat16)
            m2 = (op(s2, s1, two) * p1 + op(s2, s2) * p2).astype(jnp.bfloat16)
            if pair:
                left_m = left[h]
                q1 = jnp.dot(left_m, m1, preferred_element_type=jnp.float32)
                q2 = jnp.dot(left_m, m2, preferred_element_type=jnp.float32)
                total1, total2 = (q1, q2) if h == 0 else (total1 + q1, total2 + q2)
            else:
                mixed[2 * pos, h] = m1
                mixed[2 * pos + 1, h] = m2
        if pair:
            part_out[pos] = total2.astype(jnp.bfloat16)
            to_sibling(pos).start()
            part[pos] = total1

    def at(g, i, body):
        sign = 1 - 2 * (i % 2)
        e = i // 2
        d = g - (e > 0).astype(jnp.int32)
        zs = z + sign * d
        xs = x + (e + 1) // 2 * (1 - 2 * (e % 2))

        @pl.when((zs >= 0) & (zs < nz) & (xs >= 0) & (xs < nx) & (d >= 0) & ((d > 0) | (sign > 0)))
        def _():
            body(zs, xs)

    items = 2 * (2 * nx - 1)

    def each(g, body):
        def one(i, _):
            at(g, i, body)
            return 0

        lax.fori_loop(0, items, one, 0)

    def multiply(g):
        def one(i, _):
            @pl.when(i < items)
            def _():
                at(g, i, use)

            @pl.when(i >= 2)
            def _():
                at(g, i - 2, lambda zs, xs: add_up(zs * nx + xs))

            return 0

        lax.fori_loop(0, items + 2, one, 0)

    def use(zs, xs):
        pos = zs * nx + xs

        @pl.when(xs != x)
        def _():
            for h in range(channels):
                arrived(pos, h)
                forward(zs, xs, h)

        work(pos)

    def gather_round(g, _):
        @pl.when((g > 0) & (g < nz))
        def _():
            for h in range(channels):
                for sign in (1, -1):
                    zs = z + sign * g

                    @pl.when((zs >= 0) & (zs < nz))
                    def _():
                        arrived(zs * nx + x, h)
                        forward(zs, x, h)

        @pl.when(g <= nz)
        def _():
            if pair:
                multiply(g)
            else:
                each(g, use)

        if pair:
            @pl.when(g > 1)
            def _():
                each(g - 2, lambda zs, xs: pass_on(zs * nx + xs))

        return 0

    lax.fori_loop(0, nz + (3 if pair else 1), gather_round, 0)

    def rank_of(s):
        def look(t, rank):
            return rank + ((t < s) & (sector[t] == sector[s])).astype(jnp.int32)

        return jnp.minimum(lax.fori_loop(0, states, look, jnp.int32(0), unroll=True), 1)

    def finish(pos, _):
        for h in range(channels):
            for k, wanted in enumerate(sends(pos // nx, pos % nx, h)):
                @pl.when(wanted)
                def _():
                    hop(pos, h, k, right_all.at[pos, h]).wait_send()
        if pair:
            to_sibling(pos).wait_send()
            for kind in range(3):
                share(kind, pos).wait_send()
        return 0

    if pair:
        def all_here(pos, _):
            sum_arrived(0, pos, 1 - c)
            sum_arrived(1, pos, 1 - c)
            return 0

        lax.fori_loop(0, n, all_here, 0)
        for q in range(per):
            s = p * per + q
            at, rank = place[sector[s]], rank_of(s)
            total = sums[0, at, rank].astype(jnp.float32) + sums[1, at, rank].astype(jnp.float32)
            live = live_rows & (column_index < right_sizes[sector[s]])
            out_ref[q] = jnp.where(live, total, 0.0).astype(jnp.bfloat16)
        lax.fori_loop(0, n, finish, 0)
        return

    def product(s):
        slot = 2 * place[sector[s]] + rank_of(s)
        total = jnp.dot(left[0], mixed[slot, 0], preferred_element_type=jnp.float32)
        for h in range(1, channels):
            total += jnp.dot(left[h], mixed[slot, h], preferred_element_type=jnp.float32)
        return total

    def owner_chip(i):
        return lax.rem(y + 1 + i // per, ny)

    def to_core(i):
        return pltpu.make_async_remote_copy(
            src_ref=out_core.at[i], dst_ref=in_core.at[i],
            send_sem=core_send.at[i], recv_sem=core_recv.at[i],
            device_id=(b, sibling), device_id_type=MESH,
        )

    def to_chip(i):
        return pltpu.make_async_remote_copy(
            src_ref=out_chip.at[i], dst_ref=in_chip.at[i],
            send_sem=chip_send.at[i], recv_sem=chip_recv.at[i],
            device_id=(b, owner_chip(i) * cores + c), device_id_type=MESH,
        )

    remote = (ny - 1) * per
    lag = min(3, count)

    def reduce_step(i, _):
        @pl.when(i < count)
        def _():
            s = (owner_chip(i) * cores + (1 - c)) * per + i % per
            out_core[i] = product(s).astype(jnp.bfloat16)
            to_core(i).start()

        @pl.when(i >= lag)
        def _():
            j = i - lag
            s = (owner_chip(j) * cores + c) * per + j % per
            total = product(s)
            to_core(j).wait_recv()
            total = total + in_core[j].astype(jnp.float32)

            @pl.when(j < remote)
            def _():
                out_chip[j] = total.astype(jnp.bfloat16)
                to_chip(j).start()

            @pl.when(j >= remote)
            def _():
                own[j - remote] = total

        return 0

    lax.fori_loop(0, count + lag, reduce_step, 0)

    for q in range(per):
        total = own[q]
        for dy in range(ny - 1):
            to_chip(dy * per + q).wait_recv()
            total = total + in_chip[dy * per + q].astype(jnp.float32)
        live = live_rows & (column_index < right_sizes[sector[p * per + q]])
        out_ref[q] = jnp.where(live, total, 0.0).astype(jnp.bfloat16)

    lax.fori_loop(0, n, finish, 0)

    def finish_core(i, _):
        to_core(i).wait_send()
        return 0

    lax.fori_loop(0, count, finish_core, 0)

    def finish_chip(i, _):
        to_chip(i).wait_send()
        return 0

    lax.fori_loop(0, remote, finish_chip, 0)


def sum_of(k, values):
    if isinstance(k, int):
        return values[k]
    total = 0
    for i, v in enumerate(values):
        if v:
            total = total + (k == i).astype(jnp.int32) * v
    return total


def halves_kernel(
    n, m,
    sector, place, left_sizes, right_sizes, ops_ref,
    wave_hbm, left_hbm, right_hbm,
    out_ref,
    right_all, away, wave, left, ops, coef, part, part_out, part_in, fin, arr, states_of, mine, held,
    local_sem, gather_send, gather_recv, early_send, left_recv, ops_send, ops_recv,
    part_send, part_recv, fin_send, fin_recv, pass_send, pass_recv, piece_recv,
):
    nz, nx = plane_of(n)
    states, rows, _ = wave.shape
    half = rows // 2
    channels = left_hbm.shape[0]
    per = out_ref.shape[0]
    units = 2 * channels
    b = lax.axis_index("bond")
    p = lax.axis_index("mpo")
    z, x = b // nx, b % nx
    y, c = p // 2, p % 2
    sibling = y * 2 + (1 - c)
    peer = (1 - y) * 2 + c
    end = (z == 0) | (z == nz - 1)
    way = 1 - 2 * (z >= nz // 2).astype(jnp.int32)
    bf16, f32 = jnp.bfloat16, jnp.float32
    L, S, X = 0, 1, 2
    targets = (b + way * nx, b - way * nx, z * nx + (1 - x))

    def own_half(h, of):
        return right_hbm.at[h, pl.ds(pl.multiple_of(of * half, half), half)]

    barrier = pltpu.get_barrier_semaphore()
    for target in (L, X):
        pl.semaphore_signal(barrier, inc=1, device_id=(targets[target], p), device_id_type=MESH)

    @pl.when(jnp.logical_not(end))
    def _():
        pl.semaphore_signal(barrier, inc=1, device_id=(targets[S], p), device_id_type=MESH)

    for other in (sibling, peer):
        pl.semaphore_signal(barrier, inc=1, device_id=(b, other), device_id_type=MESH)

    wave_copy = pltpu.make_async_copy(wave_hbm, wave, local_sem.at[0])
    left_copy = pltpu.make_async_copy(left_hbm, left.at[pl.ds(0, channels)], local_sem.at[1])
    own_copies = [
        pltpu.make_async_copy(own_half(h, 1 - y), away.at[h], local_sem.at[2])
        for h in range(channels)
    ] + [
        pltpu.make_async_copy(own_half(h, y), right_all.at[b, h], local_sem.at[2])
        for h in range(channels)
    ]
    for own in own_copies:
        own.start()
    left_copy.start()
    pl.semaphore_wait(barrier, 5 - end.astype(jnp.int32))

    def to_device(src, dst, send, recv, device):
        return pltpu.make_async_remote_copy(
            src_ref=src, dst_ref=dst, send_sem=send, recv_sem=recv,
            device_id=device, device_id_type=MESH,
        )

    def hop(pos, u, kind, src, batch=1):
        return to_device(
            src, right_all.at[pos, u], gather_send.at[batch], gather_recv.at[pos, u],
            (targets[kind], p),
        )

    whole = pl.ds(0, half)
    pieces = (pl.ds(0, half // 2), pl.ds(half // 2, half // 2))

    def first(h, at, recv):
        return to_device(
            away.at[h, at], right_all.at[b, channels + h, at], early_send, recv, (b, peer)
        )

    firsts = [(0, pieces[0], piece_recv), (0, pieces[1], gather_recv.at[b, channels])] + [
        (h, whole, gather_recv.at[b, channels + h]) for h in range(1, channels)
    ]

    def left_to_peer(h):
        return to_device(
            left.at[h], left.at[channels + h], early_send, left_recv, (b, peer)
        )

    ops_to_peer = to_device(
        ops_ref, ops.at[pl.ds(channels, channels)], ops_send, ops_recv, (b, peer)
    )

    pltpu.make_async_copy(right_hbm, left.at[pl.ds(0, channels)], local_sem.at[2]).wait()
    for h, at, recv in firsts:
        first(h, at, recv).start()
    for h in range(channels):
        for kind in (L, X):
            hop(b, h, kind, right_all.at[b, h], 0).start()

        @pl.when(jnp.logical_not(end))
        def _():
            hop(b, h, S, right_all.at[b, h], 0).start()

    left_copy.wait()
    ops_to_peer.start()

    def send_left():
        for h in range(channels):
            left_to_peer(h).start()


    def place_of(off, other):
        return (z + way * off) * nx + ((1 - x) if other else x)

    def event(off, other, u, kinds):
        pos = place_of(off, other)
        if (off, other, u) == (0, 0, channels):
            for first_of in firsts[:2]:
                first(*first_of).wait_recv()
                view = right_all.at[b, u, first_of[1]]
                for kind in kinds:
                    to_device(
                        view, view, gather_send.at[0], gather_recv.at[b, u], (targets[kind], p)
                    ).start()
            return
        hop(pos, u, X, right_all.at[pos, u]).wait_recv()
        for kind in kinds:
            hop(pos, u, kind, right_all.at[pos, u], 0 if (off, other) == (0, 0) else 1).start()

    def settled(view, sem):
        to_device(view, view, sem, sem, (b, sibling)).wait_send()

    lo, hi = range(channels), range(channels, units)
    end_order = [(0, 0), (0, 1), (1, 0), (1, 1), (2, 0), (2, 1), (3, 0), (3, 1)]
    mid_order = [(0, 0), (0, 1), (-1, 0), (1, 0), (-1, 1), (2, 0), (1, 1), (2, 1)]
    end_before = {
        "own": [(0, 0, 2, (L, X)), (1, 0, 0, (X,)), (0, 0, 3, (L, X)), (1, 0, 1, (X,))],
        "start": [(1, 0, u, (X,)) for u in hi]
        + [(0, 1, u, ()) for u in lo] + [(0, 1, u, (L,)) for u in hi] + [(2, 0, 0, (X,))],
        1: [(2, 0, 1, (X,))],
        2: [(2, 0, 2, (X,))],
        3: [(2, 0, 3, (X,))] + [(1, 1, u, ()) for u in range(units)],
        4: [(3, 0, 0, (X,))],
        5: [(3, 0, 1, (X,))],
        "5 low": [(2, 1, u, ()) for u in lo],
        "5 high": [(2, 1, u, ()) for u in hi],
        "6 high": [(3, 0, u, ()) for u in hi],
    }
    mid_before = {
        "own": [
            (0, 0, 2, (L, S, X)), (0, 0, 3, (L, S, X)),
            (-1, 0, 0, (L, X)), (1, 0, 0, (S, X)), (-1, 0, 1, (L, X)), (1, 0, 1, (S, X)),
        ],
        "start": [
            (-1, 0, 2, (L,)), (1, 0, 2, (S, X)), (-1, 0, 3, (L,)), (1, 0, 3, (S, X)),
        ] + [(0, 1, u, ()) for u in range(units)] + [(2, 0, 0, (S, X))],
        1: [(2, 0, 1, (S, X)), (-1, 1, 2, (L,))],
        2: [(-1, 1, 3, (L,)), (2, 0, 2, (S,))],
        3: [(2, 0, 3, (S,))],
        4: [(2, 1, 2, (S,))] + [(-1, 1, u, ()) for u in lo],
        5: [(2, 1, 3, (S,))],
        "6 low": [(1, 1, u, ()) for u in lo],
        "6 high": [(1, 1, u, ()) for u in hi],
    }

    last_mid = lo

    def run(stage):
        @pl.when(end)
        def _():
            for e in end_before.get(stage, ()):
                event(*e)

        @pl.when(jnp.logical_not(end))
        def _():
            for e in mid_before.get(stage, ()):
                event(*e)

    def pos_of(k):
        off = jnp.where(end, sum_of(k, [o for o, _ in end_order]), sum_of(k, [o for o, _ in mid_order]))
        other = jnp.where(end, sum_of(k, [o for _, o in end_order]), sum_of(k, [o for _, o in mid_order]))
        return (z + way * off) * nx + x + other * (1 - 2 * x)

    def list_states(k, _):
        pos = pos_of(k)

        def look(s, carry):
            s1, s2 = carry
            hit = place[sector[s]] == pos
            return jnp.where(hit & (s < s1), s, s1), jnp.where(hit, s, s2)

        s1, s2 = lax.fori_loop(0, states, look, (jnp.int32(states - 1), jnp.int32(0)), unroll=True)
        states_of[k, 0] = s1
        states_of[k, 1] = s2
        states_of[k, 2] = right_sizes[sector[s1]]
        return 0

    lax.fori_loop(0, n, list_states, 0)

    def list_mine(q, _):
        s = p * per + q

        def look(t, rank):
            return rank + ((t < s) & (sector[t] == sector[s])).astype(jnp.int32)

        mine[q, 0] = place[sector[s]]
        mine[q, 1] = jnp.minimum(lax.fori_loop(0, states, look, jnp.int32(0), unroll=True), 1)
        return 0

    lax.fori_loop(0, per, list_mine, 0)

    def pick_operators():
        ops_to_peer.wait_recv()
        square = (states, states)
        op_row = lax.broadcasted_iota(jnp.int32, square, 0)
        op_column = lax.broadcasted_iota(jnp.int32, square, 1)
        named = jnp.zeros(square, jnp.int32)
        for r in range(states):
            named = jnp.where(op_row == r, states_of[r // 2, r % 2], named)
        pick = jnp.where(named == op_column, 1.0, 0.0).astype(bf16)
        same = op_row == op_column
        twin = op_row + 1 - 2 * (op_row % 2) == op_column
        for u in range(units):
            picked = jnp.dot(pick, ops[u], preferred_element_type=f32).astype(bf16)
            table = lax.dot_general(
                picked, pick, (((1,), (1,)), ((), ())), preferred_element_type=f32
            )
            for i, chosen in enumerate((same, twin)):
                column = jnp.sum(jnp.where(chosen, table, 0.0), axis=1, keepdims=True)
                coef[u, i] = jnp.broadcast_to(column, (states, 128))

    ops[pl.ds(0, channels)] = ops_ref[...]
    wave_copy.start()
    run("own")
    send_left()
    pick_operators()
    run("start")

    wave_copy.wait()
    both_left = left.at[pl.ds(channels, channels)]
    to_device(both_left, both_left, early_send, left_recv, (b, peer)).wait_recv()

    row_index = lax.broadcasted_iota(jnp.int32, (rows, rows), 0)
    column_index = lax.broadcasted_iota(jnp.int32, (rows, rows), 1)
    half_row = lax.broadcasted_iota(jnp.int32, (rows, half), 0)
    half_column = lax.broadcasted_iota(jnp.int32, (rows, half), 1) + y * half

    def to_sibling(pos):
        return to_device(
            part_out.at[pos], part_in.at[pos], part_send, part_recv.at[pos], (b, sibling)
        )

    def to_peer(pos):
        return to_device(fin.at[pos], arr.at[pos], fin_send, fin_recv.at[pos], (b, peer))

    def passing(pos):
        return to_device(arr.at[pos], arr.at[pos], pass_send, pass_recv, (b, sibling))

    def masked_pair(k):
        live = (row_index < left_sizes[b]) & (column_index < states_of[k, 2])

        def masked(s):
            return jnp.where(live, wave[s].astype(f32), 0.0).astype(bf16)

        return jnp.concatenate([masked(states_of[k, 0]), masked(states_of[k, 1])], axis=0)

    def products(k, both, units_of, factor):
        parts = lax.dot_general(
            both, factor, (((1,), (1,)), ((), ())), preferred_element_type=f32
        ).astype(bf16).astype(f32)
        total = None
        for i, u in enumerate(units_of):
            p1 = parts[:rows, i * half:(i + 1) * half]
            p2 = parts[rows:, i * half:(i + 1) * half]
            own1, own2 = coef[u, 0, pl.ds(2 * k, 1)], coef[u, 0, pl.ds(2 * k + 1, 1)]
            cross1, cross2 = coef[u, 1, pl.ds(2 * k, 1)], coef[u, 1, pl.ds(2 * k + 1, 1)]
            mixed = jnp.concatenate(
                [(own1 * p1 + cross1 * p2).astype(bf16), (cross2 * p1 + own2 * p2).astype(bf16)],
                axis=1,
            )
            product = jnp.dot(left[u], mixed, preferred_element_type=f32)
            total = product if total is None else total + product
        return total

    def some(k, both, units_of):
        factor = right_all[pos_of(k), pl.ds(units_of[0], channels)].reshape(channels * half, rows)
        return products(k, both, units_of, factor)

    def give(k, total):
        pos = pos_of(k)
        part_out[pos] = total.astype(bf16)
        to_sibling(pos).start()

    def compute(k):
        both = masked_pair(k)
        total = some(k, both, lo) + some(k, both, hi)
        give(k, total)
        part[pos_of(k)] = total

    def finish(k, total):
        part[pos_of(k)] = total

        @pl.when(c == 0)
        def _():
            add_up(k)
            send(k)

        give(k, part[pos_of(k)])

    def compute_last(k):
        pos = pos_of(k)
        held[...] = masked_pair(k)
        for i in range(channels):
            pair = (i, channels + i)

            @pl.when(end)
            def _():
                for u in pair:
                    event(3, 1, u, ())

            @pl.when(jnp.logical_not(end))
            def _():
                if pair[0] in last_mid:
                    event(2, 1, pair[0], ())

            factor = jnp.concatenate([right_all[pos, u] for u in pair], axis=0)
            total = products(k, held[...], pair, factor)
            if i == 0:
                part[pos] = total
            elif i < channels - 1:
                part[pos] += total
            else:
                finish(k, part[pos] + total)

    def add_up(k):
        pos = pos_of(k)
        to_sibling(pos).wait_recv()
        live = (half_row < left_sizes[b]) & (half_column < states_of[k, 2])
        for r in range(2):
            cut = slice(r * half, (r + 1) * half)
            total = part[pos, :, cut] + part_in[pos, :, cut].astype(f32)
            fin[pos, r] = jnp.where(live, total, 0.0).astype(bf16)

    def send(k):
        to_peer(pos_of(k)).start()

    def pass_on(k):
        pos = pos_of(k)
        to_peer(pos).wait_recv()
        passing(pos).start()

    def free_sends():
        settled(left.at[pl.ds(0, channels + channels // 2)], early_send)
        ops_to_peer.wait_send()

        @pl.when(end)
        def _():
            settled(right_all.at[pl.ds(0, 2)], gather_send.at[0])
            settled(right_all.at[pl.ds(0, 3)], gather_send.at[1])

        @pl.when(jnp.logical_not(end))
        def _():
            settled(right_all.at[pl.ds(0, 3)], gather_send.at[0])

    def on_core(core, *jobs):
        @pl.when(c == core)
        def _():
            for job, k in jobs:
                job(k)

    def step(k, _):
        for stage in range(1, 5):
            @pl.when(k == stage)
            def _():
                if stage >= 2:
                    on_core(1, (add_up, stage - 2))
                run(stage)

        compute(k)

        @pl.when((c == 0) & (k >= 1))
        def _():
            add_up(k - 1)
            send(k - 1)

        return 0

    def low_half(k, _):
        for stage in (5, 6):
            @pl.when(k == stage)
            def _():
                run(f"{stage} low")

        part[pos_of(k)] = some(k, masked_pair(k), lo)
        return 0

    def high_half(k, _):
        for stage in (5, 6):
            @pl.when(k == stage)
            def _():
                run(f"{stage} high")

        finish(k, part[pos_of(k)] + some(k, masked_pair(k), hi))
        return 0

    lax.fori_loop(0, 5, step, 0)
    on_core(1, (add_up, 3))
    run(5)
    on_core(0, (add_up, 4), (send, 4))
    lax.fori_loop(5, 7, low_half, 0)
    lax.fori_loop(5, 7, high_half, 0)
    on_core(0, (pass_on, 0), (pass_on, 1), (pass_on, 2))
    free_sends()
    compute_last(7)
    on_core(1, (add_up, 4))
    on_core(0, *[(pass_on, k) for k in range(3, n - 1)])
    on_core(1, (add_up, 5), (add_up, 6), (add_up, 7))

    @pl.when(jnp.logical_not(end))
    def _():
        settled(right_all.at[pl.ds(0, 6)], gather_send.at[1])

    settled(part_out, part_send)
    mine_at = pl.ds(pl.multiple_of(y * half, half), half)
    others_at = pl.ds(pl.multiple_of((1 - y) * half, half), half)
    for q in range(per):
        out_ref[q, :, mine_at] = fin[mine[q, 0], mine[q, 1]]

    @pl.when(c == 0)
    def _():
        settled(arr, fin_send)
        pass_on(n - 1)

    @pl.when(c == 1)
    def _():
        to_device(arr, arr, pass_send, pass_recv, (b, sibling)).wait_recv()

    for q in range(per):
        out_ref[q, :, others_at] = arr[mine[q, 0], mine[q, 1]]

    @pl.when(c == 0)
    def _():
        settled(arr, pass_send)


def shards(n, m, wave_blocks, left_environment, right_environment, site_operators,
           right_sector, left_sizes, right_sizes, sector_place):
    states, rows = wave_blocks.shape[1:3]
    channels = left_environment.shape[0]
    per = states // m
    cores = 2 if m % 2 == 0 else 1
    ny = m // cores
    count = ny * per
    remote = max(1, (ny - 1) * per)
    block = (rows, rows)
    bf16, f32 = jnp.bfloat16, jnp.float32
    smem = pl.BlockSpec(memory_space=pltpu.SMEM)
    hbm = pl.BlockSpec(memory_space=pl.ANY)
    dma = pltpu.SemaphoreType.DMA
    nz, nx = plane_of(n)
    by_halves = (nz, nx, ny, cores, channels) == (4, 2, 2, 2, 2) and states == 2 * n
    if by_halves:
        half = (rows // 2, rows)
        tall = (rows, rows // 2)
        scratch = [
            pltpu.VMEM((n, 2 * channels) + half, bf16),
            pltpu.VMEM((channels,) + half, bf16),
            pltpu.VMEM((states,) + block, bf16),
            pltpu.VMEM((2 * channels,) + block, bf16),
            pltpu.VMEM((2 * channels, states, states), bf16),
            pltpu.VMEM((2 * channels, 2, states, 128), f32),
            pltpu.VMEM((n,) + block, f32),
            pltpu.VMEM((n,) + block, bf16),
            pltpu.VMEM((n,) + block, bf16),
            pltpu.VMEM((n, 2) + tall, bf16),
            pltpu.VMEM((n, 2) + tall, bf16),
            pltpu.SMEM((n, 3), jnp.int32),
            pltpu.SMEM((per, 2), jnp.int32),
            pltpu.VMEM((2 * rows, rows), bf16),
            dma((3,)), dma((2,)), dma((n, 2 * channels)), dma, dma, dma, dma,
            dma, dma((n,)), dma, dma((n,)), dma, dma, dma,
        ]
    elif ny == 2 and cores == 2:
        rest = [
            pltpu.VMEM((n,) + block, f32),
            pltpu.VMEM((n,) + block, bf16),
            pltpu.VMEM((n,) + block, bf16),
            pltpu.VMEM((2, n, 2) + block, bf16),
            dma((n,)), dma((n,)), dma((3, n)), dma((2, n, 2)),
        ]
    else:
        rest = [
            pltpu.VMEM((2 * n, channels) + block, bf16),
            pltpu.VMEM((count,) + block, bf16),
            pltpu.VMEM((count,) + block, bf16),
            pltpu.VMEM((remote,) + block, bf16),
            pltpu.VMEM((remote,) + block, bf16),
            pltpu.VMEM((per,) + block, f32),
            dma((count,)), dma((count,)), dma((remote,)), dma((remote,)),
        ]
    if not by_halves:
        scratch = [
            pltpu.VMEM((n, channels) + block, bf16),
            pltpu.VMEM((states,) + block, bf16),
            pltpu.VMEM((channels,) + block, bf16),
            dma((3,)), dma((n, channels, 4)), dma((n, channels)),
            *rest,
        ]
    out = pl.pallas_call(
        functools.partial(halves_kernel if by_halves else kernel, n, m),
        out_shape=pltpu.VMEM((per,) + block, bf16),
        in_specs=[smem] * 4 + [pl.BlockSpec(memory_space=pltpu.VMEM)] + [hbm] * 3,
        out_specs=pl.BlockSpec(memory_space=pltpu.VMEM),
        scratch_shapes=scratch,
        compiler_params=pltpu.CompilerParams(
            collective_id=0, has_side_effects=True, vmem_limit_bytes=60 * 1024 * 1024
        ),
    )(
        right_sector.reshape(states), sector_place, left_sizes, right_sizes,
        site_operators,
        wave_blocks.reshape((states,) + block),
        left_environment.reshape((channels,) + block),
        right_environment.reshape((channels,) + block),
    )
    return out.reshape((1, per) + block)


def solution(mesh):
    placed = (
        P("bond", None, None, None),
        P("mpo", "bond", None, None),
        P("mpo", "bond", None, None),
        P("mpo", None, None),
        P("bond", None, None),
        P(),
        P(),
        P(),
    )
    body = functools.partial(shards, mesh.shape["bond"], mesh.shape["mpo"])
    return jax.shard_map(
        body, mesh=mesh, in_specs=placed, out_specs=P("bond", "mpo", None, None), check_vma=False
    )
```

```python
import functools

import jax
import jax.numpy as jnp
from jax import lax
from jax.experimental import pallas as pl
from jax.experimental.pallas import tpu as pltpu
from jax.sharding import PartitionSpec as P

MESH = pl.DeviceIdType.MESH


def plane_of(count):
    nx = 1
    while (2 * nx) * (2 * nx) * 2 <= count and count % (2 * nx) == 0:
        nx *= 2
    return count // nx, nx


def kernel(
    n, m,
    sector, place, left_sizes, right_sizes, ops,
    wave_hbm, left_hbm, right_hbm,
    out_ref,
    right_all, wave, left, local_sem, gather_send, gather_recv, *rest,
):
    nz, nx = plane_of(n)
    cores = 2 if m % 2 == 0 else 1
    ny = m // cores
    states, rows, _ = wave.shape
    channels = left.shape[0]
    per = out_ref.shape[0]
    count = ny * per
    pair = ny == 2 and cores == 2
    if pair:
        (part, part_out, part_in, sums,
         part_send, part_recv, sum_send, sum_recv) = rest
    else:
        (mixed, out_core, in_core, out_chip, in_chip, own,
         core_send, core_recv, chip_send, chip_recv) = rest
    b = lax.axis_index("bond")
    p = lax.axis_index("mpo")
    z, x = b // nx, b % nx
    y, c = p // cores, p % cores
    sibling = y * cores + (1 - c)

    wave_copy = pltpu.make_async_copy(wave_hbm, wave, local_sem.at[0])
    left_copy = pltpu.make_async_copy(left_hbm, left, local_sem.at[1])
    own_copy = pltpu.make_async_copy(right_hbm, right_all.at[b], local_sem.at[2])
    wave_copy.start()
    left_copy.start()
    own_copy.start()

    steps = ((nx, z + 1 < nz), (-nx, z > 0), (1, x + 1 < nx), (-1, x > 0))
    barrier = pltpu.get_barrier_semaphore()
    greeted = ny
    for step, there in steps:
        greeted = greeted + there.astype(jnp.int32)

        @pl.when(there)
        def _():
            pl.semaphore_signal(barrier, inc=1, device_id=(b + step, p), device_id_type=MESH)

    pl.semaphore_signal(barrier, inc=1, device_id=(b, sibling), device_id_type=MESH)
    for dy in range(1, ny):
        other = lax.rem(y + dy, ny) * cores + c
        pl.semaphore_signal(barrier, inc=1, device_id=(b, other), device_id_type=MESH)
    pl.semaphore_wait(barrier, greeted)

    def hop(pos, h, k, src):
        return pltpu.make_async_remote_copy(
            src_ref=src,
            dst_ref=right_all.at[pos, h],
            send_sem=gather_send.at[pos, h, k],
            recv_sem=gather_recv.at[pos, h],
            device_id=(b + steps[k][0], p),
            device_id_type=MESH,
        )

    def sends(zs, xs, h):
        column = xs == x
        if nx == 2 and h == channels - 1 and channels > 1:
            detour = (zs == 0) | (zs == nz - 1)
            along, across = column | detour, ~detour | (zs == z)
        else:
            along, across = column, True
        return (
            along & (zs <= z) & (z + 1 < nz),
            along & (zs >= z) & (z > 0),
            across & (xs <= x) & (x + 1 < nx),
            across & (xs >= x) & (x > 0),
        )

    def forward(zs, xs, h):
        pos = zs * nx + xs
        for k, wanted in enumerate(sends(zs, xs, h)):
            @pl.when(wanted)
            def _():
                hop(pos, h, k, right_all.at[pos, h]).start()

    def arrived(pos, h):
        hop(pos, h, 0, right_all.at[pos, h]).wait_recv()

    for h in range(channels):
        for k in (0, 1, 2, 3):
            @pl.when(steps[k][1])
            def _():
                hop(b, h, k, right_hbm.at[h]).start()

    wave_copy.wait()
    left_copy.wait()
    own_copy.wait()

    row_index = lax.broadcasted_iota(jnp.int32, (rows, rows), 0)
    column_index = lax.broadcasted_iota(jnp.int32, (rows, rows), 1)
    live_rows = row_index < left_sizes[b]
    op_row = lax.broadcasted_iota(jnp.int32, (states, states), 0)
    op_column = lax.broadcasted_iota(jnp.int32, (states, states), 1)

    def to_sibling(pos):
        return pltpu.make_async_remote_copy(
            src_ref=part_out.at[pos], dst_ref=part_in.at[pos],
            send_sem=part_send.at[pos], recv_sem=part_recv.at[pos],
            device_id=(b, sibling), device_id_type=MESH,
        )

    def share(kind, pos):
        source, target = (0, 0, 1)[kind], (0, 1, 1)[kind]
        device = (1 - y) * cores + c if kind == 1 else sibling
        return pltpu.make_async_remote_copy(
            src_ref=sums.at[source, pos, c], dst_ref=sums.at[target, pos, c],
            send_sem=sum_send.at[kind, pos], recv_sem=sum_recv.at[target, pos, c],
            device_id=(b, device), device_id_type=MESH,
        )

    def sum_arrived(target, pos, rank):
        pltpu.make_async_remote_copy(
            src_ref=sums.at[target, pos, rank], dst_ref=sums.at[target, pos, rank],
            send_sem=sum_send.at[0, pos], recv_sem=sum_recv.at[target, pos, rank],
            device_id=(b, sibling), device_id_type=MESH,
        ).wait_recv()

    def add_up(pos):
        to_sibling(pos).wait_recv()
        sums[0, pos, c] = (part[pos] + part_in[pos].astype(jnp.float32)).astype(jnp.bfloat16)
        share(1, pos).start()
        share(0, pos).start()

    def pass_on(pos):
        sum_arrived(1, pos, c)
        share(2, pos).start()

    def work(pos):
        def look(s, carry):
            first, last, hits = carry
            hit = place[sector[s]] == pos
            first = jnp.where(hit & (hits == 0), s, first)
            last = jnp.where(hit, s, last)
            return first, last, hits + hit.astype(jnp.int32)

        zero = jnp.int32(0)
        s1, s2, hits = lax.fori_loop(0, states, look, (zero, zero, zero), unroll=True)
        if pair:
            s1, s2 = jnp.where(c == 0, s1, s2), jnp.where(c == 0, s2, s1)
        live = live_rows & (column_index < right_sizes[sector[s1]])

        def masked(s):
            return jnp.where(live, wave[s].astype(jnp.float32), 0.0).astype(jnp.bfloat16)

        both = jnp.concatenate([masked(s1), masked(s2)], axis=0)
        two = hits == 2
        for h in range(channels):
            factor = right_all[pos, h]

            parts = lax.dot_general(
                both, factor, (((1,), (1,)), ((), ())), preferred_element_type=jnp.float32
            ).astype(jnp.bfloat16).astype(jnp.float32)
            p1, p2 = parts[:rows], parts[rows:]
            table = ops[h].astype(jnp.float32)

            def op(s, t, keep=True):
                picked = (op_row == s) & (op_column == t) & keep
                return jnp.sum(jnp.where(picked, table, 0.0), keepdims=True)

            m1 = (op(s1, s1) * p1 + op(s1, s2, two) * p2).astype(jnp.bfloat16)
            m2 = (op(s2, s1, two) * p1 + op(s2, s2) * p2).astype(jnp.bfloat16)
            if pair:
                left_m = left[h]
                q1 = jnp.dot(left_m, m1, preferred_element_type=jnp.float32)
                q2 = jnp.dot(left_m, m2, preferred_element_type=jnp.float32)
                total1, total2 = (q1, q2) if h == 0 else (total1 + q1, total2 + q2)
            else:
                mixed[2 * pos, h] = m1
                mixed[2 * pos + 1, h] = m2
        if pair:
            part_out[pos] = total2.astype(jnp.bfloat16)
            to_sibling(pos).start()
            part[pos] = total1

    def at(g, i, body):
        sign = 1 - 2 * (i % 2)
        e = i // 2
        d = g - (e > 0).astype(jnp.int32)
        zs = z + sign * d
        xs = x + (e + 1) // 2 * (1 - 2 * (e % 2))

        @pl.when((zs >= 0) & (zs < nz) & (xs >= 0) & (xs < nx) & (d >= 0) & ((d > 0) | (sign > 0)))
        def _():
            body(zs, xs)

    items = 2 * (2 * nx - 1)

    def each(g, body):
        def one(i, _):
            at(g, i, body)
            return 0

        lax.fori_loop(0, items, one, 0)

    def multiply(g):
        def one(i, _):
            @pl.when(i < items)
            def _():
                at(g, i, use)

            @pl.when(i >= 2)
            def _():
                at(g, i - 2, lambda zs, xs: add_up(zs * nx + xs))

            return 0

        lax.fori_loop(0, items + 2, one, 0)

    def use(zs, xs):
        pos = zs * nx + xs

        @pl.when(xs != x)
        def _():
            for h in range(channels):
                arrived(pos, h)
                forward(zs, xs, h)

        work(pos)

    def gather_round(g, _):
        @pl.when((g > 0) & (g < nz))
        def _():
            for h in range(channels):
                for sign in (1, -1):
                    zs = z + sign * g

                    @pl.when((zs >= 0) & (zs < nz))
                    def _():
                        arrived(zs * nx + x, h)
                        forward(zs, x, h)

        @pl.when(g <= nz)
        def _():
            if pair:
                multiply(g)
            else:
                each(g, use)

        if pair:
            @pl.when(g > 1)
            def _():
                each(g - 2, lambda zs, xs: pass_on(zs * nx + xs))

        return 0

    lax.fori_loop(0, nz + (3 if pair else 1), gather_round, 0)

    def rank_of(s):
        def look(t, rank):
            return rank + ((t < s) & (sector[t] == sector[s])).astype(jnp.int32)

        return jnp.minimum(lax.fori_loop(0, states, look, jnp.int32(0), unroll=True), 1)

    def finish(pos, _):
        for h in range(channels):
            for k, wanted in enumerate(sends(pos // nx, pos % nx, h)):
                @pl.when(wanted)
                def _():
                    hop(pos, h, k, right_all.at[pos, h]).wait_send()
        if pair:
            to_sibling(pos).wait_send()
            for kind in range(3):
                share(kind, pos).wait_send()
        return 0

    if pair:
        def all_here(pos, _):
            sum_arrived(0, pos, 1 - c)
            sum_arrived(1, pos, 1 - c)
            return 0

        lax.fori_loop(0, n, all_here, 0)
        for q in range(per):
            s = p * per + q
            at, rank = place[sector[s]], rank_of(s)
            total = sums[0, at, rank].astype(jnp.float32) + sums[1, at, rank].astype(jnp.float32)
            live = live_rows & (column_index < right_sizes[sector[s]])
            out_ref[q] = jnp.where(live, total, 0.0).astype(jnp.bfloat16)
        lax.fori_loop(0, n, finish, 0)
        return

    def product(s):
        slot = 2 * place[sector[s]] + rank_of(s)
        total = jnp.dot(left[0], mixed[slot, 0], preferred_element_type=jnp.float32)
        for h in range(1, channels):
            total += jnp.dot(left[h], mixed[slot, h], preferred_element_type=jnp.float32)
        return total

    def owner_chip(i):
        return lax.rem(y + 1 + i // per, ny)

    def to_core(i):
        return pltpu.make_async_remote_copy(
            src_ref=out_core.at[i], dst_ref=in_core.at[i],
            send_sem=core_send.at[i], recv_sem=core_recv.at[i],
            device_id=(b, sibling), device_id_type=MESH,
        )

    def to_chip(i):
        return pltpu.make_async_remote_copy(
            src_ref=out_chip.at[i], dst_ref=in_chip.at[i],
            send_sem=chip_send.at[i], recv_sem=chip_recv.at[i],
            device_id=(b, owner_chip(i) * cores + c), device_id_type=MESH,
        )

    remote = (ny - 1) * per
    lag = min(3, count)

    def reduce_step(i, _):
        @pl.when(i < count)
        def _():
            s = (owner_chip(i) * cores + (1 - c)) * per + i % per
            out_core[i] = product(s).astype(jnp.bfloat16)
            to_core(i).start()

        @pl.when(i >= lag)
        def _():
            j = i - lag
            s = (owner_chip(j) * cores + c) * per + j % per
            total = product(s)
            to_core(j).wait_recv()
            total = total + in_core[j].astype(jnp.float32)

            @pl.when(j < remote)
            def _():
                out_chip[j] = total.astype(jnp.bfloat16)
                to_chip(j).start()

            @pl.when(j >= remote)
            def _():
                own[j - remote] = total

        return 0

    lax.fori_loop(0, count + lag, reduce_step, 0)

    for q in range(per):
        total = own[q]
        for dy in range(ny - 1):
            to_chip(dy * per + q).wait_recv()
            total = total + in_chip[dy * per + q].astype(jnp.float32)
        live = live_rows & (column_index < right_sizes[sector[p * per + q]])
        out_ref[q] = jnp.where(live, total, 0.0).astype(jnp.bfloat16)

    lax.fori_loop(0, n, finish, 0)

    def finish_core(i, _):
        to_core(i).wait_send()
        return 0

    lax.fori_loop(0, count, finish_core, 0)

    def finish_chip(i, _):
        to_chip(i).wait_send()
        return 0

    lax.fori_loop(0, remote, finish_chip, 0)


def sum_of(k, values):
    if isinstance(k, int):
        return values[k]
    total = 0
    for i, v in enumerate(values):
        if v:
            total = total + (k == i).astype(jnp.int32) * v
    return total


def halves_kernel(
    n, m,
    sector, place, left_sizes, right_sizes, ops_ref,
    wave_hbm, left_hbm, right_hbm,
    out_ref,
    right_all, away, wave, left, ops, coef, part, part_out, part_in, fin, arr, states_of, mine, held,
    local_sem, gather_send, gather_recv, early_send, left_recv, ops_send, ops_recv,
    part_send, part_recv, fin_send, fin_recv, pass_send, pass_recv, piece_recv, last_recv,
):
    nz, nx = plane_of(n)
    states, rows, _ = wave.shape
    half = rows // 2
    channels = left_hbm.shape[0]
    per = out_ref.shape[0]
    units = 2 * channels
    b = lax.axis_index("bond")
    p = lax.axis_index("mpo")
    z, x = b // nx, b % nx
    y, c = p // 2, p % 2
    sibling = y * 2 + (1 - c)
    peer = (1 - y) * 2 + c
    end = (z == 0) | (z == nz - 1)
    way = 1 - 2 * (z >= nz // 2).astype(jnp.int32)
    bf16, f32 = jnp.bfloat16, jnp.float32
    L, S, X = 0, 1, 2
    targets = (b + way * nx, b - way * nx, z * nx + (1 - x))

    def own_half(h, of):
        return right_hbm.at[h, pl.ds(pl.multiple_of(of * half, half), half)]

    barrier = pltpu.get_barrier_semaphore()
    for target in (L, X):
        pl.semaphore_signal(barrier, inc=1, device_id=(targets[target], p), device_id_type=MESH)

    @pl.when(jnp.logical_not(end))
    def _():
        pl.semaphore_signal(barrier, inc=1, device_id=(targets[S], p), device_id_type=MESH)

    for other in (sibling, peer):
        pl.semaphore_signal(barrier, inc=1, device_id=(b, other), device_id_type=MESH)

    wave_copy = pltpu.make_async_copy(wave_hbm, wave, local_sem.at[0])
    left_copy = pltpu.make_async_copy(left_hbm, left.at[pl.ds(0, channels)], local_sem.at[1])
    own_copies = [
        pltpu.make_async_copy(own_half(h, 1 - y), away.at[h], local_sem.at[2])
        for h in range(channels)
    ] + [
        pltpu.make_async_copy(own_half(h, y), right_all.at[b, h], local_sem.at[2])
        for h in range(channels)
    ]
    for own in own_copies:
        own.start()
    left_copy.start()
    pl.semaphore_wait(barrier, 5 - end.astype(jnp.int32))

    def to_device(src, dst, send, recv, device):
        return pltpu.make_async_remote_copy(
            src_ref=src, dst_ref=dst, send_sem=send, recv_sem=recv,
            device_id=device, device_id_type=MESH,
        )

    def hop(pos, u, kind, src, batch=1):
        return to_device(
            src, right_all.at[pos, u], gather_send.at[batch], gather_recv.at[pos, u],
            (targets[kind], p),
        )

    whole = pl.ds(0, half)
    pieces = (pl.ds(0, half // 2), pl.ds(half // 2, half // 2))

    def first(h, at, recv):
        return to_device(
            away.at[h, at], right_all.at[b, channels + h, at], early_send, recv, (b, peer)
        )

    firsts = [(0, pieces[0], piece_recv), (0, pieces[1], gather_recv.at[b, channels])] + [
        (h, whole, gather_recv.at[b, channels + h]) for h in range(1, channels)
    ]

    def left_to_peer(h):
        return to_device(
            left.at[h], left.at[channels + h], early_send, left_recv, (b, peer)
        )

    ops_to_peer = to_device(
        ops_ref, ops.at[pl.ds(channels, channels)], ops_send, ops_recv, (b, peer)
    )

    pltpu.make_async_copy(right_hbm, left.at[pl.ds(0, channels)], local_sem.at[2]).wait()
    for h, at, recv in firsts:
        first(h, at, recv).start()
    for h in range(channels):
        for kind in (L, X):
            hop(b, h, kind, right_all.at[b, h], 0).start()

        @pl.when(jnp.logical_not(end))
        def _():
            hop(b, h, S, right_all.at[b, h], 0).start()

    left_copy.wait()
    ops_to_peer.start()

    def send_left():
        for h in range(channels):
            left_to_peer(h).start()


    def place_of(off, other):
        return (z + way * off) * nx + ((1 - x) if other else x)

    def event(off, other, u, kinds):
        pos = place_of(off, other)
        if (off, other, u) == (0, 0, channels):
            for first_of in firsts[:2]:
                first(*first_of).wait_recv()
                view = right_all.at[b, u, first_of[1]]
                for kind in kinds:
                    to_device(
                        view, view, gather_send.at[0], gather_recv.at[b, u], (targets[kind], p)
                    ).start()
            return
        hop(pos, u, X, right_all.at[pos, u]).wait_recv()
        for kind in kinds:
            hop(pos, u, kind, right_all.at[pos, u], 0 if (off, other) == (0, 0) else 1).start()

    def settled(view, sem):
        to_device(view, view, sem, sem, (b, sibling)).wait_send()

    lo, hi = range(channels), range(channels, units)
    end_order = [(0, 0), (0, 1), (1, 0), (1, 1), (2, 0), (2, 1), (3, 0), (3, 1)]
    mid_order = [(0, 0), (0, 1), (-1, 0), (1, 0), (-1, 1), (2, 0), (1, 1), (2, 1)]
    end_before = {
        "own": [(0, 0, 2, (L, X)), (1, 0, 0, (X,)), (0, 0, 3, (L, X)), (1, 0, 1, (X,))],
        "start": [(1, 0, u, (X,)) for u in hi]
        + [(0, 1, u, ()) for u in lo] + [(0, 1, u, (L,)) for u in hi] + [(2, 0, 0, (X,))],
        1: [(2, 0, 1, (X,))],
        2: [(2, 0, 2, (X,))],
        3: [(2, 0, 3, (X,))] + [(1, 1, u, ()) for u in range(units)],
        4: [(3, 0, 0, (X,))],
        5: [(3, 0, 1, (X,))],
        "5 low": [(2, 1, u, ()) for u in lo],
        "5 third": [(2, 1, channels, ())],
        "5 last": [(2, 1, u, ()) for u in hi[1:]],
        "6 high": [(3, 0, u, ()) for u in hi],
    }
    mid_before = {
        "own": [
            (0, 0, 2, (L, S, X)), (0, 0, 3, (L, S, X)),
            (-1, 0, 0, (L, X)), (1, 0, 0, (S, X)), (-1, 0, 1, (L, X)), (1, 0, 1, (S, X)),
        ],
        "start": [
            (-1, 0, 2, (L,)), (1, 0, 2, (S, X)), (-1, 0, 3, (L,)), (1, 0, 3, (S, X)),
        ] + [(0, 1, u, ()) for u in range(units)] + [(2, 0, 0, (S, X))],
        1: [(2, 0, 1, (S, X)), (-1, 1, 2, (L,))],
        2: [(-1, 1, 3, (L,)), (2, 0, 2, (S,))],
        3: [(2, 0, 3, (S,))],
        4: [(2, 1, 2, (S,))] + [(-1, 1, u, ()) for u in lo],
        5: [(2, 1, 3, (S,))],
        "6 low": [(1, 1, u, ()) for u in lo],
        "6 high": [(1, 1, u, ()) for u in hi],
    }

    last_mid = lo

    def run(stage):
        @pl.when(end)
        def _():
            for e in end_before.get(stage, ()):
                event(*e)

        @pl.when(jnp.logical_not(end))
        def _():
            for e in mid_before.get(stage, ()):
                event(*e)

    def pos_of(k):
        off = jnp.where(end, sum_of(k, [o for o, _ in end_order]), sum_of(k, [o for o, _ in mid_order]))
        other = jnp.where(end, sum_of(k, [o for _, o in end_order]), sum_of(k, [o for _, o in mid_order]))
        return (z + way * off) * nx + x + other * (1 - 2 * x)

    def list_states(k, _):
        pos = pos_of(k)

        def look(s, carry):
            s1, s2 = carry
            hit = place[sector[s]] == pos
            return jnp.where(hit & (s < s1), s, s1), jnp.where(hit, s, s2)

        s1, s2 = lax.fori_loop(0, states, look, (jnp.int32(states - 1), jnp.int32(0)), unroll=True)
        states_of[k, 0] = s1
        states_of[k, 1] = s2
        states_of[k, 2] = right_sizes[sector[s1]]
        return 0

    lax.fori_loop(0, n, list_states, 0)

    def list_mine(q, _):
        s = p * per + q

        def look(t, rank):
            return rank + ((t < s) & (sector[t] == sector[s])).astype(jnp.int32)

        mine[q, 0] = place[sector[s]]
        mine[q, 1] = jnp.minimum(lax.fori_loop(0, states, look, jnp.int32(0), unroll=True), 1)
        return 0

    lax.fori_loop(0, per, list_mine, 0)

    def pick_operators():
        ops_to_peer.wait_recv()
        square = (states, states)
        op_row = lax.broadcasted_iota(jnp.int32, square, 0)
        op_column = lax.broadcasted_iota(jnp.int32, square, 1)
        named = jnp.zeros(square, jnp.int32)
        for r in range(states):
            named = jnp.where(op_row == r, states_of[r // 2, r % 2], named)
        pick = jnp.where(named == op_column, 1.0, 0.0).astype(bf16)
        same = op_row == op_column
        twin = op_row + 1 - 2 * (op_row % 2) == op_column
        for u in range(units):
            picked = jnp.dot(pick, ops[u], preferred_element_type=f32).astype(bf16)
            table = lax.dot_general(
                picked, pick, (((1,), (1,)), ((), ())), preferred_element_type=f32
            )
            for i, chosen in enumerate((same, twin)):
                column = jnp.sum(jnp.where(chosen, table, 0.0), axis=1, keepdims=True)
                coef[u, i] = jnp.broadcast_to(column, (states, 128))

    ops[pl.ds(0, channels)] = ops_ref[...]
    wave_copy.start()
    run("own")
    send_left()
    pick_operators()
    run("start")

    wave_copy.wait()
    both_left = left.at[pl.ds(channels, channels)]
    to_device(both_left, both_left, early_send, left_recv, (b, peer)).wait_recv()

    row_index = lax.broadcasted_iota(jnp.int32, (rows, rows), 0)
    column_index = lax.broadcasted_iota(jnp.int32, (rows, rows), 1)
    half_row = lax.broadcasted_iota(jnp.int32, (rows, half), 0)
    half_column = lax.broadcasted_iota(jnp.int32, (rows, half), 1) + y * half

    def to_sibling(pos):
        return to_device(
            part_out.at[pos], part_in.at[pos], part_send, part_recv.at[pos], (b, sibling)
        )

    def to_peer(pos):
        return to_device(fin.at[pos], arr.at[pos], fin_send, fin_recv.at[pos], (b, peer))

    def rank_to_peer(pos, r):
        recv = fin_recv.at[pos] if r == 0 else last_recv
        return to_device(fin.at[pos, r], arr.at[pos, r], fin_send, recv, (b, peer))

    def rank_passing(pos, r):
        return to_device(arr.at[pos, r], arr.at[pos, r], pass_send, pass_recv, (b, sibling))

    def passing(pos):
        return to_device(arr.at[pos], arr.at[pos], pass_send, pass_recv, (b, sibling))

    def masked_pair(k):
        live = (row_index < left_sizes[b]) & (column_index < states_of[k, 2])

        def masked(s):
            return jnp.where(live, wave[s].astype(f32), 0.0).astype(bf16)

        return jnp.concatenate([masked(states_of[k, 0]), masked(states_of[k, 1])], axis=0)

    def products(k, both, units_of, factor):
        parts = lax.dot_general(
            both, factor, (((1,), (1,)), ((), ())), preferred_element_type=f32
        ).astype(bf16).astype(f32)
        total = None
        for i, u in enumerate(units_of):
            p1 = parts[:rows, i * half:(i + 1) * half]
            p2 = parts[rows:, i * half:(i + 1) * half]
            own1, own2 = coef[u, 0, pl.ds(2 * k, 1)], coef[u, 0, pl.ds(2 * k + 1, 1)]
            cross1, cross2 = coef[u, 1, pl.ds(2 * k, 1)], coef[u, 1, pl.ds(2 * k + 1, 1)]
            mixed = jnp.concatenate(
                [(own1 * p1 + cross1 * p2).astype(bf16), (cross2 * p1 + own2 * p2).astype(bf16)],
                axis=1,
            )
            product = jnp.dot(left[u], mixed, preferred_element_type=f32)
            total = product if total is None else total + product
        return total

    def some(k, both, units_of):
        factor = right_all[pos_of(k), pl.ds(units_of[0], channels)].reshape(channels * half, rows)
        return products(k, both, units_of, factor)

    def give(k, total):
        pos = pos_of(k)
        part_out[pos] = total.astype(bf16)
        to_sibling(pos).start()

    def compute(k):
        both = masked_pair(k)
        total = some(k, both, lo) + some(k, both, hi)
        give(k, total)
        part[pos_of(k)] = total

    def finish(k, total):
        part[pos_of(k)] = total

        @pl.when(c == 0)
        def _():
            add_up(k)
            send(k)

        give(k, part[pos_of(k)])

    def compute_last(k):
        pos = pos_of(k)
        for i in range(channels):
            pair = (i, channels + i)

            @pl.when(end)
            def _():
                for u in pair:
                    event(3, 1, u, ())

            @pl.when(jnp.logical_not(end))
            def _():
                if pair[0] in last_mid:
                    event(2, 1, pair[0], ())

            factor = jnp.concatenate([right_all[pos, u] for u in pair], axis=0)
            total = products(k, held[k - 5], pair, factor)
            if i == 0:
                part[pos] = total
            elif i < channels - 1:
                part[pos] += total
            else:
                finish(k, part[pos] + total)

    def add_up(k):
        pos = pos_of(k)
        to_sibling(pos).wait_recv()
        live = (half_row < left_sizes[b]) & (half_column < states_of[k, 2])
        for r in range(2):
            cut = slice(r * half, (r + 1) * half)
            total = part[pos, :, cut] + part_in[pos, :, cut].astype(f32)
            fin[pos, r] = jnp.where(live, total, 0.0).astype(bf16)

    def send(k):
        if isinstance(k, int) and k == n - 1:
            for r in range(2):
                rank_to_peer(pos_of(k), r).start()
        else:
            to_peer(pos_of(k)).start()

    def pass_on(k):
        pos = pos_of(k)
        to_peer(pos).wait_recv()
        passing(pos).start()

    def free_sends():
        settled(left.at[pl.ds(0, channels + channels // 2)], early_send)
        ops_to_peer.wait_send()

        @pl.when(end)
        def _():
            settled(right_all.at[pl.ds(0, 2)], gather_send.at[0])
            settled(right_all.at[pl.ds(0, 3)], gather_send.at[1])

        @pl.when(jnp.logical_not(end))
        def _():
            settled(right_all.at[pl.ds(0, 3)], gather_send.at[0])

    def on_core(core, *jobs):
        @pl.when(c == core)
        def _():
            for job, k in jobs:
                job(k)

    def step(k, _):
        for stage in range(1, 5):
            @pl.when(k == stage)
            def _():
                if stage >= 2:
                    on_core(1, (add_up, stage - 2))
                run(stage)

        compute(k)

        @pl.when((c == 0) & (k >= 1))
        def _():
            add_up(k - 1)
            send(k - 1)

        return 0

    def low_half(k, _):
        for stage in (5, 6):
            @pl.when(k == stage)
            def _():
                run(f"{stage} low")

        both = masked_pair(k)
        held[k - 5] = both
        part[pos_of(k)] = some(k, both, lo)
        return 0

    def one(k, u):
        return products(k, held[k - 5], (u,), right_all[pos_of(k), u])

    def high_half(k):
        run(f"{k} high")
        finish(k, part[pos_of(k)] + some(k, held[k - 5], hi))

    lax.fori_loop(0, 5, step, 0)
    on_core(1, (add_up, 3))
    run(5)
    on_core(0, (add_up, 4), (send, 4))
    lax.fori_loop(5, 7, low_half, 0)
    held[2] = masked_pair(7)
    run("5 third")
    part[pos_of(5)] += one(5, hi[0])
    run("5 last")
    total = part[pos_of(5)]
    for u in hi[1:]:
        total = total + one(5, u)
    finish(5, total)
    high_half(6)
    on_core(0, (pass_on, 0), (pass_on, 1), (pass_on, 2))
    free_sends()
    compute_last(7)
    on_core(1, (add_up, 4))
    on_core(0, *[(pass_on, k) for k in range(3, n - 1)])
    on_core(1, (add_up, 5), (add_up, 6), (add_up, 7))

    @pl.when(jnp.logical_not(end))
    def _():
        settled(right_all.at[pl.ds(0, 6)], gather_send.at[1])

    settled(part_out, part_send)
    mine_at = pl.ds(pl.multiple_of(y * half, half), half)
    others_at = pl.ds(pl.multiple_of((1 - y) * half, half), half)
    for q in range(per):
        out_ref[q, :, mine_at] = fin[mine[q, 0], mine[q, 1]]

    @pl.when(c == 0)
    def _():
        for r in range(2):
            rank_to_peer(pos_of(n - 1), r).wait_recv()
            rank_passing(pos_of(n - 1), r).start()
        settled(arr, fin_send)

    @pl.when(c == 1)
    def _():
        to_device(arr, arr, pass_send, pass_recv, (b, sibling)).wait_recv()

    for q in range(per):
        out_ref[q, :, others_at] = arr[mine[q, 0], mine[q, 1]]

    @pl.when(c == 0)
    def _():
        settled(arr, pass_send)


def shards(n, m, wave_blocks, left_environment, right_environment, site_operators,
           right_sector, left_sizes, right_sizes, sector_place):
    states, rows = wave_blocks.shape[1:3]
    channels = left_environment.shape[0]
    per = states // m
    cores = 2 if m % 2 == 0 else 1
    ny = m // cores
    count = ny * per
    remote = max(1, (ny - 1) * per)
    block = (rows, rows)
    bf16, f32 = jnp.bfloat16, jnp.float32
    smem = pl.BlockSpec(memory_space=pltpu.SMEM)
    hbm = pl.BlockSpec(memory_space=pl.ANY)
    dma = pltpu.SemaphoreType.DMA
    nz, nx = plane_of(n)
    by_halves = (nz, nx, ny, cores, channels) == (4, 2, 2, 2, 2) and states == 2 * n
    if by_halves:
        half = (rows // 2, rows)
        tall = (rows, rows // 2)
        scratch = [
            pltpu.VMEM((n, 2 * channels) + half, bf16),
            pltpu.VMEM((channels,) + half, bf16),
            pltpu.VMEM((states,) + block, bf16),
            pltpu.VMEM((2 * channels,) + block, bf16),
            pltpu.VMEM((2 * channels, states, states), bf16),
            pltpu.VMEM((2 * channels, 2, states, 128), f32),
            pltpu.VMEM((n,) + block, f32),
            pltpu.VMEM((n,) + block, bf16),
            pltpu.VMEM((n,) + block, bf16),
            pltpu.VMEM((n, 2) + tall, bf16),
            pltpu.VMEM((n, 2) + tall, bf16),
            pltpu.SMEM((n, 3), jnp.int32),
            pltpu.SMEM((per, 2), jnp.int32),
            pltpu.VMEM((3, 2 * rows, rows), bf16),
            dma((3,)), dma((2,)), dma((n, 2 * channels)), dma, dma, dma, dma,
            dma, dma((n,)), dma, dma((n,)), dma, dma, dma, dma,
        ]
    elif ny == 2 and cores == 2:
        rest = [
            pltpu.VMEM((n,) + block, f32),
            pltpu.VMEM((n,) + block, bf16),
            pltpu.VMEM((n,) + block, bf16),
            pltpu.VMEM((2, n, 2) + block, bf16),
            dma((n,)), dma((n,)), dma((3, n)), dma((2, n, 2)),
        ]
    else:
        rest = [
            pltpu.VMEM((2 * n, channels) + block, bf16),
            pltpu.VMEM((count,) + block, bf16),
            pltpu.VMEM((count,) + block, bf16),
            pltpu.VMEM((remote,) + block, bf16),
            pltpu.VMEM((remote,) + block, bf16),
            pltpu.VMEM((per,) + block, f32),
            dma((count,)), dma((count,)), dma((remote,)), dma((remote,)),
        ]
    if not by_halves:
        scratch = [
            pltpu.VMEM((n, channels) + block, bf16),
            pltpu.VMEM((states,) + block, bf16),
            pltpu.VMEM((channels,) + block, bf16),
            dma((3,)), dma((n, channels, 4)), dma((n, channels)),
            *rest,
        ]
    out = pl.pallas_call(
        functools.partial(halves_kernel if by_halves else kernel, n, m),
        out_shape=pltpu.VMEM((per,) + block, bf16),
        in_specs=[smem] * 4 + [pl.BlockSpec(memory_space=pltpu.VMEM)] + [hbm] * 3,
        out_specs=pl.BlockSpec(memory_space=pltpu.VMEM),
        scratch_shapes=scratch,
        compiler_params=pltpu.CompilerParams(
            collective_id=0, has_side_effects=True, vmem_limit_bytes=60 * 1024 * 1024
        ),
    )(
        right_sector.reshape(states), sector_place, left_sizes, right_sizes,
        site_operators,
        wave_blocks.reshape((states,) + block),
        left_environment.reshape((channels,) + block),
        right_environment.reshape((channels,) + block),
    )
    return out.reshape((1, per) + block)


def solution(mesh):
    placed = (
        P("bond", None, None, None),
        P("mpo", "bond", None, None),
        P("mpo", "bond", None, None),
        P("mpo", None, None),
        P("bond", None, None),
        P(),
        P(),
        P(),
    )
    body = functools.partial(shards, mesh.shape["bond"], mesh.shape["mpo"])
    return jax.shard_map(
        body, mesh=mesh, in_specs=placed, out_specs=P("bond", "mpo", None, None), check_vma=False
    )
```
